32 devices in a mesh: dp: 16 (over z, y, x), tensor: 2 (over core).
Axes of the slice: x: 2, y: 2, z: 4, core: 2. Of those that a mesh axis runs over, the one named last changes fastest.
Arguments:
- activations: bfloat16 [2048, 16, 768], P(None, 'dp'), may hold values from -6 to 6
- cotangent: bfloat16 [2048, 16, 768], P(None, 'dp'), may hold values from -6 to 6
- lengths: int32 [32], replicated, may hold values from 1 to 2032, as said below
- dealing: int32 [32], replicated, may hold values from 0 to 31, as said below
- qkv_weight: bfloat16 [768, 3, 768], P(None, None, 'tensor'), may hold values from -0.21875 to 0.21875
- qv_bias: float32 [2, 768], P(None, 'tensor'), may hold values from -1.75 to 1.75
- out_weight: bfloat16 [768, 768], P('tensor'), may hold values from -3.5 to 3.5
- out_bias: float32 [768], replicated, may hold values from -1.75 to 1.75
- first_gain: float32 [768], replicated, may hold values from 0.5 to 1.5
- first_shift: float32 [768], replicated, may hold values from -1.75 to 1.75
- up_weight: bfloat16 [768, 3072], P(None, 'tensor'), may hold values from -0.21875 to 0.21875
- up_bias: float32 [3072], P('tensor'), may hold values from -1.75 to 1.75
- down_weight: bfloat16 [3072, 768], P('tensor'), may hold values from -0.109375 to 0.109375
- down_bias: float32 [768], replicated, may hold values from -1.75 to 1.75
- second_gain: float32 [768], replicated, may hold values from 0.5 to 1.5
- second_shift: float32 [768], replicated, may hold values from -1.75 to 1.75
Outputs:
- output: bfloat16 [2048, 16, 768], P(None, 'dp')
- input_grad: bfloat16 [2048, 16, 768], P(None, 'dp')
- grad_qkv_weight: float32 [768, 3, 768], P(None, None, 'tensor')
- grad_qv_bias: float32 [2, 768], P(None, 'tensor')
- grad_out_weight: float32 [768, 768], P('tensor')
- grad_out_bias: float32 [768], replicated
- grad_first_gain: float32 [768], replicated
- grad_first_shift: float32 [768], replicated
- grad_up_weight: float32 [768, 3072], P(None, 'tensor')
- grad_up_bias: float32 [3072], P('tensor')
- grad_down_weight: float32 [3072, 768], P('tensor')
- grad_down_bias: float32 [768], replicated
- grad_second_gain: float32 [768], replicated
- grad_second_shift: float32 [768], replicated
The draws below stay inside these ranges and needn't reach their ends.
Inputs may be any that keep to these rules, and one draw needn't show every extreme that they name: `lengths`: rounded up to multiples of 16, the 2 sequences of dealt slots 2 p .. 2 p + 1 fill exactly 2048 rows for every p; in every draw one sequence has exactly 2032 tokens. `dealing`: each number appears once; slot k goes to index k // 2 of dp.
All inputs are finite; a program needn't handle non-finite values.
Results may differ from the reference program's by a relative error of at most 0.017.
The reference program's roundings to bfloat16 on the way count: a program that leaves them out, or rounds other values in their place, can miss the bound.
Values may be sent and summed in bfloat16 or wider, within the bound.
A program may use at most 256 MiB of HBM per device.

```python
import math
import jax
import jax.numpy as jnp
from jax import lax

D = 768
HD = 64
FF = 3072
TOK_DEV = 2048
SEQ_DEV = 2
UNIT = 16
SEQS = 32
N_DP = 16


def plan_sequences(key):
    unit_count = TOK_DEV // UNIT
    pack_count = SEQS // SEQ_DEV
    first_key, trim_key, order_key, long_key = jax.random.split(jax.random.fold_in(key, 11), 4)
    pack_ids = jnp.arange(pack_count, dtype=jnp.int32)
    long_pack = jax.random.randint(long_key, (), 0, pack_count)
    first_units = jax.random.randint(first_key, (pack_count,), 1, unit_count)
    first_units = jnp.where(pack_ids == long_pack, unit_count - 1, first_units)
    units = jnp.stack([first_units, unit_count - first_units], axis=1).reshape(SEQS)
    trims = jax.random.randint(trim_key, (SEQS,), 0, UNIT)
    slot_ids = jnp.arange(SEQS, dtype=jnp.int32)
    trims = jnp.where(slot_ids == SEQ_DEV * long_pack, 0, trims)
    dealt_lengths = (units * UNIT - trims).astype(jnp.int32)
    order = jax.random.permutation(order_key, SEQS).astype(jnp.int32)
    given_lengths = jnp.zeros((SEQS,), jnp.int32).at[order].set(dealt_lengths)
    return (given_lengths, order)


def draw_lengths(key, part):
    return plan_sequences(key)[0]


def draw_dealing(key, part):
    return plan_sequences(key)[1]


def level_of(key, dims, cuts, smallest, top_value):
    def one(axis_at, parts):
        draws = jax.random.uniform(jax.random.fold_in(jax.random.fold_in(key, 6), axis_at), (parts,), jnp.float32, smallest / len(cuts), top_value / len(cuts))
        return jnp.repeat(jnp.exp(draws), dims[axis_at] // parts).reshape((-1,) + (1,) * (len(dims) - axis_at - 1))

    level = one(*cuts[0])
    for cut in cuts[1:]:
        level = level * one(*cut)
    return level


def normal_values(own_key, dims, spread, reach, cuts=(), held_as=jnp.bfloat16):
    values = spread * jax.random.normal(own_key, dims, jnp.float32)
    if cuts:
        values = values * level_of(own_key, dims, cuts, -0.22, 0.18)
    return jnp.clip(values, -reach, reach).astype(held_as)


def setup_inputs(seed: int = 0) -> dict:
    key_list = jax.random.split(jax.random.key(seed), 17)
    activations = normal_values(key_list[0], (TOK_DEV, UNIT, D), 1.0, 6.0, ((1, 16),))
    cotangent = normal_values(key_list[1], (TOK_DEV, UNIT, D), 1.0, 6.0, ((1, 16),))
    lengths = draw_lengths(jax.random.fold_in(key_list[16], 71), 0)
    dealing = draw_dealing(jax.random.fold_in(key_list[16], 71), 0)
    qkv_weight = normal_values(key_list[4], (D, 3, D), D ** -0.5, 0.21875, ((2, 2),))
    qv_bias = normal_values(key_list[5], (2, D), 0.3, 1.75, ((1, 2),), jnp.float32)
    out_weight = normal_values(key_list[6], (D, D), (max(1, D // 256)) ** -0.5, 3.5, ((0, 2),))
    out_bias = normal_values(key_list[7], (D,), 0.3, 1.75, (), jnp.float32)
    first_gain = jnp.clip(1.0 + 0.1 * jax.random.normal(key_list[8], (D,), jnp.float32), 0.5, 1.5)
    first_shift = normal_values(key_list[9], (D,), 0.3, 1.75, (), jnp.float32)
    up_weight = normal_values(key_list[10], (D, FF), D ** -0.5, 0.21875, ((1, 2),))
    up_bias = normal_values(key_list[11], (FF,), 0.3, 1.75, ((0, 2),), jnp.float32)
    down_weight = normal_values(key_list[12], (FF, D), FF ** -0.5, 0.109375, ((0, 2),))
    down_bias = normal_values(key_list[13], (D,), 0.3, 1.75, (), jnp.float32)
    second_gain = jnp.clip(1.0 + 0.1 * jax.random.normal(key_list[14], (D,), jnp.float32), 0.5, 1.5)
    second_shift = normal_values(key_list[15], (D,), 0.3, 1.75, (), jnp.float32)
    return dict(activations=activations, cotangent=cotangent, lengths=lengths, dealing=dealing, qkv_weight=qkv_weight, qv_bias=qv_bias, out_weight=out_weight, out_bias=out_bias, first_gain=first_gain, first_shift=first_shift, up_weight=up_weight, up_bias=up_bias, down_weight=down_weight, down_bias=down_bias, second_gain=second_gain, second_shift=second_shift)


@jax.custom_vjp
def low(v):
    return lax.optimization_barrier(v.astype(jnp.bfloat16)).astype(jnp.float32)

@jax.custom_vjp
def low_back(v):
    return v

def low_keep(v):
    return (low(v), None)

def low_pass(kept, grad):
    return (grad,)

def back_keep(v):
    return (v, None)

def back_low(kept, grad):
    return (low(grad),)
low.defvjp(low_keep, low_pass)
low_back.defvjp(back_keep, back_low)
PRECISE = lax.Precision.HIGHEST
MASKED_SCORE = -1e+30
NORM_EPSILON = 1e-05

def layer_norm(field, norm_gain, norm_shift):
    center = field - lax.optimization_barrier(jnp.mean(field, axis=-1, keepdims=True))
    variance = lax.optimization_barrier(jnp.mean(center * center, axis=-1, keepdims=True))
    return center * lax.rsqrt(variance + NORM_EPSILON) * norm_gain + norm_shift

def product(first_op, second_op):
    return jnp.dot(first_op, second_op, precision=PRECISE)

def pack_layer(params, pack_rows, segment, key_live):
    qkv_weight, qv_bias, out_weight, out_bias, first_gain, first_shift, up_weight, up_bias, down_weight, down_bias, second_gain, second_shift = params
    row_count = pack_rows.shape[0]
    head_count = D // HD
    score_scale = 1.0 / math.sqrt(HD)
    queries = low_back(low(product(pack_rows, qkv_weight[:, 0]) + qv_bias[0])).reshape(row_count, head_count, HD)
    key_rows = low_back(low(product(pack_rows, qkv_weight[:, 1]))).reshape(row_count, head_count, HD)
    values = low_back(low(product(pack_rows, qkv_weight[:, 2]) + qv_bias[1])).reshape(row_count, head_count, HD)
    raw_scores = low_back(jnp.einsum('qhd,khd->hqk', queries, key_rows, precision=PRECISE) * score_scale)
    allowed = (segment[:, None] == segment[None, :]) & key_live[None, :]
    masked = jnp.where(allowed[None], raw_scores, MASKED_SCORE)
    row_max = lax.optimization_barrier(jnp.max(masked, axis=-1, keepdims=True))
    shifted = jnp.exp(masked - row_max)
    weights = low(shifted / lax.optimization_barrier(jnp.sum(shifted, axis=-1, keepdims=True)))
    context = low_back(low(jnp.einsum('hqk,khd->qhd', weights, values, precision=PRECISE))).reshape(row_count, D)
    attention = low_back(product(context, out_weight))
    first_norm = layer_norm(pack_rows + attention + out_bias, first_gain, first_shift)
    upward = low_back(product(low(first_norm), up_weight) + up_bias)
    activated = low(jax.nn.gelu(upward, approximate=False))
    downward = low_back(product(activated, down_weight))
    return layer_norm(first_norm + downward + down_bias, second_gain, second_shift)

def reference(activations, cotangent, lengths, dealing, qkv_weight, qv_bias, out_weight, out_bias, first_gain, first_shift, up_weight, up_bias, down_weight, down_bias, second_gain, second_shift):
    padded = ((lengths + UNIT - 1) // UNIT * UNIT).astype(jnp.int32)
    given_start = (jnp.cumsum(padded) - padded).astype(jnp.int32)
    dealt_pad = padded[dealing]
    dealt_len = lengths[dealing]
    dealt_start = (jnp.cumsum(dealt_pad) - dealt_pad).astype(jnp.int32)
    row_ids = jnp.arange(TOK_DEV * N_DP, dtype=jnp.int32)
    dealt_slot = (lax.optimization_barrier(jnp.sum((dealt_start[None, :] <= row_ids[:, None]).astype(jnp.int32), axis=1)) - 1).astype(jnp.int32)
    offset = (row_ids - dealt_start[dealt_slot]).astype(jnp.int32)
    key_live = offset < dealt_len[dealt_slot]
    source_row = (given_start[dealing[dealt_slot]] + offset).astype(jnp.int32)
    flat_rows = activations.astype(jnp.float32).reshape(TOK_DEV * N_DP, D)
    flat_grad = cotangent.astype(jnp.float32).reshape(TOK_DEV * N_DP, D)
    dealt_rows = flat_rows[source_row].reshape(N_DP, TOK_DEV, D)
    dealt_grad = flat_grad[source_row].reshape(N_DP, TOK_DEV, D)
    segments = dealt_slot.reshape(N_DP, TOK_DEV)
    live_keys = key_live.reshape(N_DP, TOK_DEV)
    params = tuple((weight_arg.astype(jnp.float32) for weight_arg in (qkv_weight, qv_bias, out_weight, out_bias, first_gain, first_shift, up_weight, up_bias, down_weight, down_bias, second_gain, second_shift)))

    def forward(weights_all, rows_all):

        def one_pack(pieces):
            return pack_layer(weights_all, pieces[0], pieces[1], pieces[2])
        return lax.map(jax.checkpoint(one_pack), (rows_all, segments, live_keys))
    result, pullback = jax.vjp(forward, params, dealt_rows)
    param_grads, input_grads = pullback(dealt_grad)
    grad_qkv, grad_qv, grad_out, grad_outb, grad_fgain, grad_fshift, grad_up, grad_upb, grad_down, grad_downb, grad_sgain, grad_sshift = param_grads

    def to_given(field):
        flat = field.reshape(TOK_DEV * N_DP, D)
        placed = jnp.zeros_like(flat).at[source_row].set(flat)
        return placed.reshape(TOK_DEV, N_DP, D).astype(jnp.bfloat16)
    return (to_given(result), to_given(input_grads), grad_qkv, grad_qv, grad_out, grad_outb, grad_fgain, grad_fshift, grad_up, grad_upb, grad_down, grad_downb, grad_sgain, grad_sshift)
```

```python
import functools
import math

import jax
import jax.numpy as jnp
from jax import lax
from jax.experimental import pallas as pl
from jax.experimental.pallas import tpu as pltpu
from jax.sharding import PartitionSpec as P

HD = 64
BF = jnp.bfloat16
F32 = jnp.float32
MASKED_SCORE = -1e30
NORM_EPSILON = 1e-05
EXTRA = 16
ROOM = 56 * 2**20


def dot(a, b, dims=((1,), (0,))):
    return lax.dot_general(a, b, (dims, ((), ())), preferred_element_type=F32)


def unit_starts(lengths, starts, unit):
    def step(s, total):
        starts[s] = total
        return total + (lengths[s] + unit - 1) // unit

    lax.fori_loop(0, lengths.shape[0], step, jnp.int32(0))


def pack_windows(lengths, dealing, starts, unit, pack, first, rows, total):
    seq_a = dealing[2 * pack]
    seq_b = dealing[2 * pack + 1]
    units_a = (lengths[seq_a] + unit - 1) // unit
    shift_a = starts[seq_a]
    shift_b = starts[seq_b] - units_a
    bases = []
    for shift in (shift_a, shift_b):
        base = jnp.clip((shift + first) // 16 * 16, 0, total - rows - 16)
        bases.append(pl.multiple_of(base, 16))
    return units_a, shift_a, shift_b, bases


def deal_kernel(unit, half, lengths, dealing, core, x_ref, o_ref, starts):
    total = x_ref.shape[0]
    unit_starts(lengths, starts, unit)
    first = core[0] * half
    wide = half + 16
    slot = first + lax.broadcasted_iota(jnp.int32, (half, wide), 0)
    col = lax.broadcasted_iota(jnp.int32, (half, wide), 1)

    def one(pack, carry):
        units_a, shift_a, shift_b, (base_a, base_b) = pack_windows(
            lengths, dealing, starts, unit, pack, first, half, total
        )
        pick_a = (col + base_a == slot + shift_a) & (slot < units_a)
        pick_b = (col + base_b == slot + shift_b) & (slot >= units_a)
        rows = dot(pick_a.astype(F32).astype(BF), x_ref[pl.ds(base_a, wide), :])
        rows += dot(pick_b.astype(F32).astype(BF), x_ref[pl.ds(base_b, wide), :])
        o_ref[pl.ds(pl.multiple_of(pack * half, 16), half), :] = rows.astype(BF)
        return carry

    lax.fori_loop(0, total // (2 * half), one, 0, unroll=4)


def deal(x, lengths, dealing, core, unit, half):
    total, width = x.shape
    smem = pl.BlockSpec(memory_space=pltpu.SMEM)
    vmem = pl.BlockSpec(memory_space=pltpu.VMEM)
    return pl.pallas_call(
        functools.partial(deal_kernel, unit, half),
        in_specs=[smem, smem, smem, vmem],
        out_specs=vmem,
        out_shape=jax.ShapeDtypeStruct((total // 2, width), BF),
        scratch_shapes=[pltpu.SMEM(lengths.shape, jnp.int32)],
        compiler_params=pltpu.CompilerParams(vmem_limit_bytes=ROOM),
        cost_estimate=pl.CostEstimate(
            flops=4 * total * width * half, bytes_accessed=4 * total * width, transcendentals=0
        ),
        name="deal",
    )(lengths, dealing, core, x)


def undeal_kernel(unit, half, lengths, dealing, core, own_ref, sib_ref, o_ref, starts):
    total = o_ref.shape[0]
    unit_starts(lengths, starts, unit)
    wide = half + 16
    row = lax.broadcasted_iota(jnp.int32, (wide, half), 0)
    col = lax.broadcasted_iota(jnp.int32, (wide, half), 1)
    o_ref[...] = jnp.zeros_like(o_ref)

    def one(pack, carry):
        for part, ref in ((core[0], own_ref), (1 - core[0], sib_ref)):
            first = part * half
            units_a, shift_a, shift_b, (base_a, base_b) = pack_windows(
                lengths, dealing, starts, unit, pack, first, half, total
            )
            slot = first + col
            pick_a = (row + base_a == slot + shift_a) & (slot < units_a)
            pick_b = (row + base_b == slot + shift_b) & (slot >= units_a)
            rows = ref[pl.ds(pl.multiple_of(pack * half, 16), half), :]
            o_ref[pl.ds(base_a, wide), :] += dot(pick_a.astype(F32).astype(BF), rows).astype(BF)
            o_ref[pl.ds(base_b, wide), :] += dot(pick_b.astype(F32).astype(BF), rows).astype(BF)
        return carry

    lax.fori_loop(0, total // (2 * half), one, 0, unroll=2)


def undeal(own, sib, lengths, dealing, core, unit, half):
    total, width = 2 * own.shape[0], own.shape[1]
    smem = pl.BlockSpec(memory_space=pltpu.SMEM)
    vmem = pl.BlockSpec(memory_space=pltpu.VMEM)
    return pl.pallas_call(
        functools.partial(undeal_kernel, unit, half),
        in_specs=[smem, smem, smem, vmem, vmem],
        out_specs=vmem,
        out_shape=jax.ShapeDtypeStruct((total, width), BF),
        scratch_shapes=[pltpu.SMEM(lengths.shape, jnp.int32)],
        compiler_params=pltpu.CompilerParams(vmem_limit_bytes=ROOM),
        cost_estimate=pl.CostEstimate(
            flops=8 * total * width * half, bytes_accessed=4 * total * width, transcendentals=0
        ),
        name="undeal",
    )(lengths, dealing, core, own, sib)


def fwd_kernel(ck, q_ref, k_ref, v_ref, kx_ref, qx_ref, c_ref, c32_ref, lse_ref, kext, vt):
    n = k_ref.shape[0]
    bq = q_ref.shape[0]

    @pl.when(pl.program_id(1) == 0)
    def _():
        kext[:, :128] = k_ref[...]
        kext[:, 128:] = kx_ref[...]
        v_t = v_ref[...].T
        ones = jnp.where(lax.broadcasted_iota(jnp.int32, (EXTRA, n), 0) == 0, 1.0, 0.0).astype(BF)
        for h in range(2):
            vt[h, :HD] = v_t[HD * h : HD * h + HD]
            vt[h, HD:] = ones

    q_t = (q_ref[...] * BF(HD**-0.5)).T
    zero = jnp.zeros((HD, bq), BF)
    qx = qx_ref[...]
    q_ext = [
        jnp.concatenate([q_t[:HD], zero, qx], axis=0),
        jnp.concatenate([zero, q_t[HD:], qx], axis=0),
    ]
    tops, sums = [None, None], [None, None]
    for first in range(0, n, ck):
        keys = slice(first, first + ck)
        for h in range(2):
            s = dot(kext[keys, : 128 + EXTRA], q_ext[h])
            top = jnp.max(s, axis=0, keepdims=True)
            if first:
                top = jnp.maximum(tops[h], top)
            part = dot(vt[h, :, keys], jnp.exp(s - top).astype(BF))
            if first:
                part = part + sums[h] * jnp.exp(tops[h] - top)
            tops[h], sums[h] = top, part
    outs = []
    for h in range(2):
        total = sums[h][HD : HD + 1]
        outs.append(sums[h][:HD] / total)
        lse_ref[0, h : h + 1] = tops[h] + jnp.log(total)
    c = jnp.concatenate(outs, axis=0).T
    c32_ref[...] = c
    c_ref[...] = c.astype(BF)


def attn_cost(n, width, products):
    return pl.CostEstimate(
        flops=products * 2 * 4 * n * n * width,
        bytes_accessed=16 * n * width,
        transcendentals=n * n * width // HD,
    )


def attn_fwd(q, k, v, kx, qx, bq=2048, ck=512):
    n, width = q.shape
    pairs = width // 128
    rows = pl.BlockSpec((bq, 128), lambda p, i: (i, p))
    keys = pl.BlockSpec((n, 128), lambda p, i: (0, p))
    return pl.pallas_call(
        functools.partial(fwd_kernel, ck),
        grid=(pairs, n // bq),
        in_specs=[
            rows,
            keys,
            keys,
            pl.BlockSpec((n, 128), lambda p, i: (0, 0)),
            pl.BlockSpec((EXTRA, bq), lambda p, i: (0, i)),
        ],
        out_specs=[rows, rows, pl.BlockSpec((1, 2, bq), lambda p, i: (p, 0, i))],
        out_shape=[
            jax.ShapeDtypeStruct((n, width), BF),
            jax.ShapeDtypeStruct((n, width), F32),
            jax.ShapeDtypeStruct((pairs, 2, n), F32),
        ],
        scratch_shapes=[pltpu.VMEM((n, 256), BF), pltpu.VMEM((2, HD + EXTRA, n), BF)],
        compiler_params=pltpu.CompilerParams(vmem_limit_bytes=ROOM),
        cost_estimate=attn_cost(n, width, 2),
        name="attn_fwd",
    )(q, k, v, kx, qx)


def split3(x):
    high = x.astype(BF)
    rest = x - high.astype(F32)
    middle = rest.astype(BF)
    return high, middle, (rest - middle.astype(F32)).astype(BF)


def bwd_kernel(
    ck, q_ref, k_ref, v_ref, g_ref, c32_ref, lse_ref, kx_ref, qx_ref, dq_ref, dk_ref, dv_ref,
    kext, vext, kt, dk_acc, dv_acc,
):
    i = pl.program_id(1)
    n = k_ref.shape[0]
    bq = q_ref.shape[0]

    @pl.when(i == 0)
    def _():
        kext[:, :128] = k_ref[...]
        kext[:, 128:] = kx_ref[...]
        vext[:, :128] = v_ref[...]
        lane = lax.broadcasted_iota(jnp.int32, (n, 128), 1)
        vext[:, 128:] = jnp.where((lane >= 2) & (lane < 5), -1.0, 0.0).astype(BF)
        kt[...] = k_ref[...].T
        dk_acc[...] = jnp.zeros_like(dk_acc)
        dv_acc[...] = jnp.zeros_like(dv_acc)

    q = q_ref[...] * BF(HD**-0.5)
    g = g_ref[...]
    q_t, g_t = q.T, g.T
    prod_t = (g.astype(F32) * c32_ref[...]).T
    zero = jnp.zeros((HD, bq), BF)
    lane = lax.broadcasted_iota(jnp.int32, (bq, 128), 1)
    row = lax.broadcasted_iota(jnp.int32, (EXTRA, bq), 0)
    qx = qx_ref[...].astype(F32)

    def with_rows(base, parts):
        for j, part in enumerate(parts):
            base = jnp.where(row == 2 + j, part.astype(F32), base)
        return base.astype(BF)

    q_ext, g_ext, q_own, g_own, dq_t = [], [], [], [], []
    for h in range(2):
        mine = slice(HD * h, HD * h + HD)
        delta = jnp.sum(prod_t[mine], axis=0, keepdims=True)
        q_rows = with_rows(qx, split3(lse_ref[0, h : h + 1]))
        g_rows = with_rows(jnp.zeros((EXTRA, bq), F32), split3(delta))
        for out, turned, extra in ((q_ext, q_t, q_rows), (g_ext, g_t, g_rows)):
            both = [turned[mine], zero] if h == 0 else [zero, turned[mine]]
            out.append(jnp.concatenate(both + [extra], axis=0))
        ours = (lane < HD) if h == 0 else (lane >= HD)
        q_own.append(jnp.where(ours, q, BF(0)))
        g_own.append(jnp.where(ours, g, BF(0)))
        dq_t.append(jnp.zeros((HD, bq), F32))
    for first in range(0, n, ck):
        keys = slice(first, first + ck)
        dv = jnp.zeros((ck, 128), F32)
        dk = jnp.zeros((ck, 128), F32)
        for h in range(2):
            p = jnp.exp(dot(kext[keys, : 128 + EXTRA], q_ext[h]))
            ds = (p * dot(vext[keys, : 128 + EXTRA], g_ext[h])).astype(BF)
            dv = dv + dot(p.astype(BF), g_own[h])
            dk = dk + dot(ds, q_own[h])
            dq_t[h] = dq_t[h] + dot(kt[HD * h : HD * h + HD, keys], ds)
        dv_acc[keys] += dv
        dk_acc[keys] += dk
    dq_ref[...] = (jnp.concatenate(dq_t, axis=0).T * HD**-0.5).astype(BF)

    @pl.when(i == pl.num_programs(1) - 1)
    def _():
        dk_ref[...] = dk_acc[...].astype(BF)
        dv_ref[...] = dv_acc[...].astype(BF)


def attn_bwd(q, k, v, g, c32, lse, kx, qx, bq=1024, ck=512):
    n, width = q.shape
    pairs = width // 128
    rows = pl.BlockSpec((bq, 128), lambda p, i: (i, p))
    keys = pl.BlockSpec((n, 128), lambda p, i: (0, p))
    return pl.pallas_call(
        functools.partial(bwd_kernel, ck),
        grid=(pairs, n // bq),
        in_specs=[
            rows,
            keys,
            keys,
            rows,
            rows,
            pl.BlockSpec((1, 2, bq), lambda p, i: (p, 0, i)),
            pl.BlockSpec((n, 128), lambda p, i: (0, 0)),
            pl.BlockSpec((EXTRA, bq), lambda p, i: (0, i)),
        ],
        out_specs=[rows, keys, keys],
        out_shape=[jax.ShapeDtypeStruct((n, width), BF)] * 3,
        scratch_shapes=[
            pltpu.VMEM((n, 256), BF),
            pltpu.VMEM((n, 256), BF),
            pltpu.VMEM((128, n), BF),
            pltpu.VMEM((n, 128), F32),
            pltpu.VMEM((n, 128), F32),
        ],
        compiler_params=pltpu.CompilerParams(vmem_limit_bytes=ROOM),
        cost_estimate=attn_cost(n, width, 5),
        name="attn_bwd",
    )(q, k, v, g, c32, lse, kx, qx)


def norm_parts(field, norm_gain, norm_shift):
    center = field - jnp.mean(field, axis=-1, keepdims=True)
    inv_std = lax.rsqrt(jnp.mean(center * center, axis=-1, keepdims=True) + NORM_EPSILON)
    normed = center * inv_std
    return (normed * norm_gain + norm_shift, normed, inv_std)


def norm_back(incoming, normed, inv_std, norm_gain):
    scaled = incoming * norm_gain
    return inv_std * (
        scaled
        - jnp.mean(scaled, axis=-1, keepdims=True)
        - normed * jnp.mean(scaled * normed, axis=-1, keepdims=True)
    )


def over_rows(first_op, second_op):
    return dot(first_op, second_op, ((0,), (0,)))


def over_cols(first_op, second_op):
    return dot(first_op, second_op, ((1,), (1,)))


def local(
    activations, cotangent, lengths, dealing, qkv_weight, qv_bias, out_weight, out_bias,
    first_gain, first_shift, up_weight, up_bias, down_weight, down_bias, second_gain, second_shift,
):
    unit = lax.axis_size("dp")
    pack = lax.axis_index("dp")
    core = lax.axis_index("tensor")
    rows = activations.shape[0]
    width = activations.shape[2]
    half = rows // unit // 2

    def swap(x):
        return lax.ppermute(x, "tensor", [(0, 1), (1, 0)])

    core_arg = core.astype(jnp.int32).reshape(1)

    def send(field):
        dealt = deal(field.reshape(rows, width), lengths, dealing, core_arg, unit, half)
        got = lax.all_to_all(dealt.reshape(unit, half, width), "dp", 0, 0, tiled=True)
        return got.reshape(rows // 2, width)

    x_own = send(activations)
    cotangent_own = send(cotangent)
    out_sib, up_sib, down_sib = swap(out_weight), swap(up_weight), swap(down_weight)
    up_bias_sib = swap(up_bias)
    x_all = jnp.concatenate([x_own, swap(x_own)], axis=0)

    at = jnp.arange(rows, dtype=jnp.int32)
    at_core = jnp.where(at < rows // 2, core, 1 - core)
    position = (at_core * half + at % half) * unit + at % (rows // 2) // half
    pair = lax.dynamic_slice_in_dim(dealing, 2 * pack, 2, 0)
    seq_ids = jnp.arange(lengths.shape[0], dtype=jnp.int32)
    pair_len = jnp.sum(jnp.where(pair[:, None] == seq_ids[None, :], lengths[None, :], 0), axis=1)
    split = (pair_len[0] + unit - 1) // unit * unit
    second = position >= split
    live = jnp.where(second, position - split < pair_len[1], position < pair_len[0])
    lane = jnp.arange(128, dtype=jnp.int32)[None, :]
    barred = jnp.where(live & second, 0, jnp.where(live, 1, 2))[:, None]
    key_extra = jnp.where(
        lane < 2,
        jnp.where((lane == barred) | (barred == 2), MASKED_SCORE, 0.0),
        jnp.where(lane < 5, -1.0, 0.0),
    ).astype(BF)
    turn = jnp.arange(EXTRA, dtype=jnp.int32)[:, None]
    query_extra = (turn == second.astype(jnp.int32)[None, :]).astype(BF)

    queries = (dot(x_all, qkv_weight[:, 0]) + qv_bias[0]).astype(BF)
    key_rows = dot(x_all, qkv_weight[:, 1]).astype(BF)
    values = (dot(x_all, qkv_weight[:, 2]) + qv_bias[1]).astype(BF)
    context, context_wide, log_total = attn_fwd(queries, key_rows, values, key_extra, query_extra)
    mine = slice(0, rows // 2)
    theirs = slice(rows // 2, rows)
    context_own = context[mine]
    context_sib = swap(context[theirs])
    attention = dot(context_own, out_weight) + dot(context_sib, out_sib)
    first_out, first_normed, first_inv = norm_parts(
        x_own.astype(F32) + attention + out_bias, first_gain, first_shift
    )
    first_low = first_out.astype(BF)

    def feed(up, bias):
        upward = dot(first_low, up) + bias
        cumulative = 0.5 * (1.0 + lax.erf(upward * math.sqrt(0.5)))
        density = jnp.exp(-0.5 * upward * upward) * (1.0 / math.sqrt(2.0 * math.pi))
        return (upward * cumulative).astype(BF), cumulative + upward * density

    active_own, slope_own = feed(up_weight, up_bias)
    active_sib, slope_sib = feed(up_sib, up_bias_sib)
    downward = dot(active_own, down_weight) + dot(active_sib, down_sib)
    second_out, second_normed, second_inv = norm_parts(
        first_out + downward + down_bias, second_gain, second_shift
    )
    outer = cotangent_own.astype(F32)
    grad_second_gain = jnp.sum(outer * second_normed, axis=0)
    grad_second_shift = jnp.sum(outer, axis=0)
    grad_h2 = norm_back(outer, second_normed, second_inv, second_gain)
    grad_down_bias = jnp.sum(grad_h2, axis=0)
    grad_branch = grad_h2.astype(BF)
    grad_up_own = (over_cols(grad_branch, down_weight) * slope_own).astype(BF)
    grad_up_sib = (over_cols(grad_branch, down_sib) * slope_sib).astype(BF)
    grad_y1 = grad_h2 + over_cols(grad_up_own, up_weight) + over_cols(grad_up_sib, up_sib)
    grad_first_gain = jnp.sum(grad_y1 * first_normed, axis=0)
    grad_first_shift = jnp.sum(grad_y1, axis=0)
    grad_h1 = norm_back(grad_y1, first_normed, first_inv, first_gain)
    grad_out_bias = jnp.sum(grad_h1, axis=0)
    grad_attn = grad_h1.astype(BF)
    grad_context = jnp.concatenate(
        [
            over_cols(grad_attn, out_weight).astype(BF),
            swap(over_cols(grad_attn, out_sib).astype(BF)),
        ],
        axis=0,
    )

    def chip_sum(own_part, sib_part):
        return (own_part + swap(sib_part.astype(BF)).astype(F32)).astype(BF)

    def all_packs(parts):
        return [x.astype(F32) for x in lax.psum(parts, "dp")]

    down_part = chip_sum(over_rows(active_own, grad_branch), over_rows(active_sib, grad_branch))
    up_part = chip_sum(over_rows(first_low, grad_up_own), over_rows(first_low, grad_up_sib))
    out_part = chip_sum(over_rows(context_own, grad_attn), over_rows(context_sib, grad_attn))
    grad_down_weight, grad_up_weight, grad_out_weight = all_packs([down_part, up_part, out_part])

    grad_queries, grad_keys, grad_values = attn_bwd(
        queries, key_rows, values, grad_context, context_wide, log_total, key_extra, query_extra
    )
    input_part = (
        over_cols(grad_queries, qkv_weight[:, 0])
        + over_cols(grad_keys, qkv_weight[:, 1])
        + over_cols(grad_values, qkv_weight[:, 2])
    )
    grad_inputs = (
        grad_h1 + input_part[mine] + swap(input_part[theirs].astype(BF)).astype(F32)
    ).astype(BF)

    def send_back(field):
        got = lax.all_to_all(field.reshape(unit, half, width), "dp", 0, 0, tiled=True)
        got = got.reshape(rows // 2, width)
        back = undeal(got, swap(got), lengths, dealing, core_arg, unit, half)
        return back.reshape(rows, 1, width)

    output = send_back(second_out.astype(BF))
    input_grad = send_back(grad_inputs)
    qkv_parts = [over_rows(x_all, grad) for grad in (grad_queries, grad_keys, grad_values)]
    qkv_parts = all_packs([part.astype(BF) for part in qkv_parts])
    grad_qkv_weight = jnp.stack(qkv_parts, axis=1)
    bias_own = jnp.sum(grad_up_own.astype(F32), axis=0)
    bias_sib = jnp.sum(grad_up_sib.astype(F32), axis=0)
    grad_up_bias = lax.psum(bias_own + swap(bias_sib), "dp")
    grad_qv_bias = lax.psum(
        jnp.stack([jnp.sum(g.astype(F32), axis=0) for g in (grad_queries, grad_values)]), "dp"
    )
    vectors = lax.psum(
        jnp.stack(
            [
                grad_out_bias,
                grad_first_gain,
                grad_first_shift,
                grad_down_bias,
                grad_second_gain,
                grad_second_shift,
            ]
        ),
        ("dp", "tensor"),
    )
    (
        grad_out_bias,
        grad_first_gain,
        grad_first_shift,
        grad_down_bias,
        grad_second_gain,
        grad_second_shift,
    ) = vectors
    return (
        output,
        input_grad,
        grad_qkv_weight,
        grad_qv_bias,
        grad_out_weight,
        grad_out_bias,
        grad_first_gain,
        grad_first_shift,
        grad_up_weight,
        grad_up_bias,
        grad_down_weight,
        grad_down_bias,
        grad_second_gain,
        grad_second_shift,
    )


def solution(mesh):
    placed = (
        P(None, "dp", None),
        P(None, "dp", None),
        P(),
        P(),
        P(None, None, "tensor"),
        P(None, "tensor"),
        P("tensor", None),
        P(),
        P(),
        P(),
        P(None, "tensor"),
        P("tensor"),
        P("tensor", None),
        P(),
        P(),
        P(),
    )
    return jax.shard_map(
        local,
        mesh=mesh,
        in_specs=placed,
        out_specs=(
            P(None, "dp", None),
            P(None, "dp", None),
            P(None, None, "tensor"),
            P(None, "tensor"),
            P("tensor", None),
            P(),
            P(),
            P(),
            P(None, "tensor"),
            P("tensor"),
            P("tensor", None),
            P(),
            P(),
            P(),
        ),
        check_vma=False,
    )
```

```python
import functools
import math

import jax
import jax.numpy as jnp
from jax import lax
from jax.experimental import pallas as pl
from jax.experimental.pallas import tpu as pltpu
from jax.sharding import PartitionSpec as P

HD = 64
BF = jnp.bfloat16
F32 = jnp.float32
MASKED_SCORE = -1e30
NORM_EPSILON = 1e-05
EXTRA = 16
ROOM = 56 * 2**20


def dot(a, b, dims=((1,), (0,))):
    return lax.dot_general(a, b, (dims, ((), ())), preferred_element_type=F32)


def unit_starts(lengths, starts, unit):
    def step(s, total):
        starts[s] = total
        return total + (lengths[s] + unit - 1) // unit

    lax.fori_loop(0, lengths.shape[0], step, jnp.int32(0))


def pack_windows(lengths, dealing, starts, unit, pack, first, rows, total):
    seq_a = dealing[2 * pack]
    seq_b = dealing[2 * pack + 1]
    units_a = (lengths[seq_a] + unit - 1) // unit
    shift_a = starts[seq_a]
    shift_b = starts[seq_b] - units_a
    bases = []
    for shift in (shift_a, shift_b):
        base = jnp.clip((shift + first) // 16 * 16, 0, total - rows - 16)
        bases.append(pl.multiple_of(base, 16))
    return units_a, shift_a, shift_b, bases


def deal_kernel(unit, half, lengths, dealing, core, x_ref, o_ref, starts):
    total = x_ref.shape[0]
    unit_starts(lengths, starts, unit)
    first = core[0] * half
    wide = half + 16
    slot = first + lax.broadcasted_iota(jnp.int32, (half, wide), 0)
    col = lax.broadcasted_iota(jnp.int32, (half, wide), 1)

    def one(pack, carry):
        units_a, shift_a, shift_b, (base_a, base_b) = pack_windows(
            lengths, dealing, starts, unit, pack, first, half, total
        )
        pick_a = (col + base_a == slot + shift_a) & (slot < units_a)
        pick_b = (col + base_b == slot + shift_b) & (slot >= units_a)
        rows = dot(pick_a.astype(F32).astype(BF), x_ref[pl.ds(base_a, wide), :])
        rows += dot(pick_b.astype(F32).astype(BF), x_ref[pl.ds(base_b, wide), :])
        o_ref[pl.ds(pl.multiple_of(pack * half, 16), half), :] = rows.astype(BF)
        return carry

    lax.fori_loop(0, total // (2 * half), one, 0, unroll=4)


def deal(x, lengths, dealing, core, unit, half):
    total, width = x.shape
    smem = pl.BlockSpec(memory_space=pltpu.SMEM)
    vmem = pl.BlockSpec(memory_space=pltpu.VMEM)
    return pl.pallas_call(
        functools.partial(deal_kernel, unit, half),
        in_specs=[smem, smem, smem, vmem],
        out_specs=vmem,
        out_shape=jax.ShapeDtypeStruct((total // 2, width), BF),
        scratch_shapes=[pltpu.SMEM(lengths.shape, jnp.int32)],
        compiler_params=pltpu.CompilerParams(vmem_limit_bytes=ROOM),
        cost_estimate=pl.CostEstimate(
            flops=4 * total * width * half, bytes_accessed=4 * total * width, transcendentals=0
        ),
        name="deal",
    )(lengths, dealing, core, x)


def undeal_kernel(unit, half, lengths, dealing, core, own_ref, sib_ref, o_ref, starts):
    total = o_ref.shape[0]
    unit_starts(lengths, starts, unit)
    wide = half + 16
    row = lax.broadcasted_iota(jnp.int32, (wide, half), 0)
    col = lax.broadcasted_iota(jnp.int32, (wide, half), 1)
    o_ref[...] = jnp.zeros_like(o_ref)

    def one(pack, carry):
        for part, ref in ((core[0], own_ref), (1 - core[0], sib_ref)):
            first = part * half
            units_a, shift_a, shift_b, (base_a, base_b) = pack_windows(
                lengths, dealing, starts, unit, pack, first, half, total
            )
            slot = first + col
            pick_a = (row + base_a == slot + shift_a) & (slot < units_a)
            pick_b = (row + base_b == slot + shift_b) & (slot >= units_a)
            rows = ref[pl.ds(pl.multiple_of(pack * half, 16), half), :]
            o_ref[pl.ds(base_a, wide), :] += dot(pick_a.astype(F32).astype(BF), rows).astype(BF)
            o_ref[pl.ds(base_b, wide), :] += dot(pick_b.astype(F32).astype(BF), rows).astype(BF)
        return carry

    lax.fori_loop(0, total // (2 * half), one, 0, unroll=2)


def undeal(own, sib, lengths, dealing, core, unit, half):
    total, width = 2 * own.shape[0], own.shape[1]
    smem = pl.BlockSpec(memory_space=pltpu.SMEM)
    vmem = pl.BlockSpec(memory_space=pltpu.VMEM)
    return pl.pallas_call(
        functools.partial(undeal_kernel, unit, half),
        in_specs=[smem, smem, smem, vmem, vmem],
        out_specs=vmem,
        out_shape=jax.ShapeDtypeStruct((total, width), BF),
        scratch_shapes=[pltpu.SMEM(lengths.shape, jnp.int32)],
        compiler_params=pltpu.CompilerParams(vmem_limit_bytes=ROOM),
        cost_estimate=pl.CostEstimate(
            flops=8 * total * width * half, bytes_accessed=4 * total * width, transcendentals=0
        ),
        name="undeal",
    )(lengths, dealing, core, own, sib)


def fwd_kernel(ck, q_ref, k_ref, v_ref, kx_ref, qx_ref, c_ref, c32_ref, lse_ref, kext, vt):
    n = k_ref.shape[0]
    bq = q_ref.shape[0]

    @pl.when(pl.program_id(1) == 0)
    def _():
        kext[:, :128] = k_ref[...]
        kext[:, 128:] = kx_ref[...]
        v_t = v_ref[...].T
        ones = jnp.where(lax.broadcasted_iota(jnp.int32, (EXTRA, n), 0) == 0, 1.0, 0.0).astype(BF)
        for h in range(2):
            vt[h, :HD] = v_t[HD * h : HD * h + HD]
            vt[h, HD:] = ones

    q_t = (q_ref[...] * BF(HD**-0.5)).T
    zero = jnp.zeros((HD, bq), BF)
    qx = qx_ref[...]
    q_ext = [
        jnp.concatenate([q_t[:HD], zero, qx], axis=0),
        jnp.concatenate([zero, q_t[HD:], qx], axis=0),
    ]
    tops, sums = [None, None], [None, None]
    for first in range(0, n, ck):
        keys = slice(first, first + ck)
        for h in range(2):
            s = dot(kext[keys, : 128 + EXTRA], q_ext[h])
            top = jnp.max(s, axis=0, keepdims=True)
            if first:
                top = jnp.maximum(tops[h], top)
            part = dot(vt[h, :, keys], jnp.exp(s - top).astype(BF))
            if first:
                part = part + sums[h] * jnp.exp(tops[h] - top)
            tops[h], sums[h] = top, part
    outs = []
    for h in range(2):
        total = sums[h][HD : HD + 1]
        outs.append(sums[h][:HD] / total)
        lse_ref[0, h : h + 1] = tops[h] + jnp.log(total)
    c = jnp.concatenate(outs, axis=0).T
    c32_ref[...] = c
    c_ref[...] = c.astype(BF)


def attn_cost(n, width, products):
    return pl.CostEstimate(
        flops=products * 2 * 4 * n * n * width,
        bytes_accessed=16 * n * width,
        transcendentals=n * n * width // HD,
    )


def attn_fwd(q, k, v, kx, qx, bq=2048, ck=512):
    n, width = q.shape
    pairs = width // 128
    rows = pl.BlockSpec((bq, 128), lambda p, i: (i, p))
    keys = pl.BlockSpec((n, 128), lambda p, i: (0, p))
    return pl.pallas_call(
        functools.partial(fwd_kernel, ck),
        grid=(pairs, n // bq),
        in_specs=[
            rows,
            keys,
            keys,
            pl.BlockSpec((n, 128), lambda p, i: (0, 0)),
            pl.BlockSpec((EXTRA, bq), lambda p, i: (0, i)),
        ],
        out_specs=[rows, rows, pl.BlockSpec((1, 2, bq), lambda p, i: (p, 0, i))],
        out_shape=[
            jax.ShapeDtypeStruct((n, width), BF),
            jax.ShapeDtypeStruct((n, width), F32),
            jax.ShapeDtypeStruct((pairs, 2, n), F32),
        ],
        scratch_shapes=[pltpu.VMEM((n, 256), BF), pltpu.VMEM((2, HD + EXTRA, n), BF)],
        compiler_params=pltpu.CompilerParams(vmem_limit_bytes=ROOM),
        cost_estimate=attn_cost(n, width, 2),
        name="attn_fwd",
    )(q, k, v, kx, qx)


def split3(x):
    high = x.astype(BF)
    rest = x - high.astype(F32)
    middle = rest.astype(BF)
    return high, middle, (rest - middle.astype(F32)).astype(BF)


def bwd_kernel(
    ck, q_ref, k_ref, v_ref, g_ref, c32_ref, lse_ref, kx_ref, qx_ref, dq_ref, dk_ref, dv_ref,
    kext, vext, kt, dk_acc, dv_acc,
):
    i = pl.program_id(1)
    n = k_ref.shape[0]
    bq = q_ref.shape[0]

    @pl.when(i == 0)
    def _():
        kext[:, :128] = k_ref[...]
        kext[:, 128:] = kx_ref[...]
        vext[:, :128] = v_ref[...]
        lane = lax.broadcasted_iota(jnp.int32, (n, 128), 1)
        vext[:, 128:] = jnp.where((lane >= 2) & (lane < 5), -1.0, 0.0).astype(BF)
        kt[...] = k_ref[...].T
        dk_acc[...] = jnp.zeros_like(dk_acc)
        dv_acc[...] = jnp.zeros_like(dv_acc)

    q = q_ref[...] * BF(HD**-0.5)
    g = g_ref[...]
    q_t, g_t = q.T, g.T
    prod_t = (g.astype(F32) * c32_ref[...]).T
    zero = jnp.zeros((HD, bq), BF)
    lane = lax.broadcasted_iota(jnp.int32, (bq, 128), 1)
    row = lax.broadcasted_iota(jnp.int32, (EXTRA, bq), 0)
    qx = qx_ref[...].astype(F32)

    def with_rows(base, parts):
        for j, part in enumerate(parts):
            base = jnp.where(row == 2 + j, part.astype(F32), base)
        return base.astype(BF)

    q_ext, g_ext, q_own, g_own, dq_t = [], [], [], [], []
    for h in range(2):
        mine = slice(HD * h, HD * h + HD)
        delta = jnp.sum(prod_t[mine], axis=0, keepdims=True)
        q_rows = with_rows(qx, split3(lse_ref[0, h : h + 1]))
        g_rows = with_rows(jnp.zeros((EXTRA, bq), F32), split3(delta))
        for out, turned, extra in ((q_ext, q_t, q_rows), (g_ext, g_t, g_rows)):
            both = [turned[mine], zero] if h == 0 else [zero, turned[mine]]
            out.append(jnp.concatenate(both + [extra], axis=0))
        ours = (lane < HD) if h == 0 else (lane >= HD)
        q_own.append(jnp.where(ours, q, BF(0)))
        g_own.append(jnp.where(ours, g, BF(0)))
        dq_t.append(jnp.zeros((HD, bq), F32))
    for first in range(0, n, ck):
        keys = slice(first, first + ck)
        dv = jnp.zeros((ck, 128), F32)
        dk = jnp.zeros((ck, 128), F32)
        for h in range(2):
            p = jnp.exp(dot(kext[keys, : 128 + EXTRA], q_ext[h]))
            ds = (p * dot(vext[keys, : 128 + EXTRA], g_ext[h])).astype(BF)
            dv = dv + dot(p.astype(BF), g_own[h])
            dk = dk + dot(ds, q_own[h])
            dq_t[h] = dq_t[h] + dot(kt[HD * h : HD * h + HD, keys], ds)
        dv_acc[keys] += dv
        dk_acc[keys] += dk
    dq_ref[...] = (jnp.concatenate(dq_t, axis=0).T * HD**-0.5).astype(BF)

    @pl.when(i == pl.num_programs(1) - 1)
    def _():
        dk_ref[...] = dk_acc[...].astype(BF)
        dv_ref[...] = dv_acc[...].astype(BF)


def attn_bwd(q, k, v, g, c32, lse, kx, qx, bq=1024, ck=512):
    n, width = q.shape
    pairs = width // 128
    rows = pl.BlockSpec((bq, 128), lambda p, i: (i, p))
    keys = pl.BlockSpec((n, 128), lambda p, i: (0, p))
    return pl.pallas_call(
        functools.partial(bwd_kernel, ck),
        grid=(pairs, n // bq),
        in_specs=[
            rows,
            keys,
            keys,
            rows,
            rows,
            pl.BlockSpec((1, 2, bq), lambda p, i: (p, 0, i)),
            pl.BlockSpec((n, 128), lambda p, i: (0, 0)),
            pl.BlockSpec((EXTRA, bq), lambda p, i: (0, i)),
        ],
        out_specs=[rows, keys, keys],
        out_shape=[jax.ShapeDtypeStruct((n, width), BF)] * 3,
        scratch_shapes=[
            pltpu.VMEM((n, 256), BF),
            pltpu.VMEM((n, 256), BF),
            pltpu.VMEM((128, n), BF),
            pltpu.VMEM((n, 128), F32),
            pltpu.VMEM((n, 128), F32),
        ],
        compiler_params=pltpu.CompilerParams(vmem_limit_bytes=ROOM),
        cost_estimate=attn_cost(n, width, 5),
        name="attn_bwd",
    )(q, k, v, g, c32, lse, kx, qx)


def bit_orders(bits):
    first = list(range(bits))
    second = [1, 2, 0] + list(range(3, bits))
    third = [2, 0, 1] + list(range(3, bits))
    return first, second, third


def cut_rows(rows, devices):
    unit = 16 * devices
    units = rows // unit
    counts = [(units + 2) // 3, (units + 1) // 3, units // 3]
    starts = [0, counts[0], counts[0] + counts[1]]
    return [(s * unit, c * unit) for s, c in zip(starts, counts) if c]


class PackSum:
    def __init__(self, devices, big, small, acc, inbox, out, small_box, send_sem, recv_sem):
        self.devices = devices
        self.bits = devices.bit_length() - 1
        self.me = lax.axis_index("dp")
        self.big, self.small, self.acc, self.inbox, self.out = big, small, acc, inbox, out
        self.small_box = small_box
        self.send_sem, self.recv_sem = send_sem, recv_sem
        self.parts = [
            (start, count, order)
            for (start, count), order in zip(cut_rows(big.shape[0], devices), bit_orders(self.bits))
        ]
        self.steps = 2 * self.bits + 1

    @staticmethod
    def scratch(rows, cols, small_shape, devices):
        bits = devices.bit_length() - 1
        return [
            pltpu.VMEM((rows, cols), BF),
            pltpu.VMEM((rows, cols), BF),
            pltpu.VMEM((rows, cols), BF),
            pltpu.VMEM((2 * bits + 1,) + small_shape, F32),
            pltpu.SemaphoreType.DMA((4, 2 * bits)),
            pltpu.SemaphoreType.DMA((4, 2 * bits)),
        ]

    def side(self, bit):
        return (self.me // 2**bit) % 2

    def partner(self, bit):
        return self.me + (1 - 2 * self.side(bit)) * 2**bit

    def region(self, part, level):
        start, count, order = self.parts[part]
        for done in range(level):
            start = start + self.side(order[done]) * (count // 2 ** (done + 1))
        return start, count // 2**level

    def rows(self, ref, start, count):
        return ref.at[pl.ds(pl.multiple_of(start, 16), count)]

    def halving(self, part, level):
        start, count = self.region(part, level)
        bit = self.parts[part][2][level]
        half = count // 2
        source = self.big if level == 0 else self.acc
        slot = self.parts[part][0] + self.parts[part][1] - count
        return pltpu.make_async_remote_copy(
            src_ref=self.rows(source, start + (1 - self.side(bit)) * half, half),
            dst_ref=self.inbox.at[pl.ds(slot, half)],
            send_sem=self.send_sem.at[part, level],
            recv_sem=self.recv_sem.at[part, level],
            device_id={"dp": self.partner(bit)},
            device_id_type=pl.DeviceIdType.MESH,
        )

    def doubling(self, part, level):
        start, count = self.region(part, level + 1)
        mine = self.rows(self.out, start, count)
        return pltpu.make_async_remote_copy(
            src_ref=mine,
            dst_ref=mine,
            send_sem=self.send_sem.at[part, self.bits + level],
            recv_sem=self.recv_sem.at[part, self.bits + level],
            device_id={"dp": self.partner(self.parts[part][2][level])},
            device_id_type=pl.DeviceIdType.MESH,
        )

    def exchange(self, level):
        return pltpu.make_async_remote_copy(
            src_ref=self.small if level == 0 else self.small_box.at[self.bits + level],
            dst_ref=self.small_box.at[level],
            send_sem=self.send_sem.at[3, level],
            recv_sem=self.recv_sem.at[3, level],
            device_id={"dp": self.partner(level)},
            device_id_type=pl.DeviceIdType.MESH,
        )

    def add(self, part, level, target):
        start, count = self.region(part, level)
        slot = self.parts[part][0] + self.parts[part][1] - count
        half = count // 2
        keep = start + self.side(self.parts[part][2][level]) * half
        source = self.big if level == 0 else self.acc
        tile = 16

        def one(i, carry):
            at = pl.ds(pl.multiple_of(keep + i * tile, 16), tile)
            came = self.inbox[pl.ds(pl.multiple_of(slot + i * tile, 16), tile), :]
            target[at, :] = (source[at, :].astype(F32) + came.astype(F32)).astype(BF)
            return carry

        lax.fori_loop(0, half // tile, one, 0)

    def step(self, k):
        bits = self.bits
        if k == 0:
            barrier = pltpu.get_barrier_semaphore()
            for bit in range(bits):
                pl.semaphore_signal(
                    barrier,
                    inc=1,
                    device_id={"dp": self.partner(bit)},
                    device_id_type=pl.DeviceIdType.MESH,
                )
            pl.semaphore_wait(barrier, bits)
        for part in range(len(self.parts)):
            if 0 < k <= bits:
                self.halving(part, k - 1).wait_recv()
                self.add(part, k - 1, self.out if k == bits else self.acc)
            elif k > bits:
                self.doubling(part, 2 * bits - k).wait_recv()
            if k < bits:
                self.halving(part, k).start()
            elif k < 2 * bits:
                self.doubling(part, 2 * bits - 1 - k).start()
        if 0 < k <= bits:
            self.exchange(k - 1).wait_recv()
            held = self.small[...] if k == 1 else self.small_box[bits + k - 1]
            self.small_box[bits + k] = held + self.small_box[k - 1]
        if k < bits:
            self.exchange(k).start()
        if k == 2 * bits:
            for part in range(len(self.parts)):
                for level in range(bits):
                    self.halving(part, level).wait_send()
                    self.doubling(part, level).wait_send()
            for level in range(bits):
                self.exchange(level).wait_send()


def pack_sum_kernel(devices, big, small, big_out, small_out, acc, inbox, out, small_box, ssem, rsem):
    comm = PackSum(devices, big, small, acc, inbox, out, small_box, ssem, rsem)
    for k in range(comm.steps):
        comm.step(k)
    big_out[...] = out[...]
    small_out[...] = small_box[2 * comm.bits]


def pack_sum(big, small, devices, ident):
    vmem = pl.BlockSpec(memory_space=pltpu.VMEM)
    return pl.pallas_call(
        functools.partial(pack_sum_kernel, devices),
        in_specs=[vmem, vmem],
        out_specs=[vmem, vmem],
        out_shape=[
            jax.ShapeDtypeStruct(big.shape, BF),
            jax.ShapeDtypeStruct(small.shape, F32),
        ],
        scratch_shapes=PackSum.scratch(*big.shape, small.shape, devices),
        compiler_params=pltpu.CompilerParams(
            vmem_limit_bytes=ROOM, collective_id=ident, has_side_effects=True
        ),
        cost_estimate=pl.CostEstimate(flops=0, bytes_accessed=200 * big.size, transcendentals=0),
        name="pack_sum",
    )(big, small)


def norm_parts(field, norm_gain, norm_shift):
    center = field - jnp.mean(field, axis=-1, keepdims=True)
    inv_std = lax.rsqrt(jnp.mean(center * center, axis=-1, keepdims=True) + NORM_EPSILON)
    normed = center * inv_std
    return (normed * norm_gain + norm_shift, normed, inv_std)


def norm_back(incoming, normed, inv_std, norm_gain):
    scaled = incoming * norm_gain
    return inv_std * (
        scaled
        - jnp.mean(scaled, axis=-1, keepdims=True)
        - normed * jnp.mean(scaled * normed, axis=-1, keepdims=True)
    )


def over_rows(first_op, second_op):
    return dot(first_op, second_op, ((0,), (0,)))


def over_cols(first_op, second_op):
    return dot(first_op, second_op, ((1,), (1,)))


def local(
    activations, cotangent, lengths, dealing, qkv_weight, qv_bias, out_weight, out_bias,
    first_gain, first_shift, up_weight, up_bias, down_weight, down_bias, second_gain, second_shift,
):
    unit = lax.axis_size("dp")
    pack = lax.axis_index("dp")
    core = lax.axis_index("tensor")
    rows = activations.shape[0]
    width = activations.shape[2]
    half = rows // unit // 2

    def swap(x):
        return lax.ppermute(x, "tensor", [(0, 1), (1, 0)])

    core_arg = core.astype(jnp.int32).reshape(1)

    def send(field):
        dealt = deal(field.reshape(rows, width), lengths, dealing, core_arg, unit, half)
        got = lax.all_to_all(dealt.reshape(unit, half, width), "dp", 0, 0, tiled=True)
        return got.reshape(rows // 2, width)

    x_own = send(activations)
    cotangent_own = send(cotangent)
    out_sib, up_sib, down_sib = swap(out_weight), swap(up_weight), swap(down_weight)
    up_bias_sib = swap(up_bias)
    x_all = jnp.concatenate([x_own, swap(x_own)], axis=0)

    at = jnp.arange(rows, dtype=jnp.int32)
    at_core = jnp.where(at < rows // 2, core, 1 - core)
    position = (at_core * half + at % half) * unit + at % (rows // 2) // half
    pair = lax.dynamic_slice_in_dim(dealing, 2 * pack, 2, 0)
    seq_ids = jnp.arange(lengths.shape[0], dtype=jnp.int32)
    pair_len = jnp.sum(jnp.where(pair[:, None] == seq_ids[None, :], lengths[None, :], 0), axis=1)
    split = (pair_len[0] + unit - 1) // unit * unit
    second = position >= split
    live = jnp.where(second, position - split < pair_len[1], position < pair_len[0])
    lane = jnp.arange(128, dtype=jnp.int32)[None, :]
    barred = jnp.where(live & second, 0, jnp.where(live, 1, 2))[:, None]
    key_extra = jnp.where(
        lane < 2,
        jnp.where((lane == barred) | (barred == 2), MASKED_SCORE, 0.0),
        jnp.where(lane < 5, -1.0, 0.0),
    ).astype(BF)
    turn = jnp.arange(EXTRA, dtype=jnp.int32)[:, None]
    query_extra = (turn == second.astype(jnp.int32)[None, :]).astype(BF)

    queries = (dot(x_all, qkv_weight[:, 0]) + qv_bias[0]).astype(BF)
    key_rows = dot(x_all, qkv_weight[:, 1]).astype(BF)
    values = (dot(x_all, qkv_weight[:, 2]) + qv_bias[1]).astype(BF)
    context, context_wide, log_total = attn_fwd(queries, key_rows, values, key_extra, query_extra)
    mine = slice(0, rows // 2)
    theirs = slice(rows // 2, rows)
    context_own = context[mine]
    context_sib = swap(context[theirs])
    attention = dot(context_own, out_weight) + dot(context_sib, out_sib)
    first_out, first_normed, first_inv = norm_parts(
        x_own.astype(F32) + attention + out_bias, first_gain, first_shift
    )
    first_low = first_out.astype(BF)

    def feed(up, bias):
        upward = dot(first_low, up) + bias
        cumulative = 0.5 * (1.0 + lax.erf(upward * math.sqrt(0.5)))
        density = jnp.exp(-0.5 * upward * upward) * (1.0 / math.sqrt(2.0 * math.pi))
        return (upward * cumulative).astype(BF), cumulative + upward * density

    active_own, slope_own = feed(up_weight, up_bias)
    active_sib, slope_sib = feed(up_sib, up_bias_sib)
    downward = dot(active_own, down_weight) + dot(active_sib, down_sib)
    second_out, second_normed, second_inv = norm_parts(
        first_out + downward + down_bias, second_gain, second_shift
    )
    outer = cotangent_own.astype(F32)
    grad_second_gain = jnp.sum(outer * second_normed, axis=0)
    grad_second_shift = jnp.sum(outer, axis=0)
    grad_h2 = norm_back(outer, second_normed, second_inv, second_gain)
    grad_down_bias = jnp.sum(grad_h2, axis=0)
    grad_branch = grad_h2.astype(BF)
    grad_up_own = (over_cols(grad_branch, down_weight) * slope_own).astype(BF)
    grad_up_sib = (over_cols(grad_branch, down_sib) * slope_sib).astype(BF)
    grad_y1 = grad_h2 + over_cols(grad_up_own, up_weight) + over_cols(grad_up_sib, up_sib)
    grad_first_gain = jnp.sum(grad_y1 * first_normed, axis=0)
    grad_first_shift = jnp.sum(grad_y1, axis=0)
    grad_h1 = norm_back(grad_y1, first_normed, first_inv, first_gain)
    grad_out_bias = jnp.sum(grad_h1, axis=0)
    grad_attn = grad_h1.astype(BF)
    grad_context = jnp.concatenate(
        [
            over_cols(grad_attn, out_weight).astype(BF),
            swap(over_cols(grad_attn, out_sib).astype(BF)),
        ],
        axis=0,
    )

    def chip_sum(own_part, sib_part):
        return (own_part + swap(sib_part.astype(BF)).astype(F32)).astype(BF)

    def stacked(parts, rows_of):
        size = sum(part.shape[0] for part in parts)
        pad = -size % rows_of
        if pad:
            parts = parts + [jnp.zeros((pad, parts[0].shape[1]), parts[0].dtype)]
        return jnp.concatenate(parts, axis=0)

    down_part = chip_sum(over_rows(active_own, grad_branch), over_rows(active_sib, grad_branch))
    up_part = chip_sum(over_rows(first_low, grad_up_own), over_rows(first_low, grad_up_sib))
    out_part = chip_sum(over_rows(context_own, grad_attn), over_rows(context_sib, grad_attn))
    up_bias_own = jnp.sum(grad_up_own.astype(F32), axis=0)
    up_bias_part = up_bias_own + swap(jnp.sum(grad_up_sib.astype(F32), axis=0))
    vectors = jnp.stack(
        [
            grad_out_bias,
            grad_first_gain,
            grad_first_shift,
            grad_down_bias,
            grad_second_gain,
            grad_second_shift,
        ]
    )
    vectors = stacked([vectors + swap(vectors), up_bias_part.reshape(-1, width)], 8)
    shard = down_part.shape[0]
    wide_parts = [down_part, out_part] + [
        up_part[:, first : first + width] for first in range(0, shard, width)
    ]
    summed, vectors = pack_sum(stacked(wide_parts, 16 * unit), vectors, unit, 0)
    grad_down_weight = summed[:shard].astype(F32)
    at_up = shard + out_part.shape[0]
    grad_out_weight = summed[shard:at_up].astype(F32)
    grad_up_weight = jnp.concatenate(
        [summed[first : first + width] for first in range(at_up, at_up + shard, width)], axis=1
    ).astype(F32)
    (
        grad_out_bias,
        grad_first_gain,
        grad_first_shift,
        grad_down_bias,
        grad_second_gain,
        grad_second_shift,
    ) = vectors[:6]
    grad_up_bias = vectors[6 : 6 + shard // width].reshape(-1)

    grad_queries, grad_keys, grad_values = attn_bwd(
        queries, key_rows, values, grad_context, context_wide, log_total, key_extra, query_extra
    )
    input_part = (
        over_cols(grad_queries, qkv_weight[:, 0])
        + over_cols(grad_keys, qkv_weight[:, 1])
        + over_cols(grad_values, qkv_weight[:, 2])
    )
    grad_inputs = (
        grad_h1 + input_part[mine] + swap(input_part[theirs].astype(BF)).astype(F32)
    ).astype(BF)

    def send_back(field):
        got = lax.all_to_all(field.reshape(unit, half, width), "dp", 0, 0, tiled=True)
        got = got.reshape(rows // 2, width)
        back = undeal(got, swap(got), lengths, dealing, core_arg, unit, half)
        return back.reshape(rows, 1, width)

    grad_inputs, grad_queries, grad_keys, grad_values = lax.optimization_barrier(
        (grad_inputs, grad_queries, grad_keys, grad_values)
    )
    output = send_back(second_out.astype(BF))
    input_grad = send_back(grad_inputs)
    qkv_parts = [
        over_rows(x_all, grad).astype(BF) for grad in (grad_queries, grad_keys, grad_values)
    ]
    qv_part = jnp.stack([jnp.sum(g.astype(F32), axis=0) for g in (grad_queries, grad_values)])
    summed, qv_sum = pack_sum(stacked(qkv_parts, 16 * unit), stacked([qv_part], 8), unit, 1)
    grad_qkv_weight = jnp.stack(
        [summed[first : first + width] for first in range(0, 3 * width, width)], axis=1
    ).astype(F32)
    grad_qv_bias = qv_sum[:2]
    return (
        output,
        input_grad,
        grad_qkv_weight,
        grad_qv_bias,
        grad_out_weight,
        grad_out_bias,
        grad_first_gain,
        grad_first_shift,
        grad_up_weight,
        grad_up_bias,
        grad_down_weight,
        grad_down_bias,
        grad_second_gain,
        grad_second_shift,
    )


def solution(mesh):
    placed = (
        P(None, "dp", None),
        P(None, "dp", None),
        P(),
        P(),
        P(None, None, "tensor"),
        P(None, "tensor"),
        P("tensor", None),
        P(),
        P(),
        P(),
        P(None, "tensor"),
        P("tensor"),
        P("tensor", None),
        P(),
        P(),
        P(),
    )
    return jax.shard_map(
        local,
        mesh=mesh,
        in_specs=placed,
        out_specs=(
            P(None, "dp", None),
            P(None, "dp", None),
            P(None, None, "tensor"),
            P(None, "tensor"),
            P("tensor", None),
            P(),
            P(),
            P(),
            P(None, "tensor"),
            P("tensor"),
            P("tensor", None),
            P(),
            P(),
            P(),
        ),
        check_vma=False,
    )
```

```python
import functools
import math

import jax
import jax.numpy as jnp
from jax import lax
from jax.experimental import pallas as pl
from jax.experimental.pallas import tpu as pltpu
from jax.sharding import PartitionSpec as P

HD = 64
BF = jnp.bfloat16
F32 = jnp.float32
MASKED_SCORE = -1e30
NORM_EPSILON = 1e-05
EXTRA = 16
ROOM = 56 * 2**20


def dot(a, b, dims=((1,), (0,))):
    return lax.dot_general(a, b, (dims, ((), ())), preferred_element_type=F32)


def unit_starts(lengths, starts, unit):
    def step(s, total):
        starts[s] = total
        return total + (lengths[s] + unit - 1) // unit

    lax.fori_loop(0, lengths.shape[0], step, jnp.int32(0))


def pack_windows(lengths, dealing, starts, unit, pack, first, rows, total):
    seq_a = dealing[2 * pack]
    seq_b = dealing[2 * pack + 1]
    units_a = (lengths[seq_a] + unit - 1) // unit
    shift_a = starts[seq_a]
    shift_b = starts[seq_b] - units_a
    bases = []
    for shift in (shift_a, shift_b):
        base = jnp.clip((shift + first) // 16 * 16, 0, total - rows - 16)
        bases.append(pl.multiple_of(base, 16))
    return units_a, shift_a, shift_b, bases


def deal_kernel(unit, half, lengths, dealing, core, x_ref, o_ref, starts):
    total = x_ref.shape[0]
    unit_starts(lengths, starts, unit)
    first = core[0] * half
    wide = half + 16
    slot = first + lax.broadcasted_iota(jnp.int32, (half, wide), 0)
    col = lax.broadcasted_iota(jnp.int32, (half, wide), 1)

    def one(pack, carry):
        units_a, shift_a, shift_b, (base_a, base_b) = pack_windows(
            lengths, dealing, starts, unit, pack, first, half, total
        )
        pick_a = (col + base_a == slot + shift_a) & (slot < units_a)
        pick_b = (col + base_b == slot + shift_b) & (slot >= units_a)
        rows = dot(pick_a.astype(F32).astype(BF), x_ref[pl.ds(base_a, wide), :])
        rows += dot(pick_b.astype(F32).astype(BF), x_ref[pl.ds(base_b, wide), :])
        o_ref[pl.ds(pl.multiple_of(pack * half, 16), half), :] = rows.astype(BF)
        return carry

    lax.fori_loop(0, total // (2 * half), one, 0, unroll=4)


def deal(x, lengths, dealing, core, unit, half):
    total, width = x.shape
    smem = pl.BlockSpec(memory_space=pltpu.SMEM)
    vmem = pl.BlockSpec(memory_space=pltpu.VMEM)
    return pl.pallas_call(
        functools.partial(deal_kernel, unit, half),
        in_specs=[smem, smem, smem, vmem],
        out_specs=vmem,
        out_shape=jax.ShapeDtypeStruct((total // 2, width), BF),
        scratch_shapes=[pltpu.SMEM(lengths.shape, jnp.int32)],
        compiler_params=pltpu.CompilerParams(vmem_limit_bytes=ROOM),
        cost_estimate=pl.CostEstimate(
            flops=4 * total * width * half, bytes_accessed=4 * total * width, transcendentals=0
        ),
        name="deal",
    )(lengths, dealing, core, x)


def undeal_kernel(unit, half, lengths, dealing, core, own_ref, sib_ref, o_ref, starts):
    total = o_ref.shape[0]
    unit_starts(lengths, starts, unit)
    wide = half + 16
    row = lax.broadcasted_iota(jnp.int32, (wide, half), 0)
    col = lax.broadcasted_iota(jnp.int32, (wide, half), 1)
    o_ref[...] = jnp.zeros_like(o_ref)

    def one(pack, carry):
        for part, ref in ((core[0], own_ref), (1 - core[0], sib_ref)):
            first = part * half
            units_a, shift_a, shift_b, (base_a, base_b) = pack_windows(
                lengths, dealing, starts, unit, pack, first, half, total
            )
            slot = first + col
            pick_a = (row + base_a == slot + shift_a) & (slot < units_a)
            pick_b = (row + base_b == slot + shift_b) & (slot >= units_a)
            rows = ref[pl.ds(pl.multiple_of(pack * half, 16), half), :]
            o_ref[pl.ds(base_a, wide), :] += dot(pick_a.astype(F32).astype(BF), rows).astype(BF)
            o_ref[pl.ds(base_b, wide), :] += dot(pick_b.astype(F32).astype(BF), rows).astype(BF)
        return carry

    lax.fori_loop(0, total // (2 * half), one, 0, unroll=2)


def undeal(own, sib, lengths, dealing, core, unit, half):
    total, width = 2 * own.shape[0], own.shape[1]
    smem = pl.BlockSpec(memory_space=pltpu.SMEM)
    vmem = pl.BlockSpec(memory_space=pltpu.VMEM)
    return pl.pallas_call(
        functools.partial(undeal_kernel, unit, half),
        in_specs=[smem, smem, smem, vmem, vmem],
        out_specs=vmem,
        out_shape=jax.ShapeDtypeStruct((total, width), BF),
        scratch_shapes=[pltpu.SMEM(lengths.shape, jnp.int32)],
        compiler_params=pltpu.CompilerParams(vmem_limit_bytes=ROOM),
        cost_estimate=pl.CostEstimate(
            flops=8 * total * width * half, bytes_accessed=4 * total * width, transcendentals=0
        ),
        name="undeal",
    )(lengths, dealing, core, own, sib)


def fwd_kernel(ck, q_ref, k_ref, v_ref, kx_ref, qx_ref, c_ref, c32_ref, lse_ref, kext, vt):
    n = k_ref.shape[0]
    bq = q_ref.shape[0]

    @pl.when(pl.program_id(1) == 0)
    def _():
        kext[:, :128] = k_ref[...]
        kext[:, 128:] = kx_ref[...]
        v_t = v_ref[...].T
        ones = jnp.where(lax.broadcasted_iota(jnp.int32, (EXTRA, n), 0) == 0, 1.0, 0.0).astype(BF)
        for h in range(2):
            vt[h, :HD] = v_t[HD * h : HD * h + HD]
            vt[h, HD:] = ones

    q_t = (q_ref[...] * BF(HD**-0.5)).T
    zero = jnp.zeros((HD, bq), BF)
    qx = qx_ref[...]
    q_ext = [
        jnp.concatenate([q_t[:HD], zero, qx], axis=0),
        jnp.concatenate([zero, q_t[HD:], qx], axis=0),
    ]
    tops, sums = [None, None], [None, None]
    for first in range(0, n, ck):
        keys = slice(first, first + ck)
        for h in range(2):
            s = dot(kext[keys, : 128 + EXTRA], q_ext[h])
            top = jnp.max(s, axis=0, keepdims=True)
            if first:
                top = jnp.maximum(tops[h], top)
            part = dot(vt[h, :, keys], jnp.exp(s - top).astype(BF))
            if first:
                part = part + sums[h] * jnp.exp(tops[h] - top)
            tops[h], sums[h] = top, part
    outs = []
    for h in range(2):
        total = sums[h][HD : HD + 1]
        outs.append(sums[h][:HD] / total)
        lse_ref[0, h : h + 1] = tops[h] + jnp.log(total)
    c = jnp.concatenate(outs, axis=0).T
    c32_ref[...] = c
    c_ref[...] = c.astype(BF)


def attn_cost(n, width, products):
    return pl.CostEstimate(
        flops=products * 2 * 4 * n * n * width,
        bytes_accessed=16 * n * width,
        transcendentals=n * n * width // HD,
    )


def attn_fwd(q, k, v, kx, qx, bq=2048, ck=512):
    n, width = q.shape
    pairs = width // 128
    rows = pl.BlockSpec((bq, 128), lambda p, i: (i, p))
    keys = pl.BlockSpec((n, 128), lambda p, i: (0, p))
    return pl.pallas_call(
        functools.partial(fwd_kernel, ck),
        grid=(pairs, n // bq),
        in_specs=[
            rows,
            keys,
            keys,
            pl.BlockSpec((n, 128), lambda p, i: (0, 0)),
            pl.BlockSpec((EXTRA, bq), lambda p, i: (0, i)),
        ],
        out_specs=[rows, rows, pl.BlockSpec((1, 2, bq), lambda p, i: (p, 0, i))],
        out_shape=[
            jax.ShapeDtypeStruct((n, width), BF),
            jax.ShapeDtypeStruct((n, width), F32),
            jax.ShapeDtypeStruct((pairs, 2, n), F32),
        ],
        scratch_shapes=[pltpu.VMEM((n, 256), BF), pltpu.VMEM((2, HD + EXTRA, n), BF)],
        compiler_params=pltpu.CompilerParams(vmem_limit_bytes=ROOM),
        cost_estimate=attn_cost(n, width, 2),
        name="attn_fwd",
    )(q, k, v, kx, qx)


def split3(x):
    high = x.astype(BF)
    rest = x - high.astype(F32)
    middle = rest.astype(BF)
    return high, middle, (rest - middle.astype(F32)).astype(BF)


def bit_orders(bits):
    first = list(range(bits))
    second = [1, 2, 0] + list(range(3, bits))
    third = [2, 0, 1] + list(range(3, bits))
    return first, second, third


def cut_rows(rows, devices):
    unit = 16 * devices
    units = rows // unit
    counts = [(units + 2) // 3, (units + 1) // 3, units // 3]
    starts = [0, counts[0], counts[0] + counts[1]]
    return [(s * unit, c * unit) for s, c in zip(starts, counts) if c]


class PackSum:
    def __init__(self, devices, keep, big, small, acc, inbox, out, small_box, send_sem, recv_sem):
        self.devices = devices
        self.keep = keep
        self.bits = devices.bit_length() - 1
        self.me = lax.axis_index("dp")
        self.big, self.small, self.acc, self.inbox, self.out = big, small, acc, inbox, out
        self.small_box = small_box
        self.send_sem, self.recv_sem = send_sem, recv_sem
        self.parts = [
            (start, count, order)
            for (start, count), order in zip(cut_rows(big.shape[0], devices), bit_orders(self.bits))
        ]
        self.steps = 2 * self.bits + 1 - keep

    def turns(self, count):
        weigh = [2.0**-level for level in range(self.bits)]
        weigh[-1] *= 6
        weigh = weigh + weigh[:0:-1]
        return [
            min(count - 1, math.ceil(count * sum(weigh[:step]) / sum(weigh)))
            for step in range(self.steps - 1)
        ]

    @staticmethod
    def scratch(rows, cols, small_shape, devices):
        bits = devices.bit_length() - 1
        return [
            pltpu.VMEM((rows, cols), BF),
            pltpu.VMEM((rows, cols), BF),
            pltpu.VMEM((rows, cols), BF),
            pltpu.VMEM((2 * bits + 1,) + small_shape, F32),
            pltpu.SemaphoreType.DMA((4, 2 * bits)),
            pltpu.SemaphoreType.DMA((4, 2 * bits)),
        ]

    def side(self, bit):
        return (self.me // 2**bit) % 2

    def partner(self, bit):
        return self.me + (1 - 2 * self.side(bit)) * 2**bit

    def region(self, part, level):
        start, count, order = self.parts[part]
        for done in range(level):
            start = start + self.side(order[done]) * (count // 2 ** (done + 1))
        return start, count // 2**level

    def rows(self, ref, start, count):
        return ref.at[pl.ds(pl.multiple_of(start, 16), count)]

    def halving(self, part, level):
        start, count = self.region(part, level)
        bit = self.parts[part][2][level]
        half = count // 2
        source = self.big if level == 0 else self.acc
        slot = self.parts[part][0] + self.parts[part][1] - count
        return pltpu.make_async_remote_copy(
            src_ref=self.rows(source, start + (1 - self.side(bit)) * half, half),
            dst_ref=self.inbox.at[pl.ds(slot, half)],
            send_sem=self.send_sem.at[part, level],
            recv_sem=self.recv_sem.at[part, level],
            device_id={"dp": self.partner(bit)},
            device_id_type=pl.DeviceIdType.MESH,
        )

    def doubling(self, part, level):
        start, count = self.region(part, level + 1)
        mine = self.rows(self.out, start, count)
        return pltpu.make_async_remote_copy(
            src_ref=mine,
            dst_ref=mine,
            send_sem=self.send_sem.at[part, self.bits + level],
            recv_sem=self.recv_sem.at[part, self.bits + level],
            device_id={"dp": self.partner(self.parts[part][2][level])},
            device_id_type=pl.DeviceIdType.MESH,
        )

    def exchange(self, level):
        return pltpu.make_async_remote_copy(
            src_ref=self.small if level == 0 else self.small_box.at[self.bits + level],
            dst_ref=self.small_box.at[level],
            send_sem=self.send_sem.at[3, level],
            recv_sem=self.recv_sem.at[3, level],
            device_id={"dp": self.partner(level)},
            device_id_type=pl.DeviceIdType.MESH,
        )

    def add(self, part, level, target):
        start, count = self.region(part, level)
        slot = self.parts[part][0] + self.parts[part][1] - count
        half = count // 2
        keep = start + self.side(self.parts[part][2][level]) * half
        source = self.big if level == 0 else self.acc
        tile = 16

        def one(i, carry):
            at = pl.ds(pl.multiple_of(keep + i * tile, 16), tile)
            came = self.inbox[pl.ds(pl.multiple_of(slot + i * tile, 16), tile), :]
            target[at, :] = (source[at, :].astype(F32) + came.astype(F32)).astype(BF)
            return carry

        lax.fori_loop(0, half // tile, one, 0)

    def step(self, k):
        bits = self.bits
        if k == 0:
            barrier = pltpu.get_barrier_semaphore()
            for bit in range(bits):
                pl.semaphore_signal(
                    barrier,
                    inc=1,
                    device_id={"dp": self.partner(bit)},
                    device_id_type=pl.DeviceIdType.MESH,
                )
            pl.semaphore_wait(barrier, bits)
        for part in range(len(self.parts)):
            if 0 < k <= bits:
                self.halving(part, k - 1).wait_recv()
                self.add(part, k - 1, self.out if k == bits else self.acc)
            elif k > bits:
                self.doubling(part, 2 * bits - k).wait_recv()
            if k < bits:
                self.halving(part, k).start()
            elif k < self.steps - 1:
                self.doubling(part, 2 * bits - 1 - k).start()
        if 0 < k <= bits:
            self.exchange(k - 1).wait_recv()
            held = self.small[...] if k == 1 else self.small_box[bits + k - 1]
            self.small_box[bits + k] = held + self.small_box[k - 1]
        if k < bits:
            self.exchange(k).start()
        if k == self.steps - 1:
            for part in range(len(self.parts)):
                for level in range(bits):
                    self.halving(part, level).wait_send()
                for level in range(self.keep, bits):
                    self.doubling(part, level).wait_send()
            for level in range(bits):
                self.exchange(level).wait_send()


def pack_sum_kernel(devices, big, small, big_out, small_out, acc, inbox, out, small_box, ssem, rsem):
    comm = PackSum(devices, 0, big, small, acc, inbox, out, small_box, ssem, rsem)
    for k in range(comm.steps):
        comm.step(k)
    big_out[...] = out[...]
    small_out[...] = small_box[2 * comm.bits]


def pack_sum(big, small, devices, ident):
    vmem = pl.BlockSpec(memory_space=pltpu.VMEM)
    return pl.pallas_call(
        functools.partial(pack_sum_kernel, devices),
        in_specs=[vmem, vmem],
        out_specs=[vmem, vmem],
        out_shape=[
            jax.ShapeDtypeStruct(big.shape, BF),
            jax.ShapeDtypeStruct(small.shape, F32),
        ],
        scratch_shapes=PackSum.scratch(*big.shape, small.shape, devices),
        compiler_params=pltpu.CompilerParams(
            vmem_limit_bytes=ROOM, collective_id=ident, has_side_effects=True
        ),
        cost_estimate=pl.CostEstimate(flops=0, bytes_accessed=200 * big.size, transcendentals=0),
        name="pack_sum",
    )(big, small)


def bwd_kernel(
    ck, devices, turns, q_ref, k_ref, v_ref, g_ref, c32_ref, lse_ref, kx_ref, qx_ref, big, small,
    dq_ref, dk_ref, dv_ref, half_out, small_out,
    kext, vext, kt, dk_acc, dv_acc, *comm_refs,
):
    i = pl.program_id(1)
    comm = PackSum(devices, 1, big, small, *comm_refs)
    turn = pl.program_id(0) * pl.num_programs(1) + i
    last = comm.steps - 1
    for step, at in enumerate(comm.turns(turns)):

        @pl.when(turn == at)
        def _(step=step):
            comm.step(step)

    n = k_ref.shape[0]
    bq = q_ref.shape[0]

    @pl.when(i == 0)
    def _():
        kext[:, :128] = k_ref[...]
        kext[:, 128:] = kx_ref[...]
        vext[:, :128] = v_ref[...]
        lane = lax.broadcasted_iota(jnp.int32, (n, 128), 1)
        vext[:, 128:] = jnp.where((lane >= 2) & (lane < 5), -1.0, 0.0).astype(BF)
        kt[...] = k_ref[...].T
        dk_acc[...] = jnp.zeros_like(dk_acc)
        dv_acc[...] = jnp.zeros_like(dv_acc)

    q = q_ref[...] * BF(HD**-0.5)
    g = g_ref[...]
    q_t, g_t = q.T, g.T
    prod_t = (g.astype(F32) * c32_ref[...]).T
    zero = jnp.zeros((HD, bq), BF)
    lane = lax.broadcasted_iota(jnp.int32, (bq, 128), 1)
    row = lax.broadcasted_iota(jnp.int32, (EXTRA, bq), 0)
    qx = qx_ref[...].astype(F32)

    def with_rows(base, parts):
        for j, part in enumerate(parts):
            base = jnp.where(row == 2 + j, part.astype(F32), base)
        return base.astype(BF)

    q_ext, g_ext, q_own, g_own, dq_t = [], [], [], [], []
    for h in range(2):
        mine = slice(HD * h, HD * h + HD)
        delta = jnp.sum(prod_t[mine], axis=0, keepdims=True)
        q_rows = with_rows(qx, split3(lse_ref[0, h : h + 1]))
        g_rows = with_rows(jnp.zeros((EXTRA, bq), F32), split3(delta))
        for out, turned, extra in ((q_ext, q_t, q_rows), (g_ext, g_t, g_rows)):
            both = [turned[mine], zero] if h == 0 else [zero, turned[mine]]
            out.append(jnp.concatenate(both + [extra], axis=0))
        ours = (lane < HD) if h == 0 else (lane >= HD)
        q_own.append(jnp.where(ours, q, BF(0)))
        g_own.append(jnp.where(ours, g, BF(0)))
        dq_t.append(jnp.zeros((HD, bq), F32))
    for first in range(0, n, ck):
        keys = slice(first, first + ck)
        dv = jnp.zeros((ck, 128), F32)
        dk = jnp.zeros((ck, 128), F32)
        for h in range(2):
            p = jnp.exp(dot(kext[keys, : 128 + EXTRA], q_ext[h]))
            ds = (p * dot(vext[keys, : 128 + EXTRA], g_ext[h])).astype(BF)
            dv = dv + dot(p.astype(BF), g_own[h])
            dk = dk + dot(ds, q_own[h])
            dq_t[h] = dq_t[h] + dot(kt[HD * h : HD * h + HD, keys], ds)
        dv_acc[keys] += dv
        dk_acc[keys] += dk
    dq_ref[...] = (jnp.concatenate(dq_t, axis=0).T * HD**-0.5).astype(BF)

    @pl.when(i == pl.num_programs(1) - 1)
    def _():
        dk_ref[...] = dk_acc[...].astype(BF)
        dv_ref[...] = dv_acc[...].astype(BF)

    @pl.when(turn == turns - 1)
    def _():
        comm.step(last)
        for part, (start, count, _) in enumerate(comm.parts):
            first, size = comm.region(part, 1)
            half_out[pl.ds(start // 2, size)] = comm.rows(comm.out, first, size)[...]
        small_out[...] = comm.small_box[2 * comm.bits]


def attn_bwd(q, k, v, g, c32, lse, kx, qx, big, small, devices, ident, bq=512, ck=1024):
    n, width = q.shape
    pairs = width // 128
    rows = pl.BlockSpec((bq, 128), lambda p, i: (i, p))
    keys = pl.BlockSpec((n, 128), lambda p, i: (0, p))
    half_shape = (big.shape[0] // 2, big.shape[1])

    def whole(shape):
        return pl.BlockSpec(shape, lambda p, i: (0, 0), pipeline_mode=pl.Buffered(1))

    return pl.pallas_call(
        functools.partial(bwd_kernel, ck, devices, pairs * (n // bq)),
        grid=(pairs, n // bq),
        in_specs=[
            rows,
            keys,
            keys,
            rows,
            rows,
            pl.BlockSpec((1, 2, bq), lambda p, i: (p, 0, i)),
            pl.BlockSpec((n, 128), lambda p, i: (0, 0)),
            pl.BlockSpec((EXTRA, bq), lambda p, i: (0, i)),
            whole(big.shape),
            whole(small.shape),
        ],
        out_specs=[rows, keys, keys, whole(half_shape), whole(small.shape)],
        out_shape=[jax.ShapeDtypeStruct((n, width), BF)] * 3
        + [jax.ShapeDtypeStruct(half_shape, BF), jax.ShapeDtypeStruct(small.shape, F32)],
        scratch_shapes=[
            pltpu.VMEM((n, 256), BF),
            pltpu.VMEM((n, 256), BF),
            pltpu.VMEM((128, n), BF),
            pltpu.VMEM((n, 128), F32),
            pltpu.VMEM((n, 128), F32),
            *PackSum.scratch(*big.shape, small.shape, devices),
        ],
        compiler_params=pltpu.CompilerParams(
            vmem_limit_bytes=ROOM, collective_id=ident, has_side_effects=True
        ),
        cost_estimate=attn_cost(n, width, 5),
        name="attn_bwd",
    )(q, k, v, g, c32, lse, kx, qx, big, small)


def norm_parts(field, norm_gain, norm_shift):
    center = field - jnp.mean(field, axis=-1, keepdims=True)
    inv_std = lax.rsqrt(jnp.mean(center * center, axis=-1, keepdims=True) + NORM_EPSILON)
    normed = center * inv_std
    return (normed * norm_gain + norm_shift, normed, inv_std)


def norm_back(incoming, normed, inv_std, norm_gain):
    scaled = incoming * norm_gain
    return inv_std * (
        scaled
        - jnp.mean(scaled, axis=-1, keepdims=True)
        - normed * jnp.mean(scaled * normed, axis=-1, keepdims=True)
    )


def over_rows(first_op, second_op):
    return dot(first_op, second_op, ((0,), (0,)))


def over_cols(first_op, second_op):
    return dot(first_op, second_op, ((1,), (1,)))


def local(
    activations, cotangent, lengths, dealing, qkv_weight, qv_bias, out_weight, out_bias,
    first_gain, first_shift, up_weight, up_bias, down_weight, down_bias, second_gain, second_shift,
):
    unit = lax.axis_size("dp")
    pack = lax.axis_index("dp")
    core = lax.axis_index("tensor")
    rows = activations.shape[0]
    width = activations.shape[2]
    half = rows // unit // 2

    def swap(x):
        return lax.ppermute(x, "tensor", [(0, 1), (1, 0)])

    core_arg = core.astype(jnp.int32).reshape(1)

    def send(field):
        dealt = deal(field.reshape(rows, width), lengths, dealing, core_arg, unit, half)
        got = lax.all_to_all(dealt.reshape(unit, half, width), "dp", 0, 0, tiled=True)
        return got.reshape(rows // 2, width)

    x_own = send(activations)
    cotangent_own = send(cotangent)
    out_sib, up_sib, down_sib = swap(out_weight), swap(up_weight), swap(down_weight)
    up_bias_sib = swap(up_bias)
    x_all = jnp.concatenate([x_own, swap(x_own)], axis=0)

    at = jnp.arange(rows, dtype=jnp.int32)
    at_core = jnp.where(at < rows // 2, core, 1 - core)
    position = (at_core * half + at % half) * unit + at % (rows // 2) // half
    pair = lax.dynamic_slice_in_dim(dealing, 2 * pack, 2, 0)
    seq_ids = jnp.arange(lengths.shape[0], dtype=jnp.int32)
    pair_len = jnp.sum(jnp.where(pair[:, None] == seq_ids[None, :], lengths[None, :], 0), axis=1)
    split = (pair_len[0] + unit - 1) // unit * unit
    second = position >= split
    live = jnp.where(second, position - split < pair_len[1], position < pair_len[0])
    lane = jnp.arange(128, dtype=jnp.int32)[None, :]
    barred = jnp.where(live & second, 0, jnp.where(live, 1, 2))[:, None]
    key_extra = jnp.where(
        lane < 2,
        jnp.where((lane == barred) | (barred == 2), MASKED_SCORE, 0.0),
        jnp.where(lane < 5, -1.0, 0.0),
    ).astype(BF)
    turn = jnp.arange(EXTRA, dtype=jnp.int32)[:, None]
    query_extra = (turn == second.astype(jnp.int32)[None, :]).astype(BF)

    queries = (dot(x_all, qkv_weight[:, 0]) + qv_bias[0]).astype(BF)
    key_rows = dot(x_all, qkv_weight[:, 1]).astype(BF)
    values = (dot(x_all, qkv_weight[:, 2]) + qv_bias[1]).astype(BF)
    context, context_wide, log_total = attn_fwd(queries, key_rows, values, key_extra, query_extra)
    mine = slice(0, rows // 2)
    theirs = slice(rows // 2, rows)
    context_own = context[mine]
    context_sib = swap(context[theirs])
    attention = dot(context_own, out_weight) + dot(context_sib, out_sib)
    first_out, first_normed, first_inv = norm_parts(
        x_own.astype(F32) + attention + out_bias, first_gain, first_shift
    )
    first_low = first_out.astype(BF)

    def feed(up, bias):
        upward = dot(first_low, up) + bias
        cumulative = 0.5 * (1.0 + lax.erf(upward * math.sqrt(0.5)))
        density = jnp.exp(-0.5 * upward * upward) * (1.0 / math.sqrt(2.0 * math.pi))
        return (upward * cumulative).astype(BF), cumulative + upward * density

    active_own, slope_own = feed(up_weight, up_bias)
    active_sib, slope_sib = feed(up_sib, up_bias_sib)
    downward = dot(active_own, down_weight) + dot(active_sib, down_sib)
    second_out, second_normed, second_inv = norm_parts(
        first_out + downward + down_bias, second_gain, second_shift
    )
    outer = cotangent_own.astype(F32)
    grad_second_gain = jnp.sum(outer * second_normed, axis=0)
    grad_second_shift = jnp.sum(outer, axis=0)
    grad_h2 = norm_back(outer, second_normed, second_inv, second_gain)
    grad_down_bias = jnp.sum(grad_h2, axis=0)
    grad_branch = grad_h2.astype(BF)
    grad_up_own = (over_cols(grad_branch, down_weight) * slope_own).astype(BF)
    grad_up_sib = (over_cols(grad_branch, down_sib) * slope_sib).astype(BF)
    grad_y1 = grad_h2 + over_cols(grad_up_own, up_weight) + over_cols(grad_up_sib, up_sib)
    grad_first_gain = jnp.sum(grad_y1 * first_normed, axis=0)
    grad_first_shift = jnp.sum(grad_y1, axis=0)
    grad_h1 = norm_back(grad_y1, first_normed, first_inv, first_gain)
    grad_out_bias = jnp.sum(grad_h1, axis=0)
    grad_attn = grad_h1.astype(BF)
    grad_context = jnp.concatenate(
        [
            over_cols(grad_attn, out_weight).astype(BF),
            swap(over_cols(grad_attn, out_sib).astype(BF)),
        ],
        axis=0,
    )

    def chip_sum(own_part, sib_part):
        return (own_part + swap(sib_part.astype(BF)).astype(F32)).astype(BF)

    def stacked(parts, rows_of):
        size = sum(part.shape[0] for part in parts)
        pad = -size % rows_of
        if pad:
            parts = parts + [jnp.zeros((pad, parts[0].shape[1]), parts[0].dtype)]
        return jnp.concatenate(parts, axis=0)

    down_part = chip_sum(over_rows(active_own, grad_branch), over_rows(active_sib, grad_branch))
    up_part = chip_sum(over_rows(first_low, grad_up_own), over_rows(first_low, grad_up_sib))
    out_part = chip_sum(over_rows(context_own, grad_attn), over_rows(context_sib, grad_attn))
    up_bias_own = jnp.sum(grad_up_own.astype(F32), axis=0)
    up_bias_part = up_bias_own + swap(jnp.sum(grad_up_sib.astype(F32), axis=0))
    vectors = jnp.stack(
        [
            grad_out_bias,
            grad_first_gain,
            grad_first_shift,
            grad_down_bias,
            grad_second_gain,
            grad_second_shift,
        ]
    )
    vectors = stacked([vectors + swap(vectors), up_bias_part.reshape(-1, width)], 8)
    shard = down_part.shape[0]
    wide_parts = [down_part, out_part] + [
        up_part[:, first : first + width] for first in range(0, shard, width)
    ]
    wide = stacked(wide_parts, 16 * unit)
    grad_queries, grad_keys, grad_values, halves, vectors = attn_bwd(
        queries, key_rows, values, grad_context, context_wide, log_total, key_extra, query_extra,
        wide, vectors, unit, 0,
    )
    input_part = (
        over_cols(grad_queries, qkv_weight[:, 0])
        + over_cols(grad_keys, qkv_weight[:, 1])
        + over_cols(grad_values, qkv_weight[:, 2])
    )
    grad_inputs = (
        grad_h1 + input_part[mine] + swap(input_part[theirs].astype(BF)).astype(F32)
    ).astype(BF)

    def send_back(field):
        got = lax.all_to_all(field.reshape(unit, half, width), "dp", 0, 0, tiled=True)
        return got.reshape(rows // 2, width)

    def settle(got):
        back = undeal(got, swap(got), lengths, dealing, core_arg, unit, half)
        return back.reshape(rows, 1, width)

    pieces = []
    for (start, count), order in zip(cut_rows(wide.shape[0], unit), bit_orders(unit.bit_length() - 1)):
        held = halves[start // 2 : (start + count) // 2]
        step = 2 ** order[0]
        came = lax.ppermute(held, "dp", [(i, i ^ step) for i in range(unit)])
        low = pack // step % 2 == 0
        pieces += [jnp.where(low, held, came), jnp.where(low, came, held)]
    summed = jnp.concatenate(pieces, axis=0)
    grad_down_weight = summed[:shard].astype(F32)
    at_up = shard + out_part.shape[0]
    grad_out_weight = summed[shard:at_up].astype(F32)
    grad_up_weight = jnp.concatenate(
        [summed[first : first + width] for first in range(at_up, at_up + shard, width)], axis=1
    ).astype(F32)
    (
        grad_out_bias,
        grad_first_gain,
        grad_first_shift,
        grad_down_bias,
        grad_second_gain,
        grad_second_shift,
    ) = vectors[:6]
    grad_up_bias = vectors[6 : 6 + shard // width].reshape(-1)

    grad_inputs, grad_queries, grad_keys, grad_values = lax.optimization_barrier(
        (grad_inputs, grad_queries, grad_keys, grad_values)
    )
    output = settle(send_back(second_out.astype(BF)))
    got_inputs = send_back(grad_inputs)
    qkv_parts = [
        over_rows(x_all, grad).astype(BF) for grad in (grad_queries, grad_keys, grad_values)
    ]
    qv_part = jnp.stack([jnp.sum(g.astype(F32), axis=0) for g in (grad_queries, grad_values)])
    summed, qv_sum = pack_sum(stacked(qkv_parts, 16 * unit), stacked([qv_part], 8), unit, 1)
    grad_qkv_weight = jnp.stack(
        [summed[first : first + width] for first in range(0, 3 * width, width)], axis=1
    ).astype(F32)
    grad_qv_bias = qv_sum[:2]
    (
        got_inputs,
        output,
        grad_qkv_weight,
        grad_out_weight,
        grad_up_weight,
        grad_down_weight,
    ) = lax.optimization_barrier(
        (
            got_inputs,
            output,
            grad_qkv_weight,
            grad_out_weight,
            grad_up_weight,
            grad_down_weight,
        )
    )
    input_grad = settle(got_inputs)
    return (
        output,
        input_grad,
        grad_qkv_weight,
        grad_qv_bias,
        grad_out_weight,
        grad_out_bias,
        grad_first_gain,
        grad_first_shift,
        grad_up_weight,
        grad_up_bias,
        grad_down_weight,
        grad_down_bias,
        grad_second_gain,
        grad_second_shift,
    )


def solution(mesh):
    placed = (
        P(None, "dp", None),
        P(None, "dp", None),
        P(),
        P(),
        P(None, None, "tensor"),
        P(None, "tensor"),
        P("tensor", None),
        P(),
        P(),
        P(),
        P(None, "tensor"),
        P("tensor"),
        P("tensor", None),
        P(),
        P(),
        P(),
    )
    return jax.shard_map(
        local,
        mesh=mesh,
        in_specs=placed,
        out_specs=(
            P(None, "dp", None),
            P(None, "dp", None),
            P(None, None, "tensor"),
            P(None, "tensor"),
            P("tensor", None),
            P(),
            P(),
            P(),
            P(None, "tensor"),
            P("tensor"),
            P("tensor", None),
            P(),
            P(),
            P(),
        ),
        check_vma=False,
    )
```

```python
import functools
import math

import jax
import jax.numpy as jnp
from jax import lax
from jax.experimental import pallas as pl
from jax.experimental.pallas import tpu as pltpu
from jax.sharding import PartitionSpec as P

HD = 64
BF = jnp.bfloat16
F32 = jnp.float32
MASKED_SCORE = -1e30
NORM_EPSILON = 1e-05
EXTRA = 16
ROOM = 56 * 2**20


def dot(a, b, dims=((1,), (0,))):
    return lax.dot_general(a, b, (dims, ((), ())), preferred_element_type=F32)


def unit_starts(lengths, starts, unit):
    def step(s, total):
        starts[s] = total
        return total + (lengths[s] + unit - 1) // unit

    lax.fori_loop(0, lengths.shape[0], step, jnp.int32(0))


def pack_windows(lengths, dealing, starts, unit, pack, first, rows, total):
    seq_a = dealing[2 * pack]
    seq_b = dealing[2 * pack + 1]
    units_a = (lengths[seq_a] + unit - 1) // unit
    shift_a = starts[seq_a]
    shift_b = starts[seq_b] - units_a
    bases = []
    for shift in (shift_a, shift_b):
        base = jnp.clip((shift + first) // 16 * 16, 0, total - rows - 16)
        bases.append(pl.multiple_of(base, 16))
    return units_a, shift_a, shift_b, bases


def plan_kernel(unit, half, lengths, dealing, table, kx_ref, qx_ref, starts):
    unit_starts(lengths, starts, unit)

    def one(pack, carry):
        units_a = (lengths[dealing[2 * pack]] + unit - 1) // unit
        table[0, pack] = units_a
        table[1, pack] = starts[dealing[2 * pack]]
        table[2, pack] = starts[dealing[2 * pack + 1]] - units_a
        return carry

    lax.fori_loop(0, unit, one, 0)
    pack = lax.axis_index("dp")
    core = lax.axis_index("tensor")
    len_a, len_b = lengths[dealing[2 * pack]], lengths[dealing[2 * pack + 1]]
    split = (len_a + unit - 1) // unit * unit
    rows = kx_ref.shape[0]

    def place(at):
        at_core = jnp.where(at < rows // 2, core, 1 - core)
        return (at_core * half + at % half) * unit + at % (rows // 2) // half

    row = place(lax.broadcasted_iota(jnp.int32, kx_ref.shape, 0))
    lane = lax.broadcasted_iota(jnp.int32, kx_ref.shape, 1)
    later = row >= split
    live = row < jnp.where(later, split + len_b, len_a)
    barred = (lane == jnp.where(later, 0, 1)) | ~live
    kx_ref[...] = jnp.where(
        lane < 2, jnp.where(barred, MASKED_SCORE, 0.0), jnp.where(lane < 5, -1.0, 0.0)
    ).astype(BF)
    col = place(lax.broadcasted_iota(jnp.int32, qx_ref.shape, 1))
    turn = lax.broadcasted_iota(jnp.int32, qx_ref.shape, 0)
    qx_ref[...] = jnp.where(turn == jnp.where(col >= split, 1, 0), 1.0, 0.0).astype(BF)


def plan(lengths, dealing, rows, unit, half):
    smem = pl.BlockSpec(memory_space=pltpu.SMEM)
    vmem = pl.BlockSpec(memory_space=pltpu.VMEM)
    return pl.pallas_call(
        functools.partial(plan_kernel, unit, half),
        in_specs=[smem, smem],
        out_specs=[smem, vmem, vmem],
        out_shape=[
            jax.ShapeDtypeStruct((3, unit), jnp.int32),
            jax.ShapeDtypeStruct((rows, 128), BF),
            jax.ShapeDtypeStruct((EXTRA, rows), BF),
        ],
        scratch_shapes=[pltpu.SMEM(lengths.shape, jnp.int32)],
        name="plan",
    )(lengths, dealing)


def greet(count, with_sibling=True):
    barrier = pltpu.get_barrier_semaphore()
    me = lax.axis_index("dp")

    def one(k, carry):
        pl.semaphore_signal(
            barrier, 1, device_id={"dp": (me + k) % count}, device_id_type=pl.DeviceIdType.MESH
        )
        return carry

    lax.fori_loop(1, count, one, 0)
    pl.semaphore_signal(
        barrier,
        1,
        device_id={"tensor": 1 - lax.axis_index("tensor")},
        device_id_type=pl.DeviceIdType.MESH,
    )
    pl.semaphore_wait(barrier, count)


class PackExchange:
    def __init__(self, count, block, source, target, send_sem, recv_sem):
        self.count, self.block = count, block
        self.source, self.target = source, target
        self.send_sem, self.recv_sem = send_sem, recv_sem
        self.me = lax.axis_index("dp")

    def rows(self, ref, i):
        return ref.at[pl.ds(pl.multiple_of(i * self.block, 16), self.block)]

    def copy(self, peer, landing, sem):
        return pltpu.make_async_remote_copy(
            src_ref=self.rows(self.source, peer),
            dst_ref=self.rows(self.target, landing),
            send_sem=self.send_sem.at[peer],
            recv_sem=self.recv_sem.at[sem],
            device_id={"dp": peer},
            device_id_type=pl.DeviceIdType.MESH,
        )

    def send(self, peer):
        self.copy(peer, self.me, self.me).start()

    def wait_from(self, peer):
        self.copy(peer, peer, peer).wait_recv()

    def wait_sent(self, peer):
        self.copy(peer, self.me, self.me).wait_send()

    def peers(self, body):
        def one(i, carry):
            far = self.count // 2 * (1 + (i + 1) % 2) - 1 - i // 2
            body(self.across(self.me, far, self.count))
            return carry

        lax.fori_loop(0, self.count - 1, one, 0)

    @staticmethod
    def across(index, far, count):
        peer = 0
        for bit in range(count.bit_length() - 1):
            weight = 2**bit
            peer += (index // weight % 2 + far // weight % 2) % 2 * weight
        return peer

    def keep_own(self):
        self.rows(self.target, self.me)[...] = self.rows(self.source, self.me)[...]


def to_sibling(source, target, send_sem, recv_sem):
    return pltpu.make_async_remote_copy(
        src_ref=source,
        dst_ref=target,
        send_sem=send_sem,
        recv_sem=recv_sem,
        device_id={"tensor": 1 - lax.axis_index("tensor")},
        device_id_type=pl.DeviceIdType.MESH,
    )


def deal_kernel(
    unit, half, table, x_ref, g_hbm, own_ref, sib_ref, dealt_g,
    outbox, g_ref, load_sem, send_sem, recv_sem, pass_sem, take_sem,
):
    total = x_ref.shape[0]
    load = pltpu.make_async_copy(g_hbm, g_ref, load_sem)
    load.start()
    greet(unit)
    first = lax.axis_index("tensor") * half
    slot = first + lax.broadcasted_iota(jnp.int32, (half, total), 0)
    col = lax.broadcasted_iota(jnp.int32, (half, total), 1)
    swap = PackExchange(unit, half, outbox, own_ref, send_sem, recv_sem)
    team = 4

    def dealt(ref, packs, target):
        picks = []
        for i in range(team):
            pack = packs * team + i
            shift = jnp.where(slot < table[0, pack], table[1, pack], table[2, pack])
            picks.append(jnp.where(col == slot + shift, 1.0, 0.0).astype(BF))
        rows = dot(jnp.concatenate(picks, axis=0), ref[...]).astype(BF)
        at = pl.multiple_of(packs * team * half, 16)
        target[pl.ds(at, team * half)] = rows

    def passed(pack):
        return to_sibling(
            swap.rows(own_ref, pack), swap.rows(sib_ref, pack), pass_sem.at[pack], take_sem.at[pack]
        )

    def pass_on(pack):
        swap.wait_from(pack)
        passed(pack).start()

    home = swap.me // team

    def deal_out(i, carry):
        packs = swap.across(home, unit // team - 1 - i, unit // team)
        dealt(x_ref, packs, outbox)

        def send(j, carry):
            pack = packs * team + j

            @pl.when(pack != swap.me)
            def _():
                swap.send(pack)

            return carry

        lax.fori_loop(0, team, send, 0)
        return carry

    lax.fori_loop(0, unit // team, deal_out, 0)
    swap.keep_own()
    passed(swap.me).start()
    load.wait()

    def keep(packs, carry):
        dealt(g_ref, packs, dealt_g)
        return carry

    lax.fori_loop(0, unit // team, keep, 0)
    swap.peers(pass_on)
    swap.peers(swap.wait_sent)

    def end(pack, carry):
        passed(pack).wait_recv()
        passed(pack).wait_send()
        return carry

    lax.fori_loop(0, unit, end, 0)


def deal(x, g, table, unit, half, ident):
    total, width = x.shape
    smem = pl.BlockSpec(memory_space=pltpu.SMEM)
    vmem = pl.BlockSpec(memory_space=pltpu.VMEM)
    return pl.pallas_call(
        functools.partial(deal_kernel, unit, half),
        in_specs=[smem, vmem, pl.BlockSpec(memory_space=pl.ANY)],
        out_specs=[vmem, vmem, vmem],
        out_shape=[jax.ShapeDtypeStruct((total // 2, width), BF)] * 3,
        scratch_shapes=[
            pltpu.VMEM((total // 2, width), BF),
            pltpu.VMEM((total, width), BF),
            pltpu.SemaphoreType.DMA,
            *[pltpu.SemaphoreType.DMA((unit,))] * 4,
        ],
        compiler_params=pltpu.CompilerParams(
            vmem_limit_bytes=ROOM, collective_id=ident, has_side_effects=True
        ),
        cost_estimate=pl.CostEstimate(
            flops=8 * total * width * half, bytes_accessed=40 * total * width, transcendentals=0
        ),
        name="deal",
    )(table, x, g)


def undeal_kernel(unit, half, lengths, dealing, core, own_ref, sib_ref, o_ref, starts):
    total = o_ref.shape[0]
    unit_starts(lengths, starts, unit)
    wide = half + 16
    row = lax.broadcasted_iota(jnp.int32, (2 * wide, half), 0)
    col = lax.broadcasted_iota(jnp.int32, (2 * wide, half), 1)
    o_ref[...] = jnp.zeros_like(o_ref)

    def one(pack, carry):
        for part, ref in ((core[0], own_ref), (1 - core[0], sib_ref)):
            first = part * half
            units_a, shift_a, shift_b, (base_a, base_b) = pack_windows(
                lengths, dealing, starts, unit, pack, first, half, total
            )
            slot = first + col
            near = slot < units_a
            at = jnp.where(near, slot + (shift_a - base_a), slot + (shift_b - base_b + wide))
            pick = (row == at) & (near == (row < wide))
            rows = ref[pl.ds(pl.multiple_of(pack * half, 16), half), :]
            both = dot(pick.astype(F32).astype(BF), rows).astype(BF)
            o_ref[pl.ds(base_a, wide), :] += both[:wide]
            o_ref[pl.ds(base_b, wide), :] += both[wide:]
        return carry

    lax.fori_loop(0, total // (2 * half), one, 0, unroll=2)


def undeal(own, sib, lengths, dealing, core, unit, half):
    total, width = 2 * own.shape[0], own.shape[1]
    smem = pl.BlockSpec(memory_space=pltpu.SMEM)
    vmem = pl.BlockSpec(memory_space=pltpu.VMEM)
    return pl.pallas_call(
        functools.partial(undeal_kernel, unit, half),
        in_specs=[smem, smem, smem, vmem, vmem],
        out_specs=vmem,
        out_shape=jax.ShapeDtypeStruct((total, width), BF),
        scratch_shapes=[pltpu.SMEM(lengths.shape, jnp.int32)],
        compiler_params=pltpu.CompilerParams(vmem_limit_bytes=ROOM),
        cost_estimate=pl.CostEstimate(
            flops=8 * total * width * half, bytes_accessed=4 * total * width, transcendentals=0
        ),
        name="undeal",
    )(lengths, dealing, core, own, sib)


def fwd_kernel(
    ck, unit, half, x_own, x_sib, w_ref, b_ref, kx_ref, qx_ref, dealt_g,
    q_ref, k_ref, v_ref, c_ref, c_other_out, c32_ref, lse_ref, got_g_out,
    kext, vt, c_sib, c_other, got_g, send_sem, recv_sem, pass_sem, take_sem,
):
    n = k_ref.shape[0]
    pair = pl.program_id(0)
    swap = PackExchange(unit, half, dealt_g, got_g, send_sem, recv_sem)

    def passed(pair):
        cols = pl.ds(pl.multiple_of(pair * 128, 128), 128)
        return to_sibling(
            c_sib.at[:, cols], c_other.at[:, cols], pass_sem.at[pair], take_sem.at[pair]
        )

    @pl.when(pair == 0)
    def _():
        greet(unit)
        swap.peers(swap.send)
        swap.keep_own()

    w = jnp.concatenate([w_ref[0], w_ref[1], w_ref[2]], axis=1)
    bias = jnp.concatenate([b_ref[0:1], jnp.zeros((1, 128), F32), b_ref[1:2]], axis=1)
    for part, x_ref in enumerate((x_own, x_sib)):
        for first in range(0, n // 2, 512):
            made = (dot(x_ref[first : first + 512], w) + bias).astype(BF)
            at = slice(part * n // 2 + first, part * n // 2 + first + 512)
            for j, ref in enumerate((q_ref, k_ref, v_ref)):
                ref[at] = made[:, 128 * j : 128 * j + 128]
    kext[:, :128] = k_ref[...]
    kext[:, 128:] = kx_ref[...]
    v_t = v_ref[...].T
    ones = jnp.where(lax.broadcasted_iota(jnp.int32, (EXTRA, n), 0) == 0, 1.0, 0.0).astype(BF)
    for h in range(2):
        vt[h, :HD] = v_t[HD * h : HD * h + HD]
        vt[h, HD:] = ones
    q_t = (q_ref[...] * BF(HD**-0.5)).T
    zero = jnp.zeros((HD, n), BF)
    qx = qx_ref[...]
    q_ext = [
        jnp.concatenate([q_t[:HD], zero, qx], axis=0),
        jnp.concatenate([zero, q_t[HD:], qx], axis=0),
    ]
    tops, sums = [None, None], [None, None]
    for first in range(0, n, ck):
        keys = slice(first, first + ck)
        for h in range(2):
            s = dot(kext[keys, : 128 + EXTRA], q_ext[h])
            top = jnp.max(s, axis=0, keepdims=True)
            if first:
                top = jnp.maximum(tops[h], top)
            part = dot(vt[h, :, keys], jnp.exp(s - top).astype(BF))
            if first:
                part = part + sums[h] * jnp.exp(tops[h] - top)
            tops[h], sums[h] = top, part
    outs = []
    for h in range(2):
        total = sums[h][HD : HD + 1]
        outs.append(sums[h][:HD] / total)
        lse_ref[0, h : h + 1] = tops[h] + jnp.log(total)
    c = jnp.concatenate(outs, axis=0).T
    c32_ref[...] = c
    c_ref[...] = c[: n // 2].astype(BF)
    c_sib[:, pl.ds(pl.multiple_of(pair * 128, 128), 128)] = c[n // 2 :].astype(BF)
    passed(pair).start()

    @pl.when(pair == pl.num_programs(0) - 1)
    def _():
        swap.peers(swap.wait_from)
        swap.peers(swap.wait_sent)

        def end(pair, carry):
            passed(pair).wait_recv()
            passed(pair).wait_send()
            return carry

        lax.fori_loop(0, pl.num_programs(0), end, 0)
        c_other_out[...] = c_other[...]
        got_g_out[...] = got_g[...]


def attn_cost(n, width, products):
    return pl.CostEstimate(
        flops=products * 2 * 4 * n * n * width,
        bytes_accessed=16 * n * width,
        transcendentals=n * n * width // HD,
    )


def attn_fwd(x_own, x_sib, w, b, kx, qx, dealt_g, unit, half, ident, ck=512):
    n, model = 2 * x_own.shape[0], x_own.shape[1]
    width = w.shape[2]
    pairs = width // 128
    keys = pl.BlockSpec((n, 128), lambda p: (0, p))

    def whole(shape):
        return pl.BlockSpec(shape, lambda p: (0, 0), pipeline_mode=pl.Buffered(1))

    return pl.pallas_call(
        functools.partial(fwd_kernel, ck, unit, half),
        grid=(pairs,),
        in_specs=[
            whole(x_own.shape),
            whole(x_sib.shape),
            pl.BlockSpec((3, model, 128), lambda p: (0, 0, p)),
            pl.BlockSpec((2, 128), lambda p: (0, p)),
            whole(kx.shape),
            whole(qx.shape),
            whole(dealt_g.shape),
        ],
        out_specs=[
            keys,
            keys,
            keys,
            pl.BlockSpec((n // 2, 128), lambda p: (0, p)),
            whole((n // 2, width)),
            keys,
            pl.BlockSpec((1, 2, n), lambda p: (p, 0, 0)),
            whole(dealt_g.shape),
        ],
        out_shape=[jax.ShapeDtypeStruct((n, width), BF)] * 3
        + [jax.ShapeDtypeStruct((n // 2, width), BF)] * 2
        + [
            jax.ShapeDtypeStruct((n, width), F32),
            jax.ShapeDtypeStruct((pairs, 2, n), F32),
            jax.ShapeDtypeStruct(dealt_g.shape, BF),
        ],
        scratch_shapes=[
            pltpu.VMEM((n, 256), BF),
            pltpu.VMEM((2, HD + EXTRA, n), BF),
            pltpu.VMEM((n // 2, width), BF),
            pltpu.VMEM((n // 2, width), BF),
            pltpu.VMEM(dealt_g.shape, BF),
            *[pltpu.SemaphoreType.DMA((unit,))] * 2,
            *[pltpu.SemaphoreType.DMA((pairs,))] * 2,
        ],
        compiler_params=pltpu.CompilerParams(
            vmem_limit_bytes=ROOM, collective_id=ident, has_side_effects=True
        ),
        cost_estimate=attn_cost(n, width, 2),
        name="attn_fwd",
    )(x_own, x_sib, w, b, kx, qx, dealt_g)


def split3(x):
    high = x.astype(BF)
    rest = x - high.astype(F32)
    middle = rest.astype(BF)
    return high, middle, (rest - middle.astype(F32)).astype(BF)


def bit_orders(bits):
    first = list(range(bits))
    second = [1, 2, 0] + list(range(3, bits))
    third = [2, 0, 1] + list(range(3, bits))
    return first, second, third


def row_unit(devices):
    return 8 * devices


def cut_rows(rows, devices):
    unit = row_unit(devices)
    units = rows // unit
    counts = [(units + 2) // 3, (units + 1) // 3, units // 3]
    starts = [0, counts[0], counts[0] + counts[1]]
    return [(s * unit, c * unit) for s, c in zip(starts, counts) if c]


def greet_partners(bits):
    me = lax.axis_index("dp")
    barrier = pltpu.get_barrier_semaphore()
    for bit in range(bits):
        pl.semaphore_signal(
            barrier,
            inc=1,
            device_id={"dp": me + (1 - 2 * (me // 2**bit % 2)) * 2**bit},
            device_id_type=pl.DeviceIdType.MESH,
        )
    pl.semaphore_wait(barrier, bits)


class PackSum:
    def __init__(self, devices, big, small, out, came, acc, inbox, small_box, send_sem, recv_sem):
        self.came = came
        self.bits = devices.bit_length() - 1
        self.me = lax.axis_index("dp")
        self.big, self.small, self.acc, self.inbox, self.out = big, small, acc, inbox, out
        self.small_box = small_box
        self.send_sem, self.recv_sem = send_sem, recv_sem
        self.parts = [
            (start, count, order)
            for (start, count), order in zip(cut_rows(big.shape[0], devices), bit_orders(self.bits))
        ]
        self.steps = 2 * self.bits

    def slots(self, first, slot_us, last):
        size = 4e-3 * self.big.shape[0] * self.big.shape[1]
        sizes = [size / 2 ** (level + 1) / 3 for level in range(self.bits - 1)]
        sizes = sizes + [size / 2 ** (self.bits - 2)] + sizes[::-1]
        at, out = 0.0, []
        for step in range(self.steps):
            out.append(min(last, first + math.ceil(at / slot_us)))
            if step < len(sizes) and not (step == 0 and self.came):
                at += 4.5 + sizes[step] / 80
        return out

    @staticmethod
    def scratch(rows, cols, small_shape, devices):
        bits = devices.bit_length() - 1
        return [
            pltpu.VMEM((rows // 2, cols), BF),
            pltpu.VMEM((rows, cols), BF),
            pltpu.VMEM((2 * bits + 1,) + small_shape, F32),
            pltpu.SemaphoreType.DMA((4, 2 * bits)),
            pltpu.SemaphoreType.DMA((4, 2 * bits)),
        ]

    def side(self, bit):
        return (self.me // 2**bit) % 2

    def partner(self, bit):
        return self.me + (1 - 2 * self.side(bit)) * 2**bit

    def region(self, part, level):
        start, count, order = self.parts[part]
        for done in range(level):
            start = start + self.side(order[done]) * (count // 2 ** (done + 1))
        return start, count // 2**level

    def halved(self, part, start):
        return self.parts[part][0] // 2 + start - self.region(part, 1)[0]

    def rows(self, ref, start, count):
        return ref.at[pl.ds(pl.multiple_of(start, 16), count)]

    def slot(self, part, level):
        start, count, _ = self.parts[part]
        return start + count - count // 2**level

    def sending(self, part, level):
        start, count = self.region(part, level)
        bit = self.parts[part][2][level]
        if level < self.bits - 1:
            count = count // 2
            start = start + (1 - self.side(bit)) * count
        return pltpu.make_async_remote_copy(
            src_ref=self.rows(self.acc, self.halved(part, start), count)
            if level
            else self.rows(self.big, start, count),
            dst_ref=self.inbox.at[pl.ds(self.slot(part, level), count)],
            send_sem=self.send_sem.at[part, level],
            recv_sem=self.recv_sem.at[part, level],
            device_id={"dp": self.partner(bit)},
            device_id_type=pl.DeviceIdType.MESH,
        )

    def doubling(self, part, level):
        mine = self.rows(self.out, *self.region(part, level + 1))
        return pltpu.make_async_remote_copy(
            src_ref=mine,
            dst_ref=mine,
            send_sem=self.send_sem.at[part, self.bits + level],
            recv_sem=self.recv_sem.at[part, self.bits + level],
            device_id={"dp": self.partner(self.parts[part][2][level])},
            device_id_type=pl.DeviceIdType.MESH,
        )

    def exchange(self, level):
        return pltpu.make_async_remote_copy(
            src_ref=self.small if level == 0 else self.small_box.at[self.bits + level],
            dst_ref=self.small_box.at[level],
            send_sem=self.send_sem.at[3, level],
            recv_sem=self.recv_sem.at[3, level],
            device_id={"dp": self.partner(level)},
            device_id_type=pl.DeviceIdType.MESH,
        )

    def add(self, part, level):
        last = level == self.bits - 1
        kept, count = self.region(part, level if last else level + 1)
        source, first = (self.acc, self.halved(part, kept)) if level else (self.big, kept)
        if last:
            target, goal = self.out, kept
        else:
            target, goal = self.acc, self.halved(part, kept)
        slot, box = self.slot(part, level), self.inbox
        if self.came and level == 0:
            slot, box = 0, self.came[part]
        tile = math.gcd(count, 64)

        def one(i, carry):
            def at(start):
                return pl.ds(pl.multiple_of(start + i * tile, 16), tile)

            total = source[at(first), :].astype(F32) + box[at(slot), :].astype(F32)
            target[at(goal), :] = total.astype(BF)
            return carry

        lax.fori_loop(0, count // tile, one, 0)

    def step(self, k):
        bits = self.bits
        for part in range(len(self.parts)):
            if 0 < k <= bits:
                if not (self.came and k == 1):
                    self.sending(part, k - 1).wait_recv()
                self.add(part, k - 1)
            elif k > bits:
                self.doubling(part, 2 * bits - 1 - k).wait_recv()
            if k < bits:
                self.sending(part, k).start()
            elif k < self.steps - 1:
                self.doubling(part, 2 * bits - 2 - k).start()
        if self.small is not None:
            if 0 < k <= bits:
                self.exchange(k - 1).wait_recv()
                held = self.small[...] if k == 1 else self.small_box[bits + k - 1]
                self.small_box[bits + k] = held + self.small_box[k - 1]
            if k < bits:
                self.exchange(k).start()
        if k == self.steps - 1:
            for part in range(len(self.parts)):
                for level in range(1 if self.came else 0, bits):
                    self.sending(part, level).wait_send()
                for level in range(bits - 1):
                    self.doubling(part, level).wait_send()
            if self.small is not None:
                for level in range(bits):
                    self.exchange(level).wait_send()


SLOT_US = 3.6


def bwd_kernel(
    ck, devices, turns, q_ref, k_ref, v_ref, g_ref, c32_ref, lse_ref, kx_ref, qx_ref,
    x_own, x_sib, w_ref, big_a, big_b, small, *refs,
):
    i = pl.program_id(1)
    n = k_ref.shape[0]
    bq = q_ref.shape[0]
    count = len(cut_rows(big_a.shape[0], devices))
    came, refs = refs[:count], refs[count:]
    dx_ref, dx_sib_ref, dw_ref, db_ref, small_out, out_a, out_b = refs[:7]
    kext, vext, kt, x_t, dq_acc, dk_acc, dv_acc, dx_sib, sum_a, sum_b, *comm_refs = refs[7:]
    comm_a = PackSum(devices, big_a, None, sum_a, came, *comm_refs[:5])
    comm_b = PackSum(devices, big_b, small, sum_b, None, *comm_refs[5:])
    turn = pl.program_id(0) * pl.num_programs(1) + i
    per_turn = n // ck
    slots = turns * per_turn
    slots_a = comm_a.slots(0, SLOT_US, slots)
    slots_b = comm_b.slots(0, SLOT_US, slots)

    def comm_at(which):
        for comm, at in ((comm_a, slots_a), (comm_b, slots_b)):
            for step, slot in enumerate(at):
                if step == 0 and comm.came:
                    continue
                if slot < slots and slot % per_turn == which:

                    @pl.when(turn == slot // per_turn)
                    def _(comm=comm, step=step):
                        comm.step(step)

                elif slot == slots and which is None:
                    comm.step(step)

    @pl.when(turn == 0)
    def _():
        greet_partners(comm_a.bits)

    @pl.when(i == 0)
    def _():
        kext[:, :128] = k_ref[...]
        kext[:, 128:] = kx_ref[...]
        vext[:, :128] = v_ref[...]
        lane = lax.broadcasted_iota(jnp.int32, (n, 128), 1)
        vext[:, 128:] = jnp.where((lane >= 2) & (lane < 5), -1.0, 0.0).astype(BF)
        kt[...] = k_ref[...].T
        dk_acc[...] = jnp.zeros_like(dk_acc)
        dv_acc[...] = jnp.zeros_like(dv_acc)

    q = q_ref[...] * BF(HD**-0.5)
    g = g_ref[...]
    q_t, g_t = q.T, g.T
    prod_t = (g.astype(F32) * c32_ref[...]).T
    zero = jnp.zeros((HD, bq), BF)
    lane = lax.broadcasted_iota(jnp.int32, (bq, 128), 1)
    row = lax.broadcasted_iota(jnp.int32, (EXTRA, bq), 0)
    qx = qx_ref[...].astype(F32)

    def with_rows(base, parts):
        for j, part in enumerate(parts):
            base = jnp.where(row == 2 + j, part.astype(F32), base)
        return base.astype(BF)

    q_ext, g_ext, q_own, g_own, dq_t = [], [], [], [], []
    for h in range(2):
        mine = slice(HD * h, HD * h + HD)
        delta = jnp.sum(prod_t[mine], axis=0, keepdims=True)
        q_rows = with_rows(qx, split3(lse_ref[0, h : h + 1]))
        g_rows = with_rows(jnp.zeros((EXTRA, bq), F32), split3(delta))
        for out, turned, extra in ((q_ext, q_t, q_rows), (g_ext, g_t, g_rows)):
            both = [turned[mine], zero] if h == 0 else [zero, turned[mine]]
            out.append(jnp.concatenate(both + [extra], axis=0))
        ours = (lane < HD) if h == 0 else (lane >= HD)
        q_own.append(jnp.where(ours, q, BF(0)))
        g_own.append(jnp.where(ours, g, BF(0)))
        dq_t.append(jnp.zeros((HD, bq), F32))
    for first in range(0, n, ck):
        comm_at(first // ck)
        keys = slice(first, first + ck)
        dv = jnp.zeros((ck, 128), F32)
        dk = jnp.zeros((ck, 128), F32)
        for h in range(2):
            p = jnp.exp(dot(kext[keys, : 128 + EXTRA], q_ext[h]))
            ds = (p * dot(vext[keys, : 128 + EXTRA], g_ext[h])).astype(BF)
            dv = dv + dot(p.astype(BF), g_own[h])
            dk = dk + dot(ds, q_own[h])
            dq_t[h] = dq_t[h] + dot(kt[HD * h : HD * h + HD, keys], ds)
        dv_acc[keys] += dv
        dk_acc[keys] += dk
    dq = jnp.concatenate(dq_t, axis=0).T * HD**-0.5
    dq_acc[pl.ds(pl.multiple_of(i * bq, bq), bq)] = dq.astype(BF)

    @pl.when(turn == 0)
    def _():
        x_t[:, : n // 2] = x_own[...].T
        x_t[:, n // 2 :] = x_sib[...].T
        dx_ref[...] = jnp.zeros_like(dx_ref)
        dx_sib[...] = jnp.zeros_like(dx_sib)

    @pl.when(i == pl.num_programs(1) - 1)
    def _():
        width = x_own.shape[1]
        grads = [dq_acc[...], dk_acc[...].astype(BF), dv_acc[...].astype(BF)]
        joined = jnp.concatenate(grads, axis=1)
        made = dot(x_t[...], joined).astype(BF)
        for j in range(3):
            dw_ref[j * width : (j + 1) * width] = made[:, 128 * j : 128 * j + 128]
        bias = [jnp.sum(grad.astype(F32), axis=0, keepdims=True) for grad in grads[::2]]
        db_ref[...] = jnp.concatenate(bias + [jnp.zeros((6, 128), F32)], axis=0)
        tile = 512
        planes = jnp.concatenate([w_ref[j] for j in range(3)], axis=1)
        for first in range(0, n, tile):
            to_x = dot(joined[first : first + tile], planes, ((1,), (1,)))
            target, goal = (dx_ref, first) if first < n // 2 else (dx_sib, first - n // 2)
            target[goal : goal + tile] += to_x

    @pl.when(turn == turns - 1)
    def _():
        comm_at(None)
        dx_sib_ref[...] = dx_sib[...].astype(BF)
        out_a[...] = sum_a[...]
        out_b[...] = sum_b[...]
        small_out[...] = comm_b.small_box[2 * comm_b.bits]


def attn_bwd(q, k, v, g, c32, lse, kx, qx, x_own, x_sib, w, big_a, big_b, small, came, devices, ident, bq=1024, ck=512):
    n, width = q.shape
    pairs = width // 128
    model = x_own.shape[1]
    rows = pl.BlockSpec((bq, 128), lambda p, i: (i, p))
    keys = pl.BlockSpec((n, 128), lambda p, i: (0, p))
    def whole(shape):
        return pl.BlockSpec(shape, lambda p, i: (0, 0), pipeline_mode=pl.Buffered(1))

    return pl.pallas_call(
        functools.partial(bwd_kernel, ck, devices, pairs * (n // bq)),
        grid=(pairs, n // bq),
        in_specs=[
            rows,
            keys,
            keys,
            rows,
            rows,
            pl.BlockSpec((1, 2, bq), lambda p, i: (p, 0, i)),
            pl.BlockSpec((n, 128), lambda p, i: (0, 0)),
            pl.BlockSpec((EXTRA, bq), lambda p, i: (0, i)),
            whole(x_own.shape),
            whole(x_sib.shape),
            pl.BlockSpec((3, model, 128), lambda p, i: (0, 0, p)),
            whole(big_a.shape),
            whole(big_b.shape),
            whole(small.shape),
            *[whole(box.shape) for box in came],
        ],
        out_specs=[
            whole((n // 2, model)),
            whole((n // 2, model)),
            pl.BlockSpec((3 * model, 128), lambda p, i: (0, p)),
            pl.BlockSpec((8, 128), lambda p, i: (0, p)),
            whole(small.shape),
            whole(big_a.shape),
            whole(big_b.shape),
        ],
        out_shape=[
            jax.ShapeDtypeStruct((n // 2, model), F32),
            jax.ShapeDtypeStruct((n // 2, model), BF),
            jax.ShapeDtypeStruct((3 * model, width), BF),
            jax.ShapeDtypeStruct((8, width), F32),
            jax.ShapeDtypeStruct(small.shape, F32),
            jax.ShapeDtypeStruct(big_a.shape, BF),
            jax.ShapeDtypeStruct(big_b.shape, BF),
        ],
        scratch_shapes=[
            pltpu.VMEM((n, 256), BF),
            pltpu.VMEM((n, 256), BF),
            pltpu.VMEM((128, n), BF),
            pltpu.VMEM((model, n), BF),
            pltpu.VMEM((n, 128), BF),
            pltpu.VMEM((n, 128), F32),
            pltpu.VMEM((n, 128), F32),
            pltpu.VMEM((n // 2, model), F32),
            pltpu.VMEM(big_a.shape, BF),
            pltpu.VMEM(big_b.shape, BF),
            *PackSum.scratch(*big_a.shape, (8, 128), devices),
            *PackSum.scratch(*big_b.shape, small.shape, devices),
        ],
        compiler_params=pltpu.CompilerParams(
            vmem_limit_bytes=60 * 2**20, collective_id=ident, has_side_effects=True
        ),
        cost_estimate=attn_cost(n, width, 5),
        name="attn_bwd",
    )(q, k, v, g, c32, lse, kx, qx, x_own, x_sib, w, big_a, big_b, small, *came)


def tail_kernel(
    unit, half, h1_ref, dx_ref, dx_sib, big, small, own_ref, sib_ref, big_out, small_out,
    outbox, dx_came, mix_sem, mixed_sem, send_sem, recv_sem, pass_sem, take_sem, *comm_refs,
):
    comm = PackSum(unit, big, small, big_out, None, *comm_refs)
    swap = PackExchange(unit, half, outbox, own_ref, send_sem, recv_sem)

    def mix(pack):
        return to_sibling(
            swap.rows(dx_sib, pack),
            swap.rows(dx_came, pack),
            mix_sem.at[pack],
            mixed_sem.at[pack],
        )

    def passed(pack):
        return to_sibling(
            swap.rows(own_ref, pack), swap.rows(sib_ref, pack), pass_sem.at[pack], take_sem.at[pack]
        )

    def add_up(pack):
        mix(pack).wait_recv()
        at = swap.rows(dx_came, pack)[...].astype(F32)
        total = swap.rows(h1_ref, pack)[...] + swap.rows(dx_ref, pack)[...] + at
        swap.rows(outbox, pack)[...] = total.astype(BF)

    def add_and_send(pack):
        add_up(pack)
        swap.send(pack)

    def pass_on(pack):
        swap.wait_from(pack)
        passed(pack).start()

    greet(unit)
    swap.peers(lambda pack: mix(pack).start())
    mix(swap.me).start()
    comm.step(0)
    swap.peers(add_and_send)
    add_up(swap.me)
    swap.keep_own()
    passed(swap.me).start()
    comm.step(1)
    for k in range(2, comm.steps):
        comm.step(k)
    small_out[...] = comm.small_box[2 * comm.bits]
    swap.peers(pass_on)
    swap.peers(swap.wait_sent)

    def end(pack, carry):
        mix(pack).wait_send()
        passed(pack).wait()
        return carry

    lax.fori_loop(0, unit, end, 0)


def tail(h1, dx, dx_sib, big, small, unit, half, ident):
    vmem = pl.BlockSpec(memory_space=pltpu.VMEM)
    kept = [jax.ShapeDtypeStruct(dx_sib.shape, BF)] * 2
    out_shape = kept + [
        jax.ShapeDtypeStruct(big.shape, BF),
        jax.ShapeDtypeStruct(small.shape, F32),
    ]
    return pl.pallas_call(
        functools.partial(tail_kernel, unit, half),
        in_specs=[vmem] * 5,
        out_specs=[vmem] * len(out_shape),
        out_shape=out_shape,
        scratch_shapes=[
            pltpu.VMEM(dx_sib.shape, BF),
            pltpu.VMEM(dx_sib.shape, BF),
            *[pltpu.SemaphoreType.DMA((unit,))] * 6,
            *PackSum.scratch(*big.shape, small.shape, unit),
        ],
        compiler_params=pltpu.CompilerParams(
            vmem_limit_bytes=ROOM, collective_id=ident, has_side_effects=True
        ),
        cost_estimate=pl.CostEstimate(flops=0, bytes_accessed=200 * big.size, transcendentals=0),
        name="tail",
    )(h1, dx, dx_sib, big, small)


def norm_parts(field, norm_gain, norm_shift):
    center = field - jnp.mean(field, axis=-1, keepdims=True)
    inv_std = lax.rsqrt(jnp.mean(center * center, axis=-1, keepdims=True) + NORM_EPSILON)
    normed = center * inv_std
    return (normed * norm_gain + norm_shift, normed, inv_std)


def norm_back(incoming, normed, inv_std, norm_gain):
    scaled = incoming * norm_gain
    return inv_std * (
        scaled
        - jnp.mean(scaled, axis=-1, keepdims=True)
        - normed * jnp.mean(scaled * normed, axis=-1, keepdims=True)
    )


def over_rows(first_op, second_op):
    return dot(first_op, second_op, ((0,), (0,)))


def over_cols(first_op, second_op):
    return dot(first_op, second_op, ((1,), (1,)))


def local(
    activations, cotangent, lengths, dealing, qkv_weight, qv_bias, out_weight, out_bias,
    first_gain, first_shift, up_weight, up_bias, down_weight, down_bias, second_gain, second_shift,
):
    unit = lax.axis_size("dp")
    pack = lax.axis_index("dp")
    core = lax.axis_index("tensor")
    rows = activations.shape[0]
    width = activations.shape[2]
    half = rows // unit // 2

    def swap(x):
        return lax.ppermute(x, "tensor", [(0, 1), (1, 0)])

    core_arg = core.astype(jnp.int32).reshape(1)

    def send_back(field):
        got = lax.all_to_all(field.reshape(unit, half, width), "dp", 0, 0, tiled=True)
        return got.reshape(rows // 2, width)

    def undealt(own, sib):
        back = undeal(own, sib, lengths, dealing, core_arg, unit, half)
        return back.reshape(rows, 1, width)

    table, key_extra, query_extra = plan(lengths, dealing, rows, unit, half)
    x_own, x_sib, dealt_cotangent = deal(
        activations.reshape(rows, width), cotangent.reshape(rows, width), table, unit, half, 2
    )
    out_sib, up_sib, down_sib = swap(out_weight), swap(up_weight), swap(down_weight)
    up_bias_sib = swap(up_bias)

    qkv_planes = jnp.transpose(qkv_weight, (1, 0, 2))
    (
        queries, key_rows, values, context_own, context_sib, context_wide, log_total, cotangent_own,
    ) = attn_fwd(
        x_own, x_sib, qkv_planes, qv_bias, key_extra, query_extra, dealt_cotangent, unit, half, 3
    )
    attention = dot(context_own, out_weight) + dot(context_sib, out_sib)
    first_out, first_normed, first_inv = norm_parts(
        x_own.astype(F32) + attention + out_bias, first_gain, first_shift
    )
    first_low = first_out.astype(BF)

    def feed(up, bias):
        upward = dot(first_low, up) + bias
        cumulative = 0.5 * (1.0 + lax.erf(upward * math.sqrt(0.5)))
        density = jnp.exp(-0.5 * upward * upward) * (1.0 / math.sqrt(2.0 * math.pi))
        return (upward * cumulative).astype(BF), cumulative + upward * density

    active_own, slope_own = feed(up_weight, up_bias)
    active_sib, slope_sib = feed(up_sib, up_bias_sib)
    downward = dot(active_own, down_weight) + dot(active_sib, down_sib)
    second_out, second_normed, second_inv = norm_parts(
        first_out + downward + down_bias, second_gain, second_shift
    )
    got_output = send_back(second_out.astype(BF))
    outer = cotangent_own.astype(F32)
    grad_second_gain = jnp.sum(outer * second_normed, axis=0)
    grad_second_shift = jnp.sum(outer, axis=0)
    grad_h2 = norm_back(outer, second_normed, second_inv, second_gain)
    grad_down_bias = jnp.sum(grad_h2, axis=0)
    grad_branch = grad_h2.astype(BF)
    shard = down_weight.shape[0]
    granule = row_unit(unit)

    def chip_sum(own_part, sib_part):
        return (own_part + swap(sib_part.astype(BF)).astype(F32)).astype(BF)

    def stacked(parts, rows_of):
        size = sum(part.shape[0] for part in parts)
        pad = -size % rows_of
        if pad:
            parts = parts + [jnp.zeros((pad, parts[0].shape[1]), parts[0].dtype)]
        return jnp.concatenate(parts, axis=0)

    part_own = over_rows(active_own, grad_branch)
    part_sib = over_rows(active_sib, grad_branch).astype(BF)
    grad_branch, part_own, part_sib = lax.optimization_barrier((grad_branch, part_own, part_sib))
    wide_down = stacked([chip_sum(part_own, part_sib)], granule)
    came = []
    for (start, count), order in zip(
        cut_rows(wide_down.shape[0], unit), bit_orders(unit.bit_length() - 1)
    ):
        step = 2 ** order[0]
        away = lax.dynamic_slice_in_dim(
            wide_down, start + (1 - pack // step % 2) * (count // 2), count // 2, 0
        )
        came.append(lax.ppermute(away, "dp", [(i, i ^ step) for i in range(unit)]))
    grad_up_own = (over_cols(grad_branch, down_weight) * slope_own).astype(BF)
    grad_up_sib = (over_cols(grad_branch, down_sib) * slope_sib).astype(BF)
    grad_y1 = grad_h2 + over_cols(grad_up_own, up_weight) + over_cols(grad_up_sib, up_sib)
    grad_first_gain = jnp.sum(grad_y1 * first_normed, axis=0)
    grad_first_shift = jnp.sum(grad_y1, axis=0)
    grad_h1 = norm_back(grad_y1, first_normed, first_inv, first_gain)
    grad_out_bias = jnp.sum(grad_h1, axis=0)
    grad_attn = grad_h1.astype(BF)
    got_output, grad_attn = lax.optimization_barrier((got_output, grad_attn))
    grad_context = jnp.concatenate(
        [
            over_cols(grad_attn, out_weight).astype(BF),
            swap(over_cols(grad_attn, out_sib).astype(BF)),
        ],
        axis=0,
    )

    up_part = chip_sum(over_rows(first_low, grad_up_own), over_rows(first_low, grad_up_sib))
    out_part = chip_sum(over_rows(context_own, grad_attn), over_rows(context_sib, grad_attn))
    up_bias_own = jnp.sum(grad_up_own.astype(F32), axis=0)
    up_bias_part = up_bias_own + swap(jnp.sum(grad_up_sib.astype(F32), axis=0))
    vectors = jnp.stack(
        [
            grad_out_bias,
            grad_first_gain,
            grad_first_shift,
            grad_down_bias,
            grad_second_gain,
            grad_second_shift,
        ]
    )
    vectors = stacked([vectors + swap(vectors), up_bias_part.reshape(-1, width)], 8)
    wide_up = stacked(
        [up_part[:, first : first + width] for first in range(0, shard, width)] + [out_part], granule
    )
    input_part, input_sib, qkv_part, qv_part, vectors, sum_down, sum_up = attn_bwd(
        queries, key_rows, values, grad_context, context_wide, log_total, key_extra, query_extra,
        x_own, x_sib, qkv_planes, wide_down, wide_up, vectors, came, unit, 0,
    )
    inputs_own, inputs_sib, summed, qv_sum = tail(
        grad_h1, input_part, input_sib, stacked([qkv_part], granule), qv_part, unit, half, 1
    )
    grad_qkv_weight = jnp.stack(
        [summed[first : first + width] for first in range(0, 3 * width, width)], axis=1
    ).astype(F32)
    grad_qv_bias = qv_sum[:2]
    grad_down_weight = sum_down[:shard].astype(F32)
    grad_up_weight = jnp.concatenate(
        [sum_up[first : first + width] for first in range(0, shard, width)], axis=1
    ).astype(F32)
    grad_out_weight = sum_up[shard : shard + out_part.shape[0]].astype(F32)
    (
        grad_out_bias,
        grad_first_gain,
        grad_first_shift,
        grad_down_bias,
        grad_second_gain,
        grad_second_shift,
    ) = vectors[:6]
    grad_up_bias = vectors[6 : 6 + shard // width].reshape(-1)

    output = undealt(got_output, swap(got_output))
    input_grad = undealt(inputs_own, inputs_sib)
    return (
        output,
        input_grad,
        grad_qkv_weight,
        grad_qv_bias,
        grad_out_weight,
        grad_out_bias,
        grad_first_gain,
        grad_first_shift,
        grad_up_weight,
        grad_up_bias,
        grad_down_weight,
        grad_down_bias,
        grad_second_gain,
        grad_second_shift,
    )


def solution(mesh):
    placed = (
        P(None, "dp", None),
        P(None, "dp", None),
        P(),
        P(),
        P(None, None, "tensor"),
        P(None, "tensor"),
        P("tensor", None),
        P(),
        P(),
        P(),
        P(None, "tensor"),
        P("tensor"),
        P("tensor", None),
        P(),
        P(),
        P(),
    )
    return jax.shard_map(
        local,
        mesh=mesh,
        in_specs=placed,
        out_specs=(
            P(None, "dp", None),
            P(None, "dp", None),
            P(None, None, "tensor"),
            P(None, "tensor"),
            P("tensor", None),
            P(),
            P(),
            P(),
            P(None, "tensor"),
            P("tensor"),
            P("tensor", None),
            P(),
            P(),
            P(),
        ),
        check_vma=False,
    )
```

```python
import functools
import math

import jax
import jax.numpy as jnp
from jax import lax
from jax.experimental import pallas as pl
from jax.experimental.pallas import tpu as pltpu
from jax.sharding import PartitionSpec as P

HD = 64
BF = jnp.bfloat16
F32 = jnp.float32
MASKED_SCORE = -1e30
NORM_EPSILON = 1e-05
EXTRA = 16
ROOM = 56 * 2**20


def dot(a, b, dims=((1,), (0,))):
    return lax.dot_general(a, b, (dims, ((), ())), preferred_element_type=F32)


def unit_starts(lengths, starts, unit):
    def step(s, total):
        starts[s] = total
        return total + (lengths[s] + unit - 1) // unit

    lax.fori_loop(0, lengths.shape[0], step, jnp.int32(0))


def pack_windows(lengths, dealing, starts, unit, pack, first, rows, total):
    seq_a = dealing[2 * pack]
    seq_b = dealing[2 * pack + 1]
    units_a = (lengths[seq_a] + unit - 1) // unit
    shift_a = starts[seq_a]
    shift_b = starts[seq_b] - units_a
    bases = []
    for shift in (shift_a, shift_b):
        base = jnp.clip((shift + first) // 16 * 16, 0, total - rows - 16)
        bases.append(pl.multiple_of(base, 16))
    return units_a, shift_a, shift_b, bases


def plan_kernel(unit, half, lengths, dealing, table, kx_ref, qx_ref, starts):
    unit_starts(lengths, starts, unit)

    def one(pack, carry):
        units_a = (lengths[dealing[2 * pack]] + unit - 1) // unit
        table[0, pack] = units_a
        table[1, pack] = starts[dealing[2 * pack]]
        table[2, pack] = starts[dealing[2 * pack + 1]] - units_a
        return carry

    lax.fori_loop(0, unit, one, 0)
    pack = lax.axis_index("dp")
    core = lax.axis_index("tensor")
    len_a, len_b = lengths[dealing[2 * pack]], lengths[dealing[2 * pack + 1]]
    split = (len_a + unit - 1) // unit * unit
    rows = kx_ref.shape[0]

    def place(at):
        at_core = jnp.where(at < rows // 2, core, 1 - core)
        return (at_core * half + at % half) * unit + at % (rows // 2) // half

    row = place(lax.broadcasted_iota(jnp.int32, kx_ref.shape, 0))
    lane = lax.broadcasted_iota(jnp.int32, kx_ref.shape, 1)
    later = row >= split
    live = row < jnp.where(later, split + len_b, len_a)
    barred = (lane == jnp.where(later, 0, 1)) | ~live
    kx_ref[...] = jnp.where(
        lane < 2, jnp.where(barred, MASKED_SCORE, 0.0), jnp.where(lane < 5, -1.0, 0.0)
    ).astype(BF)
    col = place(lax.broadcasted_iota(jnp.int32, qx_ref.shape, 1))
    turn = lax.broadcasted_iota(jnp.int32, qx_ref.shape, 0)
    qx_ref[...] = jnp.where(turn == jnp.where(col >= split, 1, 0), 1.0, 0.0).astype(BF)


def plan(lengths, dealing, rows, unit, half):
    smem = pl.BlockSpec(memory_space=pltpu.SMEM)
    vmem = pl.BlockSpec(memory_space=pltpu.VMEM)
    return pl.pallas_call(
        functools.partial(plan_kernel, unit, half),
        in_specs=[smem, smem],
        out_specs=[smem, vmem, vmem],
        out_shape=[
            jax.ShapeDtypeStruct((3, unit), jnp.int32),
            jax.ShapeDtypeStruct((rows, 128), BF),
            jax.ShapeDtypeStruct((EXTRA, rows), BF),
        ],
        scratch_shapes=[pltpu.SMEM(lengths.shape, jnp.int32)],
        name="plan",
    )(lengths, dealing)


def greet(count, with_sibling=True):
    barrier = pltpu.get_barrier_semaphore()
    me = lax.axis_index("dp")

    def one(k, carry):
        pl.semaphore_signal(
            barrier, 1, device_id={"dp": (me + k) % count}, device_id_type=pl.DeviceIdType.MESH
        )
        return carry

    lax.fori_loop(1, count, one, 0)
    pl.semaphore_signal(
        barrier,
        1,
        device_id={"tensor": 1 - lax.axis_index("tensor")},
        device_id_type=pl.DeviceIdType.MESH,
    )
    pl.semaphore_wait(barrier, count)


class PackExchange:
    def __init__(self, count, block, source, target, send_sem, recv_sem):
        self.count, self.block = count, block
        self.source, self.target = source, target
        self.send_sem, self.recv_sem = send_sem, recv_sem
        self.me = lax.axis_index("dp")

    def rows(self, ref, i):
        return ref.at[pl.ds(pl.multiple_of(i * self.block, 16), self.block)]

    def copy(self, peer, landing, sem):
        return pltpu.make_async_remote_copy(
            src_ref=self.rows(self.source, peer),
            dst_ref=self.rows(self.target, landing),
            send_sem=self.send_sem.at[peer],
            recv_sem=self.recv_sem.at[sem],
            device_id={"dp": peer},
            device_id_type=pl.DeviceIdType.MESH,
        )

    def send(self, peer):
        self.copy(peer, self.me, self.me).start()

    def wait_from(self, peer):
        self.copy(peer, peer, peer).wait_recv()

    def wait_sent(self, peer):
        self.copy(peer, self.me, self.me).wait_send()

    def peers(self, body, first=0, last=None):
        def one(i, carry):
            far = self.count // 2 * (1 + (i + 1) % 2) - 1 - i // 2
            body(self.across(self.me, far, self.count))
            return carry

        lax.fori_loop(first, self.count - 1 if last is None else last, one, 0)

    @staticmethod
    def across(index, far, count):
        peer = 0
        for bit in range(count.bit_length() - 1):
            weight = 2**bit
            peer += (index // weight % 2 + far // weight % 2) % 2 * weight
        return peer

    def keep_own(self):
        self.rows(self.target, self.me)[...] = self.rows(self.source, self.me)[...]


def to_sibling(source, target, send_sem, recv_sem):
    return pltpu.make_async_remote_copy(
        src_ref=source,
        dst_ref=target,
        send_sem=send_sem,
        recv_sem=recv_sem,
        device_id={"tensor": 1 - lax.axis_index("tensor")},
        device_id_type=pl.DeviceIdType.MESH,
    )


def deal_kernel(
    unit, half, table, x_ref, g_hbm, own_ref, sib_ref, dealt_g,
    outbox, g_ref, load_sem, send_sem, recv_sem, pass_sem, take_sem,
):
    total = x_ref.shape[0]
    load = pltpu.make_async_copy(g_hbm, g_ref, load_sem)
    load.start()
    greet(unit)
    first = lax.axis_index("tensor") * half
    slot = first + lax.broadcasted_iota(jnp.int32, (half, total), 0)
    col = lax.broadcasted_iota(jnp.int32, (half, total), 1)
    swap = PackExchange(unit, half, outbox, own_ref, send_sem, recv_sem)
    team = 4

    def dealt(ref, packs, target):
        picks = []
        for i in range(team):
            pack = packs * team + i
            shift = jnp.where(slot < table[0, pack], table[1, pack], table[2, pack])
            picks.append(jnp.where(col == slot + shift, 1.0, 0.0).astype(BF))
        rows = dot(jnp.concatenate(picks, axis=0), ref[...]).astype(BF)
        at = pl.multiple_of(packs * team * half, 16)
        target[pl.ds(at, team * half)] = rows

    def passed(pack):
        return to_sibling(
            swap.rows(own_ref, pack), swap.rows(sib_ref, pack), pass_sem.at[pack], take_sem.at[pack]
        )

    def pass_on(pack):
        swap.wait_from(pack)
        passed(pack).start()

    home = swap.me // team

    def deal_out(i, carry):
        teams = [swap.across(home, far - i, unit // team) for far in far_teams]
        for packs in teams:
            dealt(x_ref, packs, outbox)

        def send(j, carry):
            for packs in teams:
                pack = packs * team + j

                @pl.when(pack != swap.me)
                def _(pack=pack):
                    swap.send(pack)

            return carry

        lax.fori_loop(0, team, send, 0)
        return carry

    far_teams = (unit // team - 1, unit // team // 2 - 1)
    lax.fori_loop(0, unit // team // 2, deal_out, 0)
    swap.keep_own()
    passed(swap.me).start()
    load.wait()

    def keep(packs, carry):
        dealt(g_ref, packs, dealt_g)
        return carry

    lax.fori_loop(0, unit // team, keep, 0)
    swap.peers(pass_on)
    swap.peers(swap.wait_sent)

    def end(pack, carry):
        passed(pack).wait_recv()
        passed(pack).wait_send()
        return carry

    lax.fori_loop(0, unit, end, 0)


def deal(x, g, table, unit, half, ident):
    total, width = x.shape
    smem = pl.BlockSpec(memory_space=pltpu.SMEM)
    vmem = pl.BlockSpec(memory_space=pltpu.VMEM)
    return pl.pallas_call(
        functools.partial(deal_kernel, unit, half),
        in_specs=[smem, vmem, pl.BlockSpec(memory_space=pl.ANY)],
        out_specs=[vmem, vmem, vmem],
        out_shape=[jax.ShapeDtypeStruct((total // 2, width), BF)] * 3,
        scratch_shapes=[
            pltpu.VMEM((total // 2, width), BF),
            pltpu.VMEM((total, width), BF),
            pltpu.SemaphoreType.DMA,
            *[pltpu.SemaphoreType.DMA((unit,))] * 4,
        ],
        compiler_params=pltpu.CompilerParams(
            vmem_limit_bytes=ROOM, collective_id=ident, has_side_effects=True
        ),
        cost_estimate=pl.CostEstimate(
            flops=8 * total * width * half, bytes_accessed=40 * total * width, transcendentals=0
        ),
        name="deal",
    )(table, x, g)


def undeal_kernel(unit, half, lengths, dealing, core, own_ref, sib_ref, o_ref, starts):
    total = o_ref.shape[0]
    unit_starts(lengths, starts, unit)
    wide = half + 16
    row = lax.broadcasted_iota(jnp.int32, (2 * wide, half), 0)
    col = lax.broadcasted_iota(jnp.int32, (2 * wide, half), 1)
    o_ref[...] = jnp.zeros_like(o_ref)

    def one(pack, carry):
        for part, ref in ((core[0], own_ref), (1 - core[0], sib_ref)):
            first = part * half
            units_a, shift_a, shift_b, (base_a, base_b) = pack_windows(
                lengths, dealing, starts, unit, pack, first, half, total
            )
            slot = first + col
            near = slot < units_a
            at = jnp.where(near, slot + (shift_a - base_a), slot + (shift_b - base_b + wide))
            pick = (row == at) & (near == (row < wide))
            rows = ref[pl.ds(pl.multiple_of(pack * half, 16), half), :]
            both = dot(pick.astype(F32).astype(BF), rows).astype(BF)
            o_ref[pl.ds(base_a, wide), :] += both[:wide]
            o_ref[pl.ds(base_b, wide), :] += both[wide:]
        return carry

    lax.fori_loop(0, total // (2 * half), one, 0, unroll=2)


def undeal(own, sib, lengths, dealing, core, unit, half):
    total, width = 2 * own.shape[0], own.shape[1]
    smem = pl.BlockSpec(memory_space=pltpu.SMEM)
    vmem = pl.BlockSpec(memory_space=pltpu.VMEM)
    return pl.pallas_call(
        functools.partial(undeal_kernel, unit, half),
        in_specs=[smem, smem, smem, vmem, vmem],
        out_specs=vmem,
        out_shape=jax.ShapeDtypeStruct((total, width), BF),
        scratch_shapes=[pltpu.SMEM(lengths.shape, jnp.int32)],
        compiler_params=pltpu.CompilerParams(vmem_limit_bytes=ROOM),
        cost_estimate=pl.CostEstimate(
            flops=8 * total * width * half, bytes_accessed=4 * total * width, transcendentals=0
        ),
        name="undeal",
    )(lengths, dealing, core, own, sib)


def fwd_kernel(
    ck, unit, half, x_own, x_sib, w_ref, b_ref, kx_ref, qx_ref, dealt_g,
    q_ref, k_ref, v_ref, c_ref, c_other_out, c32_ref, lse_ref, got_g_out,
    kext, vt, c_sib, c_other, got_g, send_sem, recv_sem, pass_sem, take_sem,
):
    n = k_ref.shape[0]
    pair = pl.program_id(0)
    swap = PackExchange(unit, half, dealt_g, got_g, send_sem, recv_sem)

    def passed(pair):
        cols = pl.ds(pl.multiple_of(pair * 128, 128), 128)
        return to_sibling(
            c_sib.at[:, cols], c_other.at[:, cols], pass_sem.at[pair], take_sem.at[pair]
        )

    @pl.when(pair == 0)
    def _():
        greet(unit)
        swap.peers(swap.send)
        swap.keep_own()

    w = jnp.concatenate([w_ref[0], w_ref[1], w_ref[2]], axis=1)
    bias = jnp.concatenate([b_ref[0:1], jnp.zeros((1, 128), F32), b_ref[1:2]], axis=1)
    for part, x_ref in enumerate((x_own, x_sib)):
        for first in range(0, n // 2, 512):
            made = (dot(x_ref[first : first + 512], w) + bias).astype(BF)
            at = slice(part * n // 2 + first, part * n // 2 + first + 512)
            for j, ref in enumerate((q_ref, k_ref, v_ref)):
                ref[at] = made[:, 128 * j : 128 * j + 128]
    kext[:, :128] = k_ref[...]
    kext[:, 128:] = kx_ref[...]
    v_t = v_ref[...].T
    ones = jnp.where(lax.broadcasted_iota(jnp.int32, (EXTRA, n), 0) == 0, 1.0, 0.0).astype(BF)
    for h in range(2):
        vt[h, :HD] = v_t[HD * h : HD * h + HD]
        vt[h, HD:] = ones
    q_t = (q_ref[...] * BF(HD**-0.5)).T
    zero = jnp.zeros((HD, n), BF)
    qx = qx_ref[...]
    q_ext = [
        jnp.concatenate([q_t[:HD], zero, qx], axis=0),
        jnp.concatenate([zero, q_t[HD:], qx], axis=0),
    ]
    tops, sums = [None, None], [None, None]
    for first in range(0, n, ck):
        keys = slice(first, first + ck)
        for h in range(2):
            s = dot(kext[keys, : 128 + EXTRA], q_ext[h])
            top = jnp.max(s, axis=0, keepdims=True)
            if first:
                top = jnp.maximum(tops[h], top)
            part = dot(vt[h, :, keys], jnp.exp(s - top).astype(BF))
            if first:
                part = part + sums[h] * jnp.exp(tops[h] - top)
            tops[h], sums[h] = top, part
    outs = []
    for h in range(2):
        total = sums[h][HD : HD + 1]
        outs.append(sums[h][:HD] / total)
        lse_ref[0, h : h + 1] = tops[h] + jnp.log(total)
    c = jnp.concatenate(outs, axis=0).T
    c32_ref[...] = c
    c_ref[...] = c[: n // 2].astype(BF)
    c_sib[:, pl.ds(pl.multiple_of(pair * 128, 128), 128)] = c[n // 2 :].astype(BF)
    passed(pair).start()

    @pl.when(pair == pl.num_programs(0) - 1)
    def _():
        swap.peers(swap.wait_from)
        swap.peers(swap.wait_sent)

        def end(pair, carry):
            passed(pair).wait_recv()
            passed(pair).wait_send()
            return carry

        lax.fori_loop(0, pl.num_programs(0), end, 0)
        c_other_out[...] = c_other[...]
        got_g_out[...] = got_g[...]


def attn_cost(n, width, products):
    return pl.CostEstimate(
        flops=products * 2 * 4 * n * n * width,
        bytes_accessed=16 * n * width,
        transcendentals=n * n * width // HD,
    )


def attn_fwd(x_own, x_sib, w, b, kx, qx, dealt_g, unit, half, ident, ck=512):
    n, model = 2 * x_own.shape[0], x_own.shape[1]
    width = w.shape[2]
    pairs = width // 128
    keys = pl.BlockSpec((n, 128), lambda p: (0, p))

    def whole(shape):
        return pl.BlockSpec(shape, lambda p: (0, 0), pipeline_mode=pl.Buffered(1))

    return pl.pallas_call(
        functools.partial(fwd_kernel, ck, unit, half),
        grid=(pairs,),
        in_specs=[
            whole(x_own.shape),
            whole(x_sib.shape),
            pl.BlockSpec((3, model, 128), lambda p: (0, 0, p)),
            pl.BlockSpec((2, 128), lambda p: (0, p)),
            whole(kx.shape),
            whole(qx.shape),
            whole(dealt_g.shape),
        ],
        out_specs=[
            keys,
            keys,
            keys,
            pl.BlockSpec((n // 2, 128), lambda p: (0, p)),
            whole((n // 2, width)),
            keys,
            pl.BlockSpec((1, 2, n), lambda p: (p, 0, 0)),
            whole(dealt_g.shape),
        ],
        out_shape=[jax.ShapeDtypeStruct((n, width), BF)] * 3
        + [jax.ShapeDtypeStruct((n // 2, width), BF)] * 2
        + [
            jax.ShapeDtypeStruct((n, width), F32),
            jax.ShapeDtypeStruct((pairs, 2, n), F32),
            jax.ShapeDtypeStruct(dealt_g.shape, BF),
        ],
        scratch_shapes=[
            pltpu.VMEM((n, 256), BF),
            pltpu.VMEM((2, HD + EXTRA, n), BF),
            pltpu.VMEM((n // 2, width), BF),
            pltpu.VMEM((n // 2, width), BF),
            pltpu.VMEM(dealt_g.shape, BF),
            *[pltpu.SemaphoreType.DMA((unit,))] * 2,
            *[pltpu.SemaphoreType.DMA((pairs,))] * 2,
        ],
        compiler_params=pltpu.CompilerParams(
            vmem_limit_bytes=ROOM, collective_id=ident, has_side_effects=True
        ),
        cost_estimate=attn_cost(n, width, 2),
        name="attn_fwd",
    )(x_own, x_sib, w, b, kx, qx, dealt_g)


def split3(x):
    high = x.astype(BF)
    rest = x - high.astype(F32)
    middle = rest.astype(BF)
    return high, middle, (rest - middle.astype(F32)).astype(BF)


def bit_orders(bits):
    first = list(range(bits))
    second = [1, 2, 0] + list(range(3, bits))
    third = [2, 0, 1] + list(range(3, bits))
    return first, second, third


def row_unit(devices):
    return 8 * devices


def cut_rows(rows, devices):
    unit = row_unit(devices)
    units = rows // unit
    counts = [(units + 2) // 3, (units + 1) // 3, units // 3]
    starts = [0, counts[0], counts[0] + counts[1]]
    return [(s * unit, c * unit) for s, c in zip(starts, counts) if c]


def greet_partners(bits):
    me = lax.axis_index("dp")
    barrier = pltpu.get_barrier_semaphore()
    for bit in range(bits):
        pl.semaphore_signal(
            barrier,
            inc=1,
            device_id={"dp": me + (1 - 2 * (me // 2**bit % 2)) * 2**bit},
            device_id_type=pl.DeviceIdType.MESH,
        )
    pl.semaphore_wait(barrier, bits)


class PackSum:
    def __init__(self, devices, big, small, out, came, acc, inbox, small_box, send_sem, recv_sem):
        self.came = came
        self.bits = devices.bit_length() - 1
        self.me = lax.axis_index("dp")
        self.big, self.small, self.acc, self.inbox, self.out = big, small, acc, inbox, out
        self.small_box = small_box
        self.send_sem, self.recv_sem = send_sem, recv_sem
        self.parts = [
            (start, count, order)
            for (start, count), order in zip(cut_rows(big.shape[0], devices), bit_orders(self.bits))
        ]
        self.steps = 2 * self.bits

    def slots(self, first, slot_us, last):
        size = 4e-3 * self.big.shape[0] * self.big.shape[1]
        sizes = [size / 2 ** (level + 1) / 3 for level in range(self.bits - 1)]
        sizes = sizes + [size / 2 ** (self.bits - 2)] + sizes[::-1]
        at, out = 0.0, []
        for step in range(self.steps):
            out.append(min(last, first + math.ceil(at / slot_us)))
            if step < len(sizes) and not (step == 0 and self.came):
                at += 4.5 + sizes[step] / 80
        return out

    @staticmethod
    def scratch(rows, cols, small_shape, devices):
        bits = devices.bit_length() - 1
        return [
            pltpu.VMEM((rows // 2, cols), BF),
            pltpu.VMEM((rows, cols), BF),
            pltpu.VMEM((2 * bits + 1,) + small_shape, F32),
            pltpu.SemaphoreType.DMA((4, 2 * bits)),
            pltpu.SemaphoreType.DMA((4, 2 * bits)),
        ]

    def side(self, bit):
        return (self.me // 2**bit) % 2

    def partner(self, bit):
        return self.me + (1 - 2 * self.side(bit)) * 2**bit

    def region(self, part, level):
        start, count, order = self.parts[part]
        for done in range(level):
            start = start + self.side(order[done]) * (count // 2 ** (done + 1))
        return start, count // 2**level

    def halved(self, part, start):
        return self.parts[part][0] // 2 + start - self.region(part, 1)[0]

    def rows(self, ref, start, count):
        return ref.at[pl.ds(pl.multiple_of(start, 16), count)]

    def slot(self, part, level):
        start, count, _ = self.parts[part]
        return start + count - count // 2**level

    def sending(self, part, level):
        start, count = self.region(part, level)
        bit = self.parts[part][2][level]
        if level < self.bits - 1:
            count = count // 2
            start = start + (1 - self.side(bit)) * count
        return pltpu.make_async_remote_copy(
            src_ref=self.rows(self.acc, self.halved(part, start), count)
            if level
            else self.rows(self.big, start, count),
            dst_ref=self.inbox.at[pl.ds(self.slot(part, level), count)],
            send_sem=self.send_sem.at[part, level],
            recv_sem=self.recv_sem.at[part, level],
            device_id={"dp": self.partner(bit)},
            device_id_type=pl.DeviceIdType.MESH,
        )

    def doubling(self, part, level):
        mine = self.rows(self.out, *self.region(part, level + 1))
        return pltpu.make_async_remote_copy(
            src_ref=mine,
            dst_ref=mine,
            send_sem=self.send_sem.at[part, self.bits + level],
            recv_sem=self.recv_sem.at[part, self.bits + level],
            device_id={"dp": self.partner(self.parts[part][2][level])},
            device_id_type=pl.DeviceIdType.MESH,
        )

    def exchange(self, level):
        return pltpu.make_async_remote_copy(
            src_ref=self.small if level == 0 else self.small_box.at[self.bits + level],
            dst_ref=self.small_box.at[level],
            send_sem=self.send_sem.at[3, level],
            recv_sem=self.recv_sem.at[3, level],
            device_id={"dp": self.partner(level)},
            device_id_type=pl.DeviceIdType.MESH,
        )

    def add(self, part, level):
        last = level == self.bits - 1
        kept, count = self.region(part, level if last else level + 1)
        source, first = (self.acc, self.halved(part, kept)) if level else (self.big, kept)
        if last:
            target, goal = self.out, kept
        else:
            target, goal = self.acc, self.halved(part, kept)
        slot, box = self.slot(part, level), self.inbox
        if self.came and level == 0:
            slot, box = 0, self.came[part]
        tile = math.gcd(count, 64)

        def one(i, carry):
            def at(start):
                return pl.ds(pl.multiple_of(start + i * tile, 16), tile)

            total = source[at(first), :].astype(F32) + box[at(slot), :].astype(F32)
            target[at(goal), :] = total.astype(BF)
            return carry

        lax.fori_loop(0, count // tile, one, 0)

    def step(self, k):
        bits = self.bits
        for part in range(len(self.parts)):
            if 0 < k <= bits:
                if not (self.came and k == 1):
                    self.sending(part, k - 1).wait_recv()
                self.add(part, k - 1)
            elif k > bits:
                self.doubling(part, 2 * bits - 1 - k).wait_recv()
            if k < bits:
                self.sending(part, k).start()
            elif k < self.steps - 1:
                self.doubling(part, 2 * bits - 2 - k).start()
        if self.small is not None:
            if 0 < k <= bits:
                self.exchange(k - 1).wait_recv()
                held = self.small[...] if k == 1 else self.small_box[bits + k - 1]
                self.small_box[bits + k] = held + self.small_box[k - 1]
            if k < bits:
                self.exchange(k).start()
        if k == self.steps - 1:
            for part in range(len(self.parts)):
                for level in range(1 if self.came else 0, bits):
                    self.sending(part, level).wait_send()
                for level in range(bits - 1):
                    self.doubling(part, level).wait_send()
            if self.small is not None:
                for level in range(bits):
                    self.exchange(level).wait_send()


SLOT_US = 3.6


def bwd_kernel(
    ck, devices, turns, q_ref, k_ref, v_ref, g_ref, c32_ref, lse_ref, kx_ref, qx_ref,
    x_own, x_sib, w_ref, big_a, big_b, small, *refs,
):
    i = pl.program_id(1)
    n = k_ref.shape[0]
    bq = q_ref.shape[0]
    count = len(cut_rows(big_a.shape[0], devices))
    came, refs = refs[:count], refs[count:]
    dx_ref, dx_sib_ref, dw_ref, db_ref, small_out, out_a, out_b = refs[:7]
    kext, vext, kt, x_t, dq_acc, dk_acc, dv_acc, dx_sib, sum_a, sum_b, *comm_refs = refs[7:]
    comm_a = PackSum(devices, big_a, None, sum_a, came, *comm_refs[:5])
    comm_b = PackSum(devices, big_b, small, sum_b, None, *comm_refs[5:])
    turn = pl.program_id(0) * pl.num_programs(1) + i
    per_turn = n // ck
    slots = turns * per_turn
    slots_a = comm_a.slots(0, SLOT_US, slots)
    slots_b = comm_b.slots(0, SLOT_US, slots)

    def comm_at(which):
        for comm, at in ((comm_a, slots_a), (comm_b, slots_b)):
            for step, slot in enumerate(at):
                if step == 0 and comm.came:
                    continue
                if slot < slots and slot % per_turn == which:

                    @pl.when(turn == slot // per_turn)
                    def _(comm=comm, step=step):
                        comm.step(step)

                elif slot == slots and which is None:
                    comm.step(step)

    @pl.when(turn == 0)
    def _():
        greet_partners(comm_a.bits)

    @pl.when(i == 0)
    def _():
        kext[:, :128] = k_ref[...]
        kext[:, 128:] = kx_ref[...]
        vext[:, :128] = v_ref[...]
        lane = lax.broadcasted_iota(jnp.int32, (n, 128), 1)
        vext[:, 128:] = jnp.where((lane >= 2) & (lane < 5), -1.0, 0.0).astype(BF)
        kt[...] = k_ref[...].T
        dk_acc[...] = jnp.zeros_like(dk_acc)
        dv_acc[...] = jnp.zeros_like(dv_acc)

    q = q_ref[...] * BF(HD**-0.5)
    g = g_ref[...]
    q_t, g_t = q.T, g.T
    prod_t = (g.astype(F32) * c32_ref[...]).T
    zero = jnp.zeros((HD, bq), BF)
    lane = lax.broadcasted_iota(jnp.int32, (bq, 128), 1)
    row = lax.broadcasted_iota(jnp.int32, (EXTRA, bq), 0)
    qx = qx_ref[...].astype(F32)

    def with_rows(base, parts):
        for j, part in enumerate(parts):
            base = jnp.where(row == 2 + j, part.astype(F32), base)
        return base.astype(BF)

    q_ext, g_ext, q_own, g_own, dq_t = [], [], [], [], []
    for h in range(2):
        mine = slice(HD * h, HD * h + HD)
        delta = jnp.sum(prod_t[mine], axis=0, keepdims=True)
        q_rows = with_rows(qx, split3(lse_ref[0, h : h + 1]))
        g_rows = with_rows(jnp.zeros((EXTRA, bq), F32), split3(delta))
        for out, turned, extra in ((q_ext, q_t, q_rows), (g_ext, g_t, g_rows)):
            both = [turned[mine], zero] if h == 0 else [zero, turned[mine]]
            out.append(jnp.concatenate(both + [extra], axis=0))
        ours = (lane < HD) if h == 0 else (lane >= HD)
        q_own.append(jnp.where(ours, q, BF(0)))
        g_own.append(jnp.where(ours, g, BF(0)))
        dq_t.append(jnp.zeros((HD, bq), F32))
    for first in range(0, n, ck):
        comm_at(first // ck)
        keys = slice(first, first + ck)
        dv = jnp.zeros((ck, 128), F32)
        dk = jnp.zeros((ck, 128), F32)
        for h in range(2):
            p = jnp.exp(dot(kext[keys, : 128 + EXTRA], q_ext[h]))
            ds = (p * dot(vext[keys, : 128 + EXTRA], g_ext[h])).astype(BF)
            dv = dv + dot(p.astype(BF), g_own[h])
            dk = dk + dot(ds, q_own[h])
            dq_t[h] = dq_t[h] + dot(kt[HD * h : HD * h + HD, keys], ds)
        dv_acc[keys] += dv
        dk_acc[keys] += dk
    dq = jnp.concatenate(dq_t, axis=0).T * HD**-0.5
    dq_acc[pl.ds(pl.multiple_of(i * bq, bq), bq)] = dq.astype(BF)

    @pl.when(turn == 0)
    def _():
        x_t[:, : n // 2] = x_own[...].T
        x_t[:, n // 2 :] = x_sib[...].T
        dx_ref[...] = jnp.zeros_like(dx_ref)
        dx_sib[...] = jnp.zeros_like(dx_sib)

    @pl.when(i == pl.num_programs(1) - 1)
    def _():
        width = x_own.shape[1]
        grads = [dq_acc[...], dk_acc[...].astype(BF), dv_acc[...].astype(BF)]
        joined = jnp.concatenate(grads, axis=1)
        made = dot(x_t[...], joined).astype(BF)
        for j in range(3):
            dw_ref[j * width : (j + 1) * width] = made[:, 128 * j : 128 * j + 128]
        bias = [jnp.sum(grad.astype(F32), axis=0, keepdims=True) for grad in grads[::2]]
        db_ref[...] = jnp.concatenate(bias + [jnp.zeros((6, 128), F32)], axis=0)
        tile = 512
        planes = jnp.concatenate([w_ref[j] for j in range(3)], axis=1)
        for first in range(0, n, tile):
            to_x = dot(joined[first : first + tile], planes, ((1,), (1,)))
            target, goal = (dx_ref, first) if first < n // 2 else (dx_sib, first - n // 2)
            target[goal : goal + tile] += to_x

    @pl.when(turn == turns - 1)
    def _():
        comm_at(None)
        dx_sib_ref[...] = dx_sib[...].astype(BF)
        out_a[...] = sum_a[...]
        out_b[...] = sum_b[...]
        small_out[...] = comm_b.small_box[2 * comm_b.bits]


def attn_bwd(q, k, v, g, c32, lse, kx, qx, x_own, x_sib, w, big_a, big_b, small, came, devices, ident, bq=1024, ck=512):
    n, width = q.shape
    pairs = width // 128
    model = x_own.shape[1]
    rows = pl.BlockSpec((bq, 128), lambda p, i: (i, p))
    keys = pl.BlockSpec((n, 128), lambda p, i: (0, p))
    def whole(shape):
        return pl.BlockSpec(shape, lambda p, i: (0, 0), pipeline_mode=pl.Buffered(1))

    return pl.pallas_call(
        functools.partial(bwd_kernel, ck, devices, pairs * (n // bq)),
        grid=(pairs, n // bq),
        in_specs=[
            rows,
            keys,
            keys,
            rows,
            rows,
            pl.BlockSpec((1, 2, bq), lambda p, i: (p, 0, i)),
            pl.BlockSpec((n, 128), lambda p, i: (0, 0)),
            pl.BlockSpec((EXTRA, bq), lambda p, i: (0, i)),
            whole(x_own.shape),
            whole(x_sib.shape),
            pl.BlockSpec((3, model, 128), lambda p, i: (0, 0, p)),
            whole(big_a.shape),
            whole(big_b.shape),
            whole(small.shape),
            *[whole(box.shape) for box in came],
        ],
        out_specs=[
            whole((n // 2, model)),
            whole((n // 2, model)),
            pl.BlockSpec((3 * model, 128), lambda p, i: (0, p)),
            pl.BlockSpec((8, 128), lambda p, i: (0, p)),
            whole(small.shape),
            whole(big_a.shape),
            whole(big_b.shape),
        ],
        out_shape=[
            jax.ShapeDtypeStruct((n // 2, model), F32),
            jax.ShapeDtypeStruct((n // 2, model), BF),
            jax.ShapeDtypeStruct((3 * model, width), BF),
            jax.ShapeDtypeStruct((8, width), F32),
            jax.ShapeDtypeStruct(small.shape, F32),
            jax.ShapeDtypeStruct(big_a.shape, BF),
            jax.ShapeDtypeStruct(big_b.shape, BF),
        ],
        scratch_shapes=[
            pltpu.VMEM((n, 256), BF),
            pltpu.VMEM((n, 256), BF),
            pltpu.VMEM((128, n), BF),
            pltpu.VMEM((model, n), BF),
            pltpu.VMEM((n, 128), BF),
            pltpu.VMEM((n, 128), F32),
            pltpu.VMEM((n, 128), F32),
            pltpu.VMEM((n // 2, model), F32),
            pltpu.VMEM(big_a.shape, BF),
            pltpu.VMEM(big_b.shape, BF),
            *PackSum.scratch(*big_a.shape, (8, 128), devices),
            *PackSum.scratch(*big_b.shape, small.shape, devices),
        ],
        compiler_params=pltpu.CompilerParams(
            vmem_limit_bytes=60 * 2**20, collective_id=ident, has_side_effects=True
        ),
        cost_estimate=attn_cost(n, width, 5),
        name="attn_bwd",
    )(q, k, v, g, c32, lse, kx, qx, x_own, x_sib, w, big_a, big_b, small, *came)


def norm_parts(field, gain, shift):
    center = field - jnp.mean(field, axis=-1, keepdims=True)
    inv_std = lax.rsqrt(jnp.mean(center * center, axis=-1, keepdims=True) + NORM_EPSILON)
    normed = center * inv_std
    return normed * gain + shift, normed, inv_std


def norm_back(incoming, normed, inv_std, gain):
    scaled = incoming * gain
    return inv_std * (
        scaled
        - jnp.mean(scaled, axis=-1, keepdims=True)
        - normed * jnp.mean(scaled * normed, axis=-1, keepdims=True)
    )


FF_ROWS = 256


def ff_kernel(
    unit, half, x_ref, c_own, c_sib, g_ref, out_own, out_sib, up_own, up_sib, down_own, down_sib,
    vec_ref, bias_own, bias_sib,
    low_ref, act_own, act_sib, branch_ref, du_own, du_sib, da_ref, h1_ref, dc_own, dc_sib,
    vec_out, bias_out, got_own_out, got_sib_out,
    z, got, got_sib, slope, send_sem, recv_sem, pass_sem, take_sem,
):
    i = pl.program_id(0)
    blocks = pl.num_programs(0)
    swap = PackExchange(unit, half, z, got, send_sem, recv_sem)
    team = FF_ROWS // half
    block = ff_block(i, unit, half, z.shape[0] // FF_ROWS)

    def passed(pack):
        return to_sibling(
            swap.rows(got, pack), swap.rows(got_sib, pack), pass_sem.at[pack], take_sem.at[pack]
        )

    @pl.when(i == 0)
    def _():
        greet(unit)
        vec_out[...] = jnp.zeros_like(vec_out)
        bias_out[...] = jnp.zeros_like(bias_out)

    out_bias, first_gain, first_shift, down_bias, second_gain, second_shift = (
        vec_ref[j : j + 1] for j in range(6)
    )
    attention = dot(c_own[...], out_own[...]) + dot(c_sib[...], out_sib[...])
    first, first_normed, first_inv = norm_parts(
        x_ref[...].astype(F32) + attention + out_bias, first_gain, first_shift
    )
    low = first.astype(BF)
    low_ref[...] = low
    shard = up_own.shape[1]
    wide = 512
    sides = (
        (up_own, down_own, bias_own, act_own, du_own),
        (up_sib, down_sib, bias_sib, act_sib, du_sib),
    )
    down = jnp.zeros(first.shape, F32)
    for side, (up, back, bias, act_ref, _) in enumerate(sides):
        for start in range(0, shard, wide):
            cols = slice(start, start + wide)
            upward = dot(low, up[:, cols]) + bias[:, cols]
            cumulative = 0.5 + 0.5 * lax.erf(upward * math.sqrt(0.5))
            density = jnp.exp(-0.5 * upward * upward) * (1.0 / math.sqrt(2.0 * math.pi))
            act = (upward * cumulative).astype(BF)
            act_ref[:, cols] = act
            slope[:, side * shard + start : side * shard + start + wide] = (
                cumulative + upward * density
            )
            down = down + dot(act, back[cols])
    second, second_normed, second_inv = norm_parts(
        first + down + down_bias, second_gain, second_shift
    )
    z[pl.ds(pl.multiple_of(block * FF_ROWS, 16), FF_ROWS)] = second.astype(BF)

    def send(j, carry):
        pack = block * team + j

        @pl.when(pack != swap.me)
        def _():
            swap.send(pack)

        return carry

    lax.fori_loop(0, team, send, 0)
    outer = g_ref[...].astype(F32)
    grad_h2 = norm_back(outer, second_normed, second_inv, second_gain)
    branch = grad_h2.astype(BF)
    branch_ref[...] = branch
    grad_y1 = grad_h2
    for side, (up, back, _, _, du_ref) in enumerate(sides):
        for start in range(0, shard, wide):
            cols = slice(start, start + wide)
            at = slice(side * shard + start, side * shard + start + wide)
            du = (dot(branch, back[cols], ((1,), (1,))) * slope[:, at]).astype(BF)
            du_ref[:, cols] = du
            bias_out[side : side + 1, cols] += jnp.sum(du.astype(F32), axis=0, keepdims=True)
            grad_y1 = grad_y1 + dot(du, up[:, cols], ((1,), (1,)))
    grad_h1 = norm_back(grad_y1, first_normed, first_inv, first_gain)
    h1_ref[...] = grad_h1
    da = grad_h1.astype(BF)
    da_ref[...] = da
    dc_own[...] = dot(da, out_own[...], ((1,), (1,))).astype(BF)
    dc_sib[...] = dot(da, out_sib[...], ((1,), (1,))).astype(BF)
    terms = (
        grad_h1, grad_y1 * first_normed, grad_y1, grad_h2, outer * second_normed, outer,
    )
    for j, term in enumerate(terms):
        vec_out[j : j + 1] += jnp.sum(term, axis=0, keepdims=True)

    @pl.when(i == blocks - 1)
    def _():
        swap.keep_own()
        passed(swap.me).start()

        def pass_on(pack):
            swap.wait_from(pack)
            passed(pack).start()

        swap.peers(pass_on)
        swap.peers(swap.wait_sent)

        def end(pack, carry):
            passed(pack).wait()
            return carry

        lax.fori_loop(0, unit, end, 0)
        got_own_out[...] = got[...]
        got_sib_out[...] = got_sib[...]


def ff_block(i, unit, half, blocks):
    home = lax.axis_index("dp") // (FF_ROWS // half)
    return PackExchange.across(home, blocks - 1 - i, blocks)


def feed_forward(x, c_own, c_sib, g, weights, vectors, bias_own, bias_sib, unit, half, ident):
    n, model = x.shape
    shard = bias_own.shape[1]
    width = c_own.shape[1]
    blocks = n // FF_ROWS

    def rows(cols):
        return pl.BlockSpec((FF_ROWS, cols), lambda i: (ff_block(i, unit, half, blocks), 0))

    def whole(shape):
        return pl.BlockSpec(shape, lambda i: (0, 0), pipeline_mode=pl.Buffered(1))

    shapes = [
        (model, BF), (shard, BF), (shard, BF), (model, BF), (shard, BF), (shard, BF), (model, BF),
        (model, F32), (width, BF), (width, BF),
    ]
    kept = [(vectors.shape, F32), ((8, shard), F32), ((n, model), BF), ((n, model), BF)]
    return pl.pallas_call(
        functools.partial(ff_kernel, unit, half),
        grid=(blocks,),
        in_specs=[rows(model), rows(width), rows(width), rows(model)]
        + [whole(w.shape) for w in weights]
        + [whole(vectors.shape), whole(bias_own.shape), whole(bias_sib.shape)],
        out_specs=[rows(cols) for cols, _ in shapes] + [whole(shape) for shape, _ in kept],
        out_shape=[jax.ShapeDtypeStruct((n, cols), dtype) for cols, dtype in shapes]
        + [jax.ShapeDtypeStruct(shape, dtype) for shape, dtype in kept],
        scratch_shapes=[
            pltpu.VMEM((n, model), BF),
            pltpu.VMEM((n, model), BF),
            pltpu.VMEM((n, model), BF),
            pltpu.VMEM((FF_ROWS, 2 * shard), F32),
            *[pltpu.SemaphoreType.DMA((unit,))] * 4,
        ],
        compiler_params=pltpu.CompilerParams(
            vmem_limit_bytes=ROOM, collective_id=ident, has_side_effects=True
        ),
        cost_estimate=pl.CostEstimate(
            flops=8 * n * model * (width + shard) * 2,
            bytes_accessed=40 * n * model,
            transcendentals=4 * n * shard,
        ),
        name="feed_forward",
    )(x, c_own, c_sib, g, *weights, vectors, bias_own, bias_sib)


def tail_kernel(
    unit, half, h1_ref, dx_ref, dx_sib, big, small, own_ref, sib_ref, big_out, small_out,
    outbox, dx_came, mix_sem, mixed_sem, send_sem, recv_sem, pass_sem, take_sem, *comm_refs,
):
    comm = PackSum(unit, big, small, big_out, None, *comm_refs)
    swap = PackExchange(unit, half, outbox, own_ref, send_sem, recv_sem)

    def mix(pack):
        return to_sibling(
            swap.rows(dx_sib, pack),
            swap.rows(dx_came, pack),
            mix_sem.at[pack],
            mixed_sem.at[pack],
        )

    def passed(pack):
        return to_sibling(
            swap.rows(own_ref, pack), swap.rows(sib_ref, pack), pass_sem.at[pack], take_sem.at[pack]
        )

    def add_up(pack):
        mix(pack).wait_recv()
        at = swap.rows(dx_came, pack)[...].astype(F32)
        total = swap.rows(h1_ref, pack)[...] + swap.rows(dx_ref, pack)[...] + at
        swap.rows(outbox, pack)[...] = total.astype(BF)

    def add_and_send(pack):
        add_up(pack)
        swap.send(pack)

    def pass_on(pack):
        swap.wait_from(pack)
        passed(pack).start()

    greet(unit)
    swap.peers(lambda pack: mix(pack).start())
    mix(swap.me).start()
    comm.step(0)
    share = -(-(unit - 1) // 5)
    for k in range(1, 6):
        swap.peers(add_and_send, (k - 1) * share, min(k * share, unit - 1))
        comm.step(k)
    add_up(swap.me)
    swap.keep_own()
    passed(swap.me).start()
    for k in range(6, comm.steps):
        comm.step(k)
    small_out[...] = comm.small_box[2 * comm.bits]
    swap.peers(pass_on)
    swap.peers(swap.wait_sent)

    def end(pack, carry):
        mix(pack).wait_send()
        passed(pack).wait()
        return carry

    lax.fori_loop(0, unit, end, 0)


def tail(h1, dx, dx_sib, big, small, unit, half, ident):
    vmem = pl.BlockSpec(memory_space=pltpu.VMEM)
    kept = [jax.ShapeDtypeStruct(dx_sib.shape, BF)] * 2
    out_shape = kept + [
        jax.ShapeDtypeStruct(big.shape, BF),
        jax.ShapeDtypeStruct(small.shape, F32),
    ]
    return pl.pallas_call(
        functools.partial(tail_kernel, unit, half),
        in_specs=[vmem] * 5,
        out_specs=[vmem] * len(out_shape),
        out_shape=out_shape,
        scratch_shapes=[
            pltpu.VMEM(dx_sib.shape, BF),
            pltpu.VMEM(dx_sib.shape, BF),
            *[pltpu.SemaphoreType.DMA((unit,))] * 6,
            *PackSum.scratch(*big.shape, small.shape, unit),
        ],
        compiler_params=pltpu.CompilerParams(
            vmem_limit_bytes=ROOM, collective_id=ident, has_side_effects=True
        ),
        cost_estimate=pl.CostEstimate(flops=0, bytes_accessed=200 * big.size, transcendentals=0),
        name="tail",
    )(h1, dx, dx_sib, big, small)


def over_rows(first_op, second_op):
    return dot(first_op, second_op, ((0,), (0,)))


def over_cols(first_op, second_op):
    return dot(first_op, second_op, ((1,), (1,)))


def local(
    activations, cotangent, lengths, dealing, qkv_weight, qv_bias, out_weight, out_bias,
    first_gain, first_shift, up_weight, up_bias, down_weight, down_bias, second_gain, second_shift,
):
    unit = lax.axis_size("dp")
    pack = lax.axis_index("dp")
    core = lax.axis_index("tensor")
    rows = activations.shape[0]
    width = activations.shape[2]
    half = rows // unit // 2

    def swap(x):
        return lax.ppermute(x, "tensor", [(0, 1), (1, 0)])

    core_arg = core.astype(jnp.int32).reshape(1)

    def send_back(field):
        got = lax.all_to_all(field.reshape(unit, half, width), "dp", 0, 0, tiled=True)
        return got.reshape(rows // 2, width)

    def undealt(own, sib):
        back = undeal(own, sib, lengths, dealing, core_arg, unit, half)
        return back.reshape(rows, 1, width)

    table, key_extra, query_extra = plan(lengths, dealing, rows, unit, half)
    x_own, x_sib, dealt_cotangent = deal(
        activations.reshape(rows, width), cotangent.reshape(rows, width), table, unit, half, 2
    )
    out_sib, up_sib, down_sib = swap(out_weight), swap(up_weight), swap(down_weight)
    up_bias_sib = swap(up_bias)

    qkv_planes = jnp.transpose(qkv_weight, (1, 0, 2))
    (
        queries, key_rows, values, context_own, context_sib, context_wide, log_total, cotangent_own,
    ) = attn_fwd(
        x_own, x_sib, qkv_planes, qv_bias, key_extra, query_extra, dealt_cotangent, unit, half, 3
    )
    vec_in = jnp.concatenate(
        [
            jnp.stack(
                [out_bias, first_gain, first_shift, down_bias, second_gain, second_shift], axis=0
            ),
            jnp.zeros((2, width), F32),
        ],
        axis=0,
    )
    (
        first_low, active_own, active_sib, grad_branch, grad_up_own, grad_up_sib, grad_attn,
        grad_h1, grad_context_own, grad_context_sib, vectors, up_bias_parts, got_own, got_sib,
    ) = feed_forward(
        x_own, context_own, context_sib, cotangent_own,
        (out_weight, out_sib, up_weight, up_sib, down_weight, down_sib),
        vec_in, up_bias[None], up_bias_sib[None], unit, half, 4,
    )
    shard = down_weight.shape[0]
    granule = row_unit(unit)

    def chip_sum(own_part, sib_part):
        return (own_part + swap(sib_part.astype(BF)).astype(F32)).astype(BF)

    def stacked(parts, rows_of):
        size = sum(part.shape[0] for part in parts)
        pad = -size % rows_of
        if pad:
            parts = parts + [jnp.zeros((pad, parts[0].shape[1]), parts[0].dtype)]
        return jnp.concatenate(parts, axis=0)

    part_own = over_rows(active_own, grad_branch)
    part_sib = over_rows(active_sib, grad_branch).astype(BF)
    wide_down = stacked([chip_sum(part_own, part_sib)], granule)
    came = []
    for (start, count), order in zip(
        cut_rows(wide_down.shape[0], unit), bit_orders(unit.bit_length() - 1)
    ):
        step = 2 ** order[0]
        away = lax.dynamic_slice_in_dim(
            wide_down, start + (1 - pack // step % 2) * (count // 2), count // 2, 0
        )
        came.append(lax.ppermute(away, "dp", [(i, i ^ step) for i in range(unit)]))
    grad_context = jnp.concatenate([grad_context_own, swap(grad_context_sib)], axis=0)
    up_part = chip_sum(over_rows(first_low, grad_up_own), over_rows(first_low, grad_up_sib))
    out_part = chip_sum(over_rows(context_own, grad_attn), over_rows(context_sib, grad_attn))
    up_bias_part = up_bias_parts[0] + swap(up_bias_parts[1])
    vectors = vectors[:6]
    vectors = stacked([vectors + swap(vectors), up_bias_part.reshape(-1, width)], 8)
    wide_up = stacked(
        [up_part[:, first : first + width] for first in range(0, shard, width)] + [out_part], granule
    )
    input_part, input_sib, qkv_part, qv_part, vectors, sum_down, sum_up = attn_bwd(
        queries, key_rows, values, grad_context, context_wide, log_total, key_extra, query_extra,
        x_own, x_sib, qkv_planes, wide_down, wide_up, vectors, came, unit, 0,
    )
    inputs_own, inputs_sib, summed, qv_sum = tail(
        grad_h1, input_part, input_sib, stacked([qkv_part], granule), qv_part, unit, half, 1
    )
    grad_qkv_weight = jnp.stack(
        [summed[first : first + width] for first in range(0, 3 * width, width)], axis=1
    ).astype(F32)
    grad_qv_bias = qv_sum[:2]
    grad_down_weight = sum_down[:shard].astype(F32)
    grad_up_weight = jnp.concatenate(
        [sum_up[first : first + width] for first in range(0, shard, width)], axis=1
    ).astype(F32)
    grad_out_weight = sum_up[shard : shard + out_part.shape[0]].astype(F32)
    (
        grad_out_bias,
        grad_first_gain,
        grad_first_shift,
        grad_down_bias,
        grad_second_gain,
        grad_second_shift,
    ) = vectors[:6]
    grad_up_bias = vectors[6 : 6 + shard // width].reshape(-1)

    output = undealt(got_own, got_sib)
    input_grad = undealt(inputs_own, inputs_sib)
    return (
        output,
        input_grad,
        grad_qkv_weight,
        grad_qv_bias,
        grad_out_weight,
        grad_out_bias,
        grad_first_gain,
        grad_first_shift,
        grad_up_weight,
        grad_up_bias,
        grad_down_weight,
        grad_down_bias,
        grad_second_gain,
        grad_second_shift,
    )


def solution(mesh):
    placed = (
        P(None, "dp", None),
        P(None, "dp", None),
        P(),
        P(),
        P(None, None, "tensor"),
        P(None, "tensor"),
        P("tensor", None),
        P(),
        P(),
        P(),
        P(None, "tensor"),
        P("tensor"),
        P("tensor", None),
        P(),
        P(),
        P(),
    )
    return jax.shard_map(
        local,
        mesh=mesh,
        in_specs=placed,
        out_specs=(
            P(None, "dp", None),
            P(None, "dp", None),
            P(None, None, "tensor"),
            P(None, "tensor"),
            P("tensor", None),
            P(),
            P(),
            P(),
            P(None, "tensor"),
            P("tensor"),
            P("tensor", None),
            P(),
            P(),
            P(),
        ),
        check_vma=False,
    )
```

```python
import functools
import math

import jax
import jax.numpy as jnp
from jax import lax
from jax.experimental import pallas as pl
from jax.experimental.pallas import tpu as pltpu
from jax.sharding import PartitionSpec as P

HD = 64
BF = jnp.bfloat16
F32 = jnp.float32
MASKED_SCORE = -1e30
NORM_EPSILON = 1e-05
EXTRA = 16
ROOM = 56 * 2**20


def dot(a, b, dims=((1,), (0,))):
    return lax.dot_general(a, b, (dims, ((), ())), preferred_element_type=F32)


def unit_starts(lengths, starts, unit):
    def step(s, total):
        starts[s] = total
        return total + (lengths[s] + unit - 1) // unit

    lax.fori_loop(0, lengths.shape[0], step, jnp.int32(0))


def pack_windows(lengths, dealing, starts, unit, pack, first, rows, total):
    seq_a = dealing[2 * pack]
    seq_b = dealing[2 * pack + 1]
    units_a = (lengths[seq_a] + unit - 1) // unit
    shift_a = starts[seq_a]
    shift_b = starts[seq_b] - units_a
    bases = []
    for shift in (shift_a, shift_b):
        base = jnp.clip((shift + first) // 16 * 16, 0, total - rows - 16)
        bases.append(pl.multiple_of(base, 16))
    return units_a, shift_a, shift_b, bases


def plan_kernel(unit, half, lengths, dealing, table, kx_ref, qx_ref, starts):
    unit_starts(lengths, starts, unit)

    def one(pack, carry):
        units_a = (lengths[dealing[2 * pack]] + unit - 1) // unit
        table[0, pack] = units_a
        table[1, pack] = starts[dealing[2 * pack]]
        table[2, pack] = starts[dealing[2 * pack + 1]] - units_a
        return carry

    lax.fori_loop(0, unit, one, 0)
    pack = lax.axis_index("dp")
    core = lax.axis_index("tensor")
    len_a, len_b = lengths[dealing[2 * pack]], lengths[dealing[2 * pack + 1]]
    split = (len_a + unit - 1) // unit * unit
    rows = kx_ref.shape[0]

    def place(at):
        at_core = jnp.where(at < rows // 2, core, 1 - core)
        return (at_core * half + at % half) * unit + at % (rows // 2) // half

    row = place(lax.broadcasted_iota(jnp.int32, kx_ref.shape, 0))
    lane = lax.broadcasted_iota(jnp.int32, kx_ref.shape, 1)
    later = row >= split
    live = row < jnp.where(later, split + len_b, len_a)
    barred = (lane == jnp.where(later, 0, 1)) | ~live
    kx_ref[...] = jnp.where(
        lane < 2, jnp.where(barred, MASKED_SCORE, 0.0), jnp.where(lane < 5, -1.0, 0.0)
    ).astype(BF)
    col = place(lax.broadcasted_iota(jnp.int32, qx_ref.shape, 1))
    turn = lax.broadcasted_iota(jnp.int32, qx_ref.shape, 0)
    qx_ref[...] = jnp.where(turn == jnp.where(col >= split, 1, 0), 1.0, 0.0).astype(BF)


def plan(lengths, dealing, rows, unit, half):
    smem = pl.BlockSpec(memory_space=pltpu.SMEM)
    vmem = pl.BlockSpec(memory_space=pltpu.VMEM)
    return pl.pallas_call(
        functools.partial(plan_kernel, unit, half),
        in_specs=[smem, smem],
        out_specs=[smem, vmem, vmem],
        out_shape=[
            jax.ShapeDtypeStruct((3, unit), jnp.int32),
            jax.ShapeDtypeStruct((rows, 128), BF),
            jax.ShapeDtypeStruct((EXTRA, rows), BF),
        ],
        scratch_shapes=[pltpu.SMEM(lengths.shape, jnp.int32)],
        name="plan",
    )(lengths, dealing)


def greet(count, with_sibling=True):
    barrier = pltpu.get_barrier_semaphore()
    me = lax.axis_index("dp")

    def one(k, carry):
        pl.semaphore_signal(
            barrier, 1, device_id={"dp": (me + k) % count}, device_id_type=pl.DeviceIdType.MESH
        )
        return carry

    lax.fori_loop(1, count, one, 0)
    pl.semaphore_signal(
        barrier,
        1,
        device_id={"tensor": 1 - lax.axis_index("tensor")},
        device_id_type=pl.DeviceIdType.MESH,
    )
    pl.semaphore_wait(barrier, count)


class PackExchange:
    def __init__(self, count, block, source, target, send_sem, recv_sem):
        self.count, self.block = count, block
        self.source, self.target = source, target
        self.send_sem, self.recv_sem = send_sem, recv_sem
        self.me = lax.axis_index("dp")

    def rows(self, ref, i):
        return ref.at[pl.ds(pl.multiple_of(i * self.block, 16), self.block)]

    def copy(self, peer, landing, sem):
        return pltpu.make_async_remote_copy(
            src_ref=self.rows(self.source, peer),
            dst_ref=self.rows(self.target, landing),
            send_sem=self.send_sem.at[peer],
            recv_sem=self.recv_sem.at[sem],
            device_id={"dp": peer},
            device_id_type=pl.DeviceIdType.MESH,
        )

    def send(self, peer):
        self.copy(peer, self.me, self.me).start()

    def wait_from(self, peer):
        self.copy(peer, peer, peer).wait_recv()

    def wait_sent(self, peer):
        self.copy(peer, self.me, self.me).wait_send()

    def peers(self, body, first=0, last=None):
        def one(i, carry):
            far = self.count // 2 * (1 + (i + 1) % 2) - 1 - i // 2
            body(self.across(self.me, far, self.count))
            return carry

        lax.fori_loop(first, self.count - 1 if last is None else last, one, 0)

    @staticmethod
    def across(index, far, count):
        peer = 0
        for bit in range(count.bit_length() - 1):
            weight = 2**bit
            peer += (index // weight % 2 + far // weight % 2) % 2 * weight
        return peer

    def keep_own(self):
        self.rows(self.target, self.me)[...] = self.rows(self.source, self.me)[...]


def to_sibling(source, target, send_sem, recv_sem):
    return pltpu.make_async_remote_copy(
        src_ref=source,
        dst_ref=target,
        send_sem=send_sem,
        recv_sem=recv_sem,
        device_id={"tensor": 1 - lax.axis_index("tensor")},
        device_id_type=pl.DeviceIdType.MESH,
    )


def deal_kernel(
    unit, half, table, x_ref, g_hbm, own_ref, sib_ref, dealt_g,
    outbox, g_ref, load_sem, send_sem, recv_sem, pass_sem, take_sem,
):
    total = x_ref.shape[0]
    load = pltpu.make_async_copy(g_hbm, g_ref, load_sem)
    load.start()
    greet(unit)
    first = lax.axis_index("tensor") * half
    slot = first + lax.broadcasted_iota(jnp.int32, (half, total), 0)
    col = lax.broadcasted_iota(jnp.int32, (half, total), 1)
    swap = PackExchange(unit, half, outbox, own_ref, send_sem, recv_sem)
    team = 4

    def dealt(ref, packs, target):
        picks = []
        for i in range(team):
            pack = packs * team + i
            shift = jnp.where(slot < table[0, pack], table[1, pack], table[2, pack])
            picks.append(jnp.where(col == slot + shift, 1.0, 0.0).astype(BF))
        rows = dot(jnp.concatenate(picks, axis=0), ref[...]).astype(BF)
        at = pl.multiple_of(packs * team * half, 16)
        target[pl.ds(at, team * half)] = rows

    def passed(pack):
        return to_sibling(
            swap.rows(own_ref, pack), swap.rows(sib_ref, pack), pass_sem.at[pack], take_sem.at[pack]
        )

    def pass_on(pack):
        swap.wait_from(pack)
        passed(pack).start()

    home = swap.me // team

    def deal_out(i, carry):
        teams = [swap.across(home, far - i, unit // team) for far in far_teams]
        for packs in teams:
            dealt(x_ref, packs, outbox)

        def send(j, carry):
            for packs in teams:
                pack = packs * team + j

                @pl.when(pack != swap.me)
                def _(pack=pack):
                    swap.send(pack)

            return carry

        lax.fori_loop(0, team, send, 0)
        return carry

    far_teams = (unit // team - 1, unit // team // 2 - 1)
    lax.fori_loop(0, unit // team // 2, deal_out, 0)
    swap.keep_own()
    passed(swap.me).start()
    load.wait()

    def keep(packs, carry):
        dealt(g_ref, packs, dealt_g)
        return carry

    lax.fori_loop(0, unit // team, keep, 0)
    swap.peers(pass_on)
    swap.peers(swap.wait_sent)

    def end(pack, carry):
        passed(pack).wait_recv()
        passed(pack).wait_send()
        return carry

    lax.fori_loop(0, unit, end, 0)


def deal(x, g, table, unit, half, ident):
    total, width = x.shape
    smem = pl.BlockSpec(memory_space=pltpu.SMEM)
    vmem = pl.BlockSpec(memory_space=pltpu.VMEM)
    return pl.pallas_call(
        functools.partial(deal_kernel, unit, half),
        in_specs=[smem, vmem, pl.BlockSpec(memory_space=pl.ANY)],
        out_specs=[vmem, vmem, vmem],
        out_shape=[jax.ShapeDtypeStruct((total // 2, width), BF)] * 3,
        scratch_shapes=[
            pltpu.VMEM((total // 2, width), BF),
            pltpu.VMEM((total, width), BF),
            pltpu.SemaphoreType.DMA,
            *[pltpu.SemaphoreType.DMA((unit,))] * 4,
        ],
        compiler_params=pltpu.CompilerParams(
            vmem_limit_bytes=ROOM, collective_id=ident, has_side_effects=True
        ),
        cost_estimate=pl.CostEstimate(
            flops=8 * total * width * half, bytes_accessed=40 * total * width, transcendentals=0
        ),
        name="deal",
    )(table, x, g)


def undeal_kernel(unit, half, lengths, dealing, core, own_ref, sib_ref, o_ref, starts):
    total = o_ref.shape[0]
    unit_starts(lengths, starts, unit)
    wide = half + 16
    row = lax.broadcasted_iota(jnp.int32, (2 * wide, half), 0)
    col = lax.broadcasted_iota(jnp.int32, (2 * wide, half), 1)
    o_ref[...] = jnp.zeros_like(o_ref)

    def one(pack, carry):
        for part, ref in ((core[0], own_ref), (1 - core[0], sib_ref)):
            first = part * half
            units_a, shift_a, shift_b, (base_a, base_b) = pack_windows(
                lengths, dealing, starts, unit, pack, first, half, total
            )
            slot = first + col
            near = slot < units_a
            at = jnp.where(near, slot + (shift_a - base_a), slot + (shift_b - base_b + wide))
            pick = (row == at) & (near == (row < wide))
            rows = ref[pl.ds(pl.multiple_of(pack * half, 16), half), :]
            both = dot(pick.astype(F32).astype(BF), rows).astype(BF)
            o_ref[pl.ds(base_a, wide), :] += both[:wide]
            o_ref[pl.ds(base_b, wide), :] += both[wide:]
        return carry

    lax.fori_loop(0, total // (2 * half), one, 0, unroll=2)


def undeal(own, sib, lengths, dealing, core, unit, half):
    total, width = 2 * own.shape[0], own.shape[1]
    smem = pl.BlockSpec(memory_space=pltpu.SMEM)
    vmem = pl.BlockSpec(memory_space=pltpu.VMEM)
    return pl.pallas_call(
        functools.partial(undeal_kernel, unit, half),
        in_specs=[smem, smem, smem, vmem, vmem],
        out_specs=vmem,
        out_shape=jax.ShapeDtypeStruct((total, width), BF),
        scratch_shapes=[pltpu.SMEM(lengths.shape, jnp.int32)],
        compiler_params=pltpu.CompilerParams(vmem_limit_bytes=ROOM),
        cost_estimate=pl.CostEstimate(
            flops=8 * total * width * half, bytes_accessed=4 * total * width, transcendentals=0
        ),
        name="undeal",
    )(lengths, dealing, core, own, sib)


def fwd_kernel(
    ck, unit, half, x_own, x_sib, w_ref, b_ref, kx_ref, qx_ref, dealt_g,
    q_ref, k_ref, v_ref, c_ref, c_other_out, c32_ref, lse_ref, got_g_out,
    kext, vt, c_sib, c_other, got_g, send_sem, recv_sem, pass_sem, take_sem,
):
    n = k_ref.shape[0]
    pair = pl.program_id(0)
    swap = PackExchange(unit, half, dealt_g, got_g, send_sem, recv_sem)

    def passed(pair):
        cols = pl.ds(pl.multiple_of(pair * 128, 128), 128)
        return to_sibling(
            c_sib.at[:, cols], c_other.at[:, cols], pass_sem.at[pair], take_sem.at[pair]
        )

    @pl.when(pair == 0)
    def _():
        greet(unit)
        swap.peers(swap.send)
        swap.keep_own()

    w = jnp.concatenate([w_ref[0], w_ref[1], w_ref[2]], axis=1)
    bias = jnp.concatenate([b_ref[0:1], jnp.zeros((1, 128), F32), b_ref[1:2]], axis=1)
    for part, x_ref in enumerate((x_own, x_sib)):
        for first in range(0, n // 2, 512):
            made = (dot(x_ref[first : first + 512], w) + bias).astype(BF)
            at = slice(part * n // 2 + first, part * n // 2 + first + 512)
            for j, ref in enumerate((q_ref, k_ref, v_ref)):
                ref[at] = made[:, 128 * j : 128 * j + 128]
    kext[:, :128] = k_ref[...]
    kext[:, 128:] = kx_ref[...]
    v_t = v_ref[...].T
    ones = jnp.where(lax.broadcasted_iota(jnp.int32, (EXTRA, n), 0) == 0, 1.0, 0.0).astype(BF)
    for h in range(2):
        vt[h, :HD] = v_t[HD * h : HD * h + HD]
        vt[h, HD:] = ones
    q_t = (q_ref[...] * BF(HD**-0.5)).T
    zero = jnp.zeros((HD, n), BF)
    qx = qx_ref[...]
    q_ext = [
        jnp.concatenate([q_t[:HD], zero, qx], axis=0),
        jnp.concatenate([zero, q_t[HD:], qx], axis=0),
    ]
    tops, sums = [None, None], [None, None]
    for first in range(0, n, ck):
        keys = slice(first, first + ck)
        for h in range(2):
            s = dot(kext[keys, : 128 + EXTRA], q_ext[h])
            top = jnp.max(s, axis=0, keepdims=True)
            if first:
                top = jnp.maximum(tops[h], top)
            part = dot(vt[h, :, keys], jnp.exp(s - top).astype(BF))
            if first:
                part = part + sums[h] * jnp.exp(tops[h] - top)
            tops[h], sums[h] = top, part
    outs = []
    for h in range(2):
        total = sums[h][HD : HD + 1]
        outs.append(sums[h][:HD] / total)
        lse_ref[0, h : h + 1] = tops[h] + jnp.log(total)
    c = jnp.concatenate(outs, axis=0).T
    c32_ref[...] = c
    c_ref[...] = c[: n // 2].astype(BF)
    c_sib[:, pl.ds(pl.multiple_of(pair * 128, 128), 128)] = c[n // 2 :].astype(BF)
    passed(pair).start()

    @pl.when(pair == pl.num_programs(0) - 1)
    def _():
        swap.peers(swap.wait_from)
        swap.peers(swap.wait_sent)

        def end(pair, carry):
            passed(pair).wait_recv()
            passed(pair).wait_send()
            return carry

        lax.fori_loop(0, pl.num_programs(0), end, 0)
        c_other_out[...] = c_other[...]
        got_g_out[...] = got_g[...]


def attn_cost(n, width, products):
    return pl.CostEstimate(
        flops=products * 2 * 4 * n * n * width,
        bytes_accessed=16 * n * width,
        transcendentals=n * n * width // HD,
    )


def attn_fwd(x_own, x_sib, w, b, kx, qx, dealt_g, unit, half, ident, ck=512):
    n, model = 2 * x_own.shape[0], x_own.shape[1]
    width = w.shape[2]
    pairs = width // 128
    keys = pl.BlockSpec((n, 128), lambda p: (0, p))

    def whole(shape):
        return pl.BlockSpec(shape, lambda p: (0, 0), pipeline_mode=pl.Buffered(1))

    return pl.pallas_call(
        functools.partial(fwd_kernel, ck, unit, half),
        grid=(pairs,),
        in_specs=[
            whole(x_own.shape),
            whole(x_sib.shape),
            pl.BlockSpec((3, model, 128), lambda p: (0, 0, p)),
            pl.BlockSpec((2, 128), lambda p: (0, p)),
            whole(kx.shape),
            whole(qx.shape),
            whole(dealt_g.shape),
        ],
        out_specs=[
            keys,
            keys,
            keys,
            pl.BlockSpec((n // 2, 128), lambda p: (0, p)),
            whole((n // 2, width)),
            keys,
            pl.BlockSpec((1, 2, n), lambda p: (p, 0, 0)),
            whole(dealt_g.shape),
        ],
        out_shape=[jax.ShapeDtypeStruct((n, width), BF)] * 3
        + [jax.ShapeDtypeStruct((n // 2, width), BF)] * 2
        + [
            jax.ShapeDtypeStruct((n, width), F32),
            jax.ShapeDtypeStruct((pairs, 2, n), F32),
            jax.ShapeDtypeStruct(dealt_g.shape, BF),
        ],
        scratch_shapes=[
            pltpu.VMEM((n, 256), BF),
            pltpu.VMEM((2, HD + EXTRA, n), BF),
            pltpu.VMEM((n // 2, width), BF),
            pltpu.VMEM((n // 2, width), BF),
            pltpu.VMEM(dealt_g.shape, BF),
            *[pltpu.SemaphoreType.DMA((unit,))] * 2,
            *[pltpu.SemaphoreType.DMA((pairs,))] * 2,
        ],
        compiler_params=pltpu.CompilerParams(
            vmem_limit_bytes=ROOM, collective_id=ident, has_side_effects=True
        ),
        cost_estimate=attn_cost(n, width, 2),
        name="attn_fwd",
    )(x_own, x_sib, w, b, kx, qx, dealt_g)


def split3(x):
    high = x.astype(BF)
    rest = x - high.astype(F32)
    middle = rest.astype(BF)
    return high, middle, (rest - middle.astype(F32)).astype(BF)


def bit_orders(bits):
    first = list(range(bits))
    second = [1, 2, 0] + list(range(3, bits))
    third = [2, 0, 1] + list(range(3, bits))
    return first, second, third


def row_unit(devices):
    return 8 * devices


def cut_rows(rows, devices):
    unit = row_unit(devices)
    units = rows // unit
    counts = [(units + 2) // 3, (units + 1) // 3, units // 3]
    starts = [0, counts[0], counts[0] + counts[1]]
    return [(s * unit, c * unit) for s, c in zip(starts, counts) if c]


def greet_partners(bits):
    me = lax.axis_index("dp")
    barrier = pltpu.get_barrier_semaphore()
    for bit in range(bits):
        pl.semaphore_signal(
            barrier,
            inc=1,
            device_id={"dp": me + (1 - 2 * (me // 2**bit % 2)) * 2**bit},
            device_id_type=pl.DeviceIdType.MESH,
        )
    pl.semaphore_wait(barrier, bits)


class PackSum:
    def __init__(self, devices, big, small, out, came, acc, inbox, small_box, send_sem, recv_sem):
        self.came = came
        self.bits = devices.bit_length() - 1
        self.me = lax.axis_index("dp")
        self.big, self.small, self.acc, self.inbox, self.out = big, small, acc, inbox, out
        self.small_box = small_box
        self.send_sem, self.recv_sem = send_sem, recv_sem
        self.parts = [
            (start, count, order)
            for (start, count), order in zip(cut_rows(big.shape[0], devices), bit_orders(self.bits))
        ]
        self.steps = 2 * self.bits

    def slots(self, first, slot_us, last):
        size = 4e-3 * self.big.shape[0] * self.big.shape[1]
        sizes = [size / 2 ** (level + 1) / 3 for level in range(self.bits - 1)]
        sizes = sizes + [size / 2 ** (self.bits - 2)] + sizes[::-1]
        at, out = 0.0, []
        for step in range(self.steps):
            out.append(min(last, first + math.ceil(at / slot_us)))
            if step < len(sizes) and not (step == 0 and self.came):
                at += 4.5 + sizes[step] / 80
        return out

    @staticmethod
    def scratch(rows, cols, small_shape, devices):
        bits = devices.bit_length() - 1
        return [
            pltpu.VMEM((rows // 2, cols), BF),
            pltpu.VMEM((rows, cols), BF),
            pltpu.VMEM((2 * bits + 1,) + small_shape, F32),
            pltpu.SemaphoreType.DMA((4, 2 * bits)),
            pltpu.SemaphoreType.DMA((4, 2 * bits)),
        ]

    def side(self, bit):
        return (self.me // 2**bit) % 2

    def partner(self, bit):
        return self.me + (1 - 2 * self.side(bit)) * 2**bit

    def region(self, part, level):
        start, count, order = self.parts[part]
        for done in range(level):
            start = start + self.side(order[done]) * (count // 2 ** (done + 1))
        return start, count // 2**level

    def halved(self, part, start):
        return self.parts[part][0] // 2 + start - self.region(part, 1)[0]

    def rows(self, ref, start, count):
        return ref.at[pl.ds(pl.multiple_of(start, 16), count)]

    def slot(self, part, level):
        start, count, _ = self.parts[part]
        return start + count - count // 2**level

    def sending(self, part, level):
        start, count = self.region(part, level)
        bit = self.parts[part][2][level]
        if level < self.bits - 1:
            count = count // 2
            start = start + (1 - self.side(bit)) * count
        return pltpu.make_async_remote_copy(
            src_ref=self.rows(self.acc, self.halved(part, start), count)
            if level
            else self.rows(self.big, start, count),
            dst_ref=self.inbox.at[pl.ds(self.slot(part, level), count)],
            send_sem=self.send_sem.at[part, level],
            recv_sem=self.recv_sem.at[part, level],
            device_id={"dp": self.partner(bit)},
            device_id_type=pl.DeviceIdType.MESH,
        )

    def doubling(self, part, level):
        mine = self.rows(self.out, *self.region(part, level + 1))
        return pltpu.make_async_remote_copy(
            src_ref=mine,
            dst_ref=mine,
            send_sem=self.send_sem.at[part, self.bits + level],
            recv_sem=self.recv_sem.at[part, self.bits + level],
            device_id={"dp": self.partner(self.parts[part][2][level])},
            device_id_type=pl.DeviceIdType.MESH,
        )

    def exchange(self, level):
        return pltpu.make_async_remote_copy(
            src_ref=self.small if level == 0 else self.small_box.at[self.bits + level],
            dst_ref=self.small_box.at[level],
            send_sem=self.send_sem.at[3, level],
            recv_sem=self.recv_sem.at[3, level],
            device_id={"dp": self.partner(level)},
            device_id_type=pl.DeviceIdType.MESH,
        )

    def add(self, part, level):
        last = level == self.bits - 1
        kept, count = self.region(part, level if last else level + 1)
        source, first = (self.acc, self.halved(part, kept)) if level else (self.big, kept)
        if last:
            target, goal = self.out, kept
        else:
            target, goal = self.acc, self.halved(part, kept)
        slot, box = self.slot(part, level), self.inbox
        if self.came and level == 0:
            slot, box = 0, self.came[part]
        tile = math.gcd(count, 64)

        def one(i, carry):
            def at(start):
                return pl.ds(pl.multiple_of(start + i * tile, 16), tile)

            total = source[at(first), :].astype(F32) + box[at(slot), :].astype(F32)
            target[at(goal), :] = total.astype(BF)
            return carry

        lax.fori_loop(0, count // tile, one, 0)

    def step(self, k):
        bits = self.bits
        for part in range(len(self.parts)):
            if 0 < k <= bits:
                if not (self.came and k == 1):
                    self.sending(part, k - 1).wait_recv()
                self.add(part, k - 1)
            elif k > bits:
                self.doubling(part, 2 * bits - 1 - k).wait_recv()
            if k < bits:
                self.sending(part, k).start()
            elif k < self.steps - 1:
                self.doubling(part, 2 * bits - 2 - k).start()
        if self.small is not None:
            if 0 < k <= bits:
                self.exchange(k - 1).wait_recv()
                held = self.small[...] if k == 1 else self.small_box[bits + k - 1]
                self.small_box[bits + k] = held + self.small_box[k - 1]
            if k < bits:
                self.exchange(k).start()
        if k == self.steps - 1:
            for part in range(len(self.parts)):
                for level in range(1 if self.came else 0, bits):
                    self.sending(part, level).wait_send()
                for level in range(bits - 1):
                    self.doubling(part, level).wait_send()
            if self.small is not None:
                for level in range(bits):
                    self.exchange(level).wait_send()


SLOT_US = 3.6


def bwd_kernel(
    ck, devices, turns, q_ref, k_ref, v_ref, g_ref, c32_ref, lse_ref, kx_ref, qx_ref,
    x_own, x_sib, w_ref, big_a, big_b, small, *refs,
):
    i = pl.program_id(1)
    n = k_ref.shape[0]
    bq = q_ref.shape[0]
    count = len(cut_rows(big_a.shape[0], devices))
    came, refs = refs[:count], refs[count:]
    dx_ref, dx_sib_ref, dw_ref, db_ref, small_out, out_a, out_b = refs[:7]
    kext, vext, kt, x_t, dq_acc, dk_acc, dv_acc, dx_sib, sum_a, sum_b, *comm_refs = refs[7:]
    comm_a = PackSum(devices, big_a, None, sum_a, came, *comm_refs[:5])
    comm_b = PackSum(devices, big_b, small, sum_b, None, *comm_refs[5:])
    turn = pl.program_id(0) * pl.num_programs(1) + i
    per_turn = n // ck
    slots = turns * per_turn
    slots_a = comm_a.slots(0, SLOT_US, slots)
    slots_b = comm_b.slots(0, SLOT_US, slots)

    def comm_at(which):
        for comm, at in ((comm_a, slots_a), (comm_b, slots_b)):
            for step, slot in enumerate(at):
                if step == 0 and comm.came:
                    continue
                if slot < slots and slot % per_turn == which:

                    @pl.when(turn == slot // per_turn)
                    def _(comm=comm, step=step):
                        comm.step(step)

                elif slot == slots and which is None:
                    comm.step(step)

    @pl.when(turn == 0)
    def _():
        greet_partners(comm_a.bits)

    @pl.when(i == 0)
    def _():
        kext[:, :128] = k_ref[...]
        kext[:, 128:] = kx_ref[...]
        vext[:, :128] = v_ref[...]
        lane = lax.broadcasted_iota(jnp.int32, (n, 128), 1)
        vext[:, 128:] = jnp.where((lane >= 2) & (lane < 5), -1.0, 0.0).astype(BF)
        kt[...] = k_ref[...].T
        dk_acc[...] = jnp.zeros_like(dk_acc)
        dv_acc[...] = jnp.zeros_like(dv_acc)

    q = q_ref[...] * BF(HD**-0.5)
    g = g_ref[...]
    q_t, g_t = q.T, g.T
    prod_t = (g.astype(F32) * c32_ref[...]).T
    zero = jnp.zeros((HD, bq), BF)
    lane = lax.broadcasted_iota(jnp.int32, (bq, 128), 1)
    row = lax.broadcasted_iota(jnp.int32, (EXTRA, bq), 0)
    qx = qx_ref[...].astype(F32)

    def with_rows(base, parts):
        for j, part in enumerate(parts):
            base = jnp.where(row == 2 + j, part.astype(F32), base)
        return base.astype(BF)

    q_ext, g_ext, q_own, g_own, dq_t = [], [], [], [], []
    for h in range(2):
        mine = slice(HD * h, HD * h + HD)
        delta = jnp.sum(prod_t[mine], axis=0, keepdims=True)
        q_rows = with_rows(qx, split3(lse_ref[0, h : h + 1]))
        g_rows = with_rows(jnp.zeros((EXTRA, bq), F32), split3(delta))
        for out, turned, extra in ((q_ext, q_t, q_rows), (g_ext, g_t, g_rows)):
            both = [turned[mine], zero] if h == 0 else [zero, turned[mine]]
            out.append(jnp.concatenate(both + [extra], axis=0))
        ours = (lane < HD) if h == 0 else (lane >= HD)
        q_own.append(jnp.where(ours, q, BF(0)))
        g_own.append(jnp.where(ours, g, BF(0)))
        dq_t.append(jnp.zeros((HD, bq), F32))
    for first in range(0, n, ck):
        comm_at(first // ck)
        keys = slice(first, first + ck)
        dv = jnp.zeros((ck, 128), F32)
        dk = jnp.zeros((ck, 128), F32)
        for h in range(2):
            p = jnp.exp(dot(kext[keys, : 128 + EXTRA], q_ext[h]))
            ds = (p * dot(vext[keys, : 128 + EXTRA], g_ext[h])).astype(BF)
            dv = dv + dot(p.astype(BF), g_own[h])
            dk = dk + dot(ds, q_own[h])
            dq_t[h] = dq_t[h] + dot(kt[HD * h : HD * h + HD, keys], ds)
        dv_acc[keys] += dv
        dk_acc[keys] += dk
    dq = jnp.concatenate(dq_t, axis=0).T * HD**-0.5
    dq_acc[pl.ds(pl.multiple_of(i * bq, bq), bq)] = dq.astype(BF)

    @pl.when(turn == 0)
    def _():
        x_t[:, : n // 2] = x_own[...].T
        x_t[:, n // 2 :] = x_sib[...].T
        dx_ref[...] = jnp.zeros_like(dx_ref)
        dx_sib[...] = jnp.zeros_like(dx_sib)

    @pl.when(i == pl.num_programs(1) - 1)
    def _():
        width = x_own.shape[1]
        grads = [dq_acc[...], dk_acc[...].astype(BF), dv_acc[...].astype(BF)]
        joined = jnp.concatenate(grads, axis=1)
        made = dot(x_t[...], joined).astype(BF)
        for j in range(3):
            dw_ref[j * width : (j + 1) * width] = made[:, 128 * j : 128 * j + 128]
        bias = [jnp.sum(grad.astype(F32), axis=0, keepdims=True) for grad in grads[::2]]
        db_ref[...] = jnp.concatenate(bias + [jnp.zeros((6, 128), F32)], axis=0)
        tile = 512
        planes = jnp.concatenate([w_ref[j] for j in range(3)], axis=1)
        for first in range(0, n, tile):
            to_x = dot(joined[first : first + tile], planes, ((1,), (1,)))
            target, goal = (dx_ref, first) if first < n // 2 else (dx_sib, first - n // 2)
            target[goal : goal + tile] += to_x

    @pl.when(turn == turns - 1)
    def _():
        comm_at(None)
        dx_sib_ref[...] = dx_sib[...].astype(BF)
        out_a[...] = sum_a[...]
        out_b[...] = sum_b[...]
        small_out[...] = comm_b.small_box[2 * comm_b.bits]


def attn_bwd(q, k, v, g, c32, lse, kx, qx, x_own, x_sib, w, big_a, big_b, small, came, devices, ident, bq=1024, ck=512):
    n, width = q.shape
    pairs = width // 128
    model = x_own.shape[1]
    rows = pl.BlockSpec((bq, 128), lambda p, i: (i, p))
    keys = pl.BlockSpec((n, 128), lambda p, i: (0, p))
    def whole(shape):
        return pl.BlockSpec(shape, lambda p, i: (0, 0), pipeline_mode=pl.Buffered(1))

    return pl.pallas_call(
        functools.partial(bwd_kernel, ck, devices, pairs * (n // bq)),
        grid=(pairs, n // bq),
        in_specs=[
            rows,
            keys,
            keys,
            rows,
            rows,
            pl.BlockSpec((1, 2, bq), lambda p, i: (p, 0, i)),
            pl.BlockSpec((n, 128), lambda p, i: (0, 0)),
            pl.BlockSpec((EXTRA, bq), lambda p, i: (0, i)),
            whole(x_own.shape),
            whole(x_sib.shape),
            pl.BlockSpec((3, model, 128), lambda p, i: (0, 0, p)),
            whole(big_a.shape),
            whole(big_b.shape),
            whole(small.shape),
            *[whole(box.shape) for box in came],
        ],
        out_specs=[
            whole((n // 2, model)),
            whole((n // 2, model)),
            pl.BlockSpec((3 * model, 128), lambda p, i: (0, p)),
            pl.BlockSpec((8, 128), lambda p, i: (0, p)),
            whole(small.shape),
            whole(big_a.shape),
            whole(big_b.shape),
        ],
        out_shape=[
            jax.ShapeDtypeStruct((n // 2, model), F32),
            jax.ShapeDtypeStruct((n // 2, model), BF),
            jax.ShapeDtypeStruct((3 * model, width), BF),
            jax.ShapeDtypeStruct((8, width), F32),
            jax.ShapeDtypeStruct(small.shape, F32),
            jax.ShapeDtypeStruct(big_a.shape, BF),
            jax.ShapeDtypeStruct(big_b.shape, BF),
        ],
        scratch_shapes=[
            pltpu.VMEM((n, 256), BF),
            pltpu.VMEM((n, 256), BF),
            pltpu.VMEM((128, n), BF),
            pltpu.VMEM((model, n), BF),
            pltpu.VMEM((n, 128), BF),
            pltpu.VMEM((n, 128), F32),
            pltpu.VMEM((n, 128), F32),
            pltpu.VMEM((n // 2, model), F32),
            pltpu.VMEM(big_a.shape, BF),
            pltpu.VMEM(big_b.shape, BF),
            *PackSum.scratch(*big_a.shape, (8, 128), devices),
            *PackSum.scratch(*big_b.shape, small.shape, devices),
        ],
        compiler_params=pltpu.CompilerParams(
            vmem_limit_bytes=60 * 2**20, collective_id=ident, has_side_effects=True
        ),
        cost_estimate=attn_cost(n, width, 5),
        name="attn_bwd",
    )(q, k, v, g, c32, lse, kx, qx, x_own, x_sib, w, big_a, big_b, small, *came)


def norm_parts(field, gain, shift):
    center = field - jnp.mean(field, axis=-1, keepdims=True)
    inv_std = lax.rsqrt(jnp.mean(center * center, axis=-1, keepdims=True) + NORM_EPSILON)
    normed = center * inv_std
    return normed * gain + shift, normed, inv_std


def norm_back(incoming, normed, inv_std, gain):
    scaled = incoming * gain
    return inv_std * (
        scaled
        - jnp.mean(scaled, axis=-1, keepdims=True)
        - normed * jnp.mean(scaled * normed, axis=-1, keepdims=True)
    )


FF_ROWS = 256


def ff_kernel(
    unit, half, x_ref, c_own, c_sib, g_ref, out_own, out_sib, up_own, up_sib, down_own, down_sib,
    vec_ref, bias_own, bias_sib,
    h1_ref, dc_own, dc_sib, vec_out, bias_out, got_own_out, got_sib_out, down_out, up_out, down_sib_out, up_sib_out,
    z, got, got_sib, slope, act, du, low_all, branch_all, da_all, mine, theirs,
    send_sem, recv_sem, pass_sem, take_sem, out_sem, keep_sem,
):
    i = pl.program_id(0)
    blocks = pl.num_programs(0)
    swap = PackExchange(unit, half, z, got, send_sem, recv_sem)
    team = FF_ROWS // half
    block = ff_block(i, unit, half, z.shape[0] // FF_ROWS)

    def passed(pack):
        return to_sibling(
            swap.rows(got, pack), swap.rows(got_sib, pack), pass_sem.at[pack], take_sem.at[pack]
        )

    @pl.when(i == 0)
    def _():
        greet(unit)
        vec_out[...] = jnp.zeros_like(vec_out)
        bias_out[...] = jnp.zeros_like(bias_out)

    out_bias, first_gain, first_shift, down_bias, second_gain, second_shift = (
        vec_ref[j : j + 1] for j in range(6)
    )
    here = pl.ds(pl.multiple_of(block * FF_ROWS, 16), FF_ROWS)
    attention = dot(c_own[here, :], out_own[...]) + dot(c_sib[here, :], out_sib[...])
    first, first_normed, first_inv = norm_parts(
        x_ref[...].astype(F32) + attention + out_bias, first_gain, first_shift
    )
    low = first.astype(BF)
    low_all[here, :] = low
    shard = up_own.shape[1]
    wide = 512
    sides = ((up_own, down_own, bias_own), (up_sib, down_sib, bias_sib))
    down = jnp.zeros(first.shape, F32)
    for side, (up, back, bias) in enumerate(sides):
        for start in range(0, shard, wide):
            cols = slice(start, start + wide)
            at = slice(side * shard + start, side * shard + start + wide)
            upward = dot(low, up[:, cols]) + bias[:, cols]
            cumulative = 0.5 + 0.5 * lax.erf(upward * math.sqrt(0.5))
            density = jnp.exp(-0.5 * upward * upward) * (1.0 / math.sqrt(2.0 * math.pi))
            active = (upward * cumulative).astype(BF)
            act[here, at] = active
            slope[:, at] = cumulative + upward * density
            down = down + dot(active, back[cols])
    second, second_normed, second_inv = norm_parts(
        first + down + down_bias, second_gain, second_shift
    )
    z[here, :] = second.astype(BF)

    def send(j, carry):
        pack = block * team + j

        @pl.when(pack != swap.me)
        def _():
            swap.send(pack)

        return carry

    lax.fori_loop(0, team, send, 0)
    outer = g_ref[...].astype(F32)
    grad_h2 = norm_back(outer, second_normed, second_inv, second_gain)
    branch = grad_h2.astype(BF)
    branch_all[here, :] = branch
    grad_y1 = grad_h2
    for side, (up, back, _) in enumerate(sides):
        for start in range(0, shard, wide):
            cols = slice(start, start + wide)
            at = slice(side * shard + start, side * shard + start + wide)
            inner = (dot(branch, back[cols], ((1,), (1,))) * slope[:, at]).astype(BF)
            du[here, at] = inner
            bias_out[side : side + 1, cols] += jnp.sum(inner.astype(F32), axis=0, keepdims=True)
            grad_y1 = grad_y1 + dot(inner, up[:, cols], ((1,), (1,)))
    grad_h1 = norm_back(grad_y1, first_normed, first_inv, first_gain)
    h1_ref[...] = grad_h1
    da = grad_h1.astype(BF)
    da_all[here, :] = da
    dc_own[...] = dot(da, out_own[...], ((1,), (1,))).astype(BF)
    dc_sib[...] = dot(da, out_sib[...], ((1,), (1,))).astype(BF)
    terms = (
        grad_h1, grad_y1 * first_normed, grad_y1, grad_h2, outer * second_normed, outer,
    )
    for j, term in enumerate(terms):
        vec_out[j : j + 1] += jnp.sum(term, axis=0, keepdims=True)

    model = z.shape[1]
    pieces = [
        (start, wide, lambda side, start=start: dot(
            act[:, side * shard + start : side * shard + start + wide], branch_all[...], OVER_ROWS
        ))
        for start in range(0, shard, wide)
    ] + [
        (shard + start, model, lambda side, start=start: dot(
            low_all[...], du[:, side * shard + start : side * shard + start + model], OVER_ROWS
        ))
        for start in range(0, shard, model)
    ] + [
        (2 * shard, c_own.shape[1], lambda side: dot(
            (c_sib if side else c_own)[...], da_all[...], OVER_ROWS
        ))
    ]

    def put(j, side):
        start, size, _ = pieces[j]
        source = theirs if side else mine
        down, up = (down_sib_out, up_sib_out) if side else (down_out, up_out)
        target, goal = (down, start) if start < shard else (up, start - shard)
        return pltpu.make_async_copy(
            source.at[pl.ds(start, size)], target.at[pl.ds(goal, size)], out_sem.at[side, j]
        )

    @pl.when(i == blocks - 1)
    def _():
        swap.keep_own()
        passed(swap.me).start()
        for side, kept in ((1, theirs), (0, mine)):
            for j, (start, size, product) in enumerate(pieces):
                kept[start : start + size] = product(side).astype(BF)
                put(j, side).start()

        def pass_on(pack):
            swap.wait_from(pack)
            passed(pack).start()

        swap.peers(pass_on)
        swap.peers(swap.wait_sent)

        def end(pack, carry):
            passed(pack).wait()
            return carry

        lax.fori_loop(0, unit, end, 0)
        keep_own = pltpu.make_async_copy(got, got_own_out, keep_sem.at[0])
        keep_sib = pltpu.make_async_copy(got_sib, got_sib_out, keep_sem.at[1])
        keep_own.start()
        keep_sib.start()
        for j in range(len(pieces)):
            put(j, 0).wait()
            put(j, 1).wait()
        keep_own.wait()
        keep_sib.wait()


OVER_ROWS = ((0,), (0,))


def ff_block(i, unit, half, blocks):
    home = lax.axis_index("dp") // (FF_ROWS // half)
    return PackExchange.across(home, blocks - 1 - i, blocks)


def feed_forward(x, c_own, c_sib, g, weights, vectors, bias_own, bias_sib, unit, half, ident):
    n, model = x.shape
    shard = bias_own.shape[1]
    width = c_own.shape[1]
    blocks = n // FF_ROWS

    def rows(cols):
        return pl.BlockSpec((FF_ROWS, cols), lambda i: (ff_block(i, unit, half, blocks), 0))

    def whole(shape):
        return pl.BlockSpec(shape, lambda i: (0, 0), pipeline_mode=pl.Buffered(1))

    shapes = [(model, F32), (width, BF), (width, BF)]
    kept = [(vectors.shape, F32), ((8, shard), F32)]
    shares = 2 * shard + width
    count = shard // 512 + shard // model + 1
    put = [(n, model)] * 2 + [(shard, model), (shares - shard, model)] * 2
    return pl.pallas_call(
        functools.partial(ff_kernel, unit, half),
        grid=(blocks,),
        in_specs=[rows(model), whole(c_own.shape), whole(c_sib.shape), rows(model)]
        + [whole(w.shape) for w in weights]
        + [whole(vectors.shape), whole(bias_own.shape), whole(bias_sib.shape)],
        out_specs=[rows(cols) for cols, _ in shapes]
        + [whole(shape) for shape, _ in kept]
        + [pl.BlockSpec(memory_space=pl.ANY)] * len(put),
        out_shape=[jax.ShapeDtypeStruct((n, cols), dtype) for cols, dtype in shapes]
        + [jax.ShapeDtypeStruct(shape, dtype) for shape, dtype in kept]
        + [jax.ShapeDtypeStruct(shape, BF) for shape in put],
        scratch_shapes=[
            pltpu.VMEM((n, model), BF),
            pltpu.VMEM((n, model), BF),
            pltpu.VMEM((n, model), BF),
            pltpu.VMEM((FF_ROWS, 2 * shard), F32),
            pltpu.VMEM((n, 2 * shard), BF),
            pltpu.VMEM((n, 2 * shard), BF),
            *[pltpu.VMEM((n, model), BF)] * 3,
            pltpu.VMEM((shares, model), BF),
            pltpu.VMEM((shares, model), BF),
            *[pltpu.SemaphoreType.DMA((unit,))] * 4,
            pltpu.SemaphoreType.DMA((2, count)),
            pltpu.SemaphoreType.DMA((2,)),
        ],
        compiler_params=pltpu.CompilerParams(
            vmem_limit_bytes=62 * 2**20, collective_id=ident, has_side_effects=True
        ),
        cost_estimate=pl.CostEstimate(
            flops=8 * n * model * (width + shard) * 2,
            bytes_accessed=40 * n * model,
            transcendentals=4 * n * shard,
        ),
        name="feed_forward",
    )(x, c_own, c_sib, g, *weights, vectors, bias_own, bias_sib)


def tail_kernel(
    unit, half, h1_ref, dx_ref, dx_sib, big, small, own_ref, sib_ref, big_out, small_out,
    outbox, dx_came, mix_sem, mixed_sem, send_sem, recv_sem, pass_sem, take_sem, *comm_refs,
):
    comm = PackSum(unit, big, small, big_out, None, *comm_refs)
    swap = PackExchange(unit, half, outbox, own_ref, send_sem, recv_sem)

    def mix(pack):
        return to_sibling(
            swap.rows(dx_sib, pack),
            swap.rows(dx_came, pack),
            mix_sem.at[pack],
            mixed_sem.at[pack],
        )

    def passed(pack):
        return to_sibling(
            swap.rows(own_ref, pack), swap.rows(sib_ref, pack), pass_sem.at[pack], take_sem.at[pack]
        )

    def add_up(pack):
        mix(pack).wait_recv()
        at = swap.rows(dx_came, pack)[...].astype(F32)
        total = swap.rows(h1_ref, pack)[...] + swap.rows(dx_ref, pack)[...] + at
        swap.rows(outbox, pack)[...] = total.astype(BF)

    def add_and_send(pack):
        add_up(pack)
        swap.send(pack)

    def pass_on(pack):
        swap.wait_from(pack)
        passed(pack).start()

    greet(unit)
    swap.peers(lambda pack: mix(pack).start())
    mix(swap.me).start()
    comm.step(0)
    share = -(-(unit - 1) // 5)
    for k in range(1, 6):
        swap.peers(add_and_send, (k - 1) * share, min(k * share, unit - 1))
        comm.step(k)
    add_up(swap.me)
    swap.keep_own()
    passed(swap.me).start()
    for k in range(6, comm.steps):
        comm.step(k)
    small_out[...] = comm.small_box[2 * comm.bits]
    swap.peers(pass_on)
    swap.peers(swap.wait_sent)

    def end(pack, carry):
        mix(pack).wait_send()
        passed(pack).wait()
        return carry

    lax.fori_loop(0, unit, end, 0)


def tail(h1, dx, dx_sib, big, small, unit, half, ident):
    vmem = pl.BlockSpec(memory_space=pltpu.VMEM)
    kept = [jax.ShapeDtypeStruct(dx_sib.shape, BF)] * 2
    out_shape = kept + [
        jax.ShapeDtypeStruct(big.shape, BF),
        jax.ShapeDtypeStruct(small.shape, F32),
    ]
    return pl.pallas_call(
        functools.partial(tail_kernel, unit, half),
        in_specs=[vmem] * 5,
        out_specs=[vmem] * len(out_shape),
        out_shape=out_shape,
        scratch_shapes=[
            pltpu.VMEM(dx_sib.shape, BF),
            pltpu.VMEM(dx_sib.shape, BF),
            *[pltpu.SemaphoreType.DMA((unit,))] * 6,
            *PackSum.scratch(*big.shape, small.shape, unit),
        ],
        compiler_params=pltpu.CompilerParams(
            vmem_limit_bytes=ROOM, collective_id=ident, has_side_effects=True
        ),
        cost_estimate=pl.CostEstimate(flops=0, bytes_accessed=200 * big.size, transcendentals=0),
        name="tail",
    )(h1, dx, dx_sib, big, small)


def over_rows(first_op, second_op):
    return dot(first_op, second_op, ((0,), (0,)))


def over_cols(first_op, second_op):
    return dot(first_op, second_op, ((1,), (1,)))


def local(
    activations, cotangent, lengths, dealing, qkv_weight, qv_bias, out_weight, out_bias,
    first_gain, first_shift, up_weight, up_bias, down_weight, down_bias, second_gain, second_shift,
):
    unit = lax.axis_size("dp")
    pack = lax.axis_index("dp")
    core = lax.axis_index("tensor")
    rows = activations.shape[0]
    width = activations.shape[2]
    half = rows // unit // 2

    def swap(x):
        return lax.ppermute(x, "tensor", [(0, 1), (1, 0)])

    core_arg = core.astype(jnp.int32).reshape(1)

    def send_back(field):
        got = lax.all_to_all(field.reshape(unit, half, width), "dp", 0, 0, tiled=True)
        return got.reshape(rows // 2, width)

    def undealt(own, sib):
        back = undeal(own, sib, lengths, dealing, core_arg, unit, half)
        return back.reshape(rows, 1, width)

    table, key_extra, query_extra = plan(lengths, dealing, rows, unit, half)
    x_own, x_sib, dealt_cotangent = deal(
        activations.reshape(rows, width), cotangent.reshape(rows, width), table, unit, half, 2
    )
    out_sib, up_sib, down_sib = swap(out_weight), swap(up_weight), swap(down_weight)
    up_bias_sib = swap(up_bias)

    qkv_planes = jnp.transpose(qkv_weight, (1, 0, 2))
    (
        queries, key_rows, values, context_own, context_sib, context_wide, log_total, cotangent_own,
    ) = attn_fwd(
        x_own, x_sib, qkv_planes, qv_bias, key_extra, query_extra, dealt_cotangent, unit, half, 3
    )
    vec_in = jnp.concatenate(
        [
            jnp.stack(
                [out_bias, first_gain, first_shift, down_bias, second_gain, second_shift], axis=0
            ),
            jnp.zeros((2, width), F32),
        ],
        axis=0,
    )
    (
        grad_h1, grad_context_own, grad_context_sib, vectors, up_bias_parts, got_own, got_sib,
        down_own, up_own, down_other, up_other,
    ) = feed_forward(
        x_own, context_own, context_sib, cotangent_own,
        (out_weight, out_sib, up_weight, up_sib, down_weight, down_sib),
        vec_in, up_bias[None], up_bias_sib[None], unit, half, 4,
    )
    shard = down_weight.shape[0]
    granule = row_unit(unit)

    def stacked(parts, rows_of):
        size = sum(part.shape[0] for part in parts)
        pad = -size % rows_of
        if pad:
            parts = parts + [jnp.zeros((pad, parts[0].shape[1]), parts[0].dtype)]
        return jnp.concatenate(parts, axis=0) if len(parts) > 1 else parts[0]


    def chip_sum(own_part, sib_part):
        total = own_part.astype(F32) + swap(sib_part).astype(F32)
        return stacked([total.astype(BF)], granule)

    wide_down = chip_sum(down_own, down_other)
    came = []
    for (start, count), order in zip(
        cut_rows(wide_down.shape[0], unit), bit_orders(unit.bit_length() - 1)
    ):
        step = 2 ** order[0]
        away = lax.dynamic_slice_in_dim(
            wide_down, start + (1 - pack // step % 2) * (count // 2), count // 2, 0
        )
        came.append(lax.ppermute(away, "dp", [(i, i ^ step) for i in range(unit)]))
    grad_context = jnp.concatenate([grad_context_own, swap(grad_context_sib)], axis=0)
    up_bias_part = up_bias_parts[0] + swap(up_bias_parts[1])
    vectors = vectors[:6]
    vectors = stacked([vectors + swap(vectors), up_bias_part.reshape(-1, width)], 8)
    wide_up = chip_sum(up_own, up_other)
    input_part, input_sib, qkv_part, qv_part, vectors, sum_down, sum_up = attn_bwd(
        queries, key_rows, values, grad_context, context_wide, log_total, key_extra, query_extra,
        x_own, x_sib, qkv_planes, wide_down, wide_up, vectors, came, unit, 0,
    )
    inputs_own, inputs_sib, summed, qv_sum = tail(
        grad_h1, input_part, input_sib, stacked([qkv_part], granule), qv_part, unit, half, 1
    )
    grad_qkv_weight = jnp.stack(
        [summed[first : first + width] for first in range(0, 3 * width, width)], axis=1
    ).astype(F32)
    grad_qv_bias = qv_sum[:2]
    grad_down_weight = sum_down[:shard].astype(F32)
    grad_up_weight = jnp.concatenate(
        [sum_up[first : first + width] for first in range(0, shard, width)], axis=1
    ).astype(F32)
    grad_out_weight = sum_up[shard : shard + out_weight.shape[0]].astype(F32)
    (
        grad_out_bias,
        grad_first_gain,
        grad_first_shift,
        grad_down_bias,
        grad_second_gain,
        grad_second_shift,
    ) = vectors[:6]
    grad_up_bias = vectors[6 : 6 + shard // width].reshape(-1)

    output = undealt(got_own, got_sib)
    input_grad = undealt(inputs_own, inputs_sib)
    return (
        output,
        input_grad,
        grad_qkv_weight,
        grad_qv_bias,
        grad_out_weight,
        grad_out_bias,
        grad_first_gain,
        grad_first_shift,
        grad_up_weight,
        grad_up_bias,
        grad_down_weight,
        grad_down_bias,
        grad_second_gain,
        grad_second_shift,
    )


def solution(mesh):
    placed = (
        P(None, "dp", None),
        P(None, "dp", None),
        P(),
        P(),
        P(None, None, "tensor"),
        P(None, "tensor"),
        P("tensor", None),
        P(),
        P(),
        P(),
        P(None, "tensor"),
        P("tensor"),
        P("tensor", None),
        P(),
        P(),
        P(),
    )
    return jax.shard_map(
        local,
        mesh=mesh,
        in_specs=placed,
        out_specs=(
            P(None, "dp", None),
            P(None, "dp", None),
            P(None, None, "tensor"),
            P(None, "tensor"),
            P("tensor", None),
            P(),
            P(),
            P(),
            P(None, "tensor"),
            P("tensor"),
            P("tensor", None),
            P(),
            P(),
            P(),
        ),
        check_vma=False,
    )
```

```python
import functools
import math

import jax
import jax.numpy as jnp
from jax import lax
from jax.experimental import pallas as pl
from jax.experimental.pallas import tpu as pltpu
from jax.sharding import PartitionSpec as P

HD = 64
BF = jnp.bfloat16
F32 = jnp.float32
MASKED_SCORE = -1e30
NORM_EPSILON = 1e-05
EXTRA = 16
ROOM = 56 * 2**20


def dot(a, b, dims=((1,), (0,))):
    return lax.dot_general(a, b, (dims, ((), ())), preferred_element_type=F32)


def unit_starts(lengths, starts, unit):
    def step(s, total):
        starts[s] = total
        return total + (lengths[s] + unit - 1) // unit

    lax.fori_loop(0, lengths.shape[0], step, jnp.int32(0))


def pack_windows(lengths, dealing, starts, unit, pack, first, rows, total):
    seq_a = dealing[2 * pack]
    seq_b = dealing[2 * pack + 1]
    units_a = (lengths[seq_a] + unit - 1) // unit
    shift_a = starts[seq_a]
    shift_b = starts[seq_b] - units_a
    bases = []
    for shift in (shift_a, shift_b):
        base = jnp.clip((shift + first) // 16 * 16, 0, total - rows - 16)
        bases.append(pl.multiple_of(base, 16))
    return units_a, shift_a, shift_b, bases


def plan_kernel(unit, half, lengths, dealing, table, kx_ref, qx_ref, starts):
    unit_starts(lengths, starts, unit)

    def one(pack, carry):
        units_a = (lengths[dealing[2 * pack]] + unit - 1) // unit
        table[0, pack] = units_a
        table[1, pack] = starts[dealing[2 * pack]]
        table[2, pack] = starts[dealing[2 * pack + 1]] - units_a
        return carry

    lax.fori_loop(0, unit, one, 0)
    pack = lax.axis_index("dp")
    core = lax.axis_index("tensor")
    len_a, len_b = lengths[dealing[2 * pack]], lengths[dealing[2 * pack + 1]]
    split = (len_a + unit - 1) // unit * unit
    rows = kx_ref.shape[0]

    def place(at):
        at_core = jnp.where(at < rows // 2, core, 1 - core)
        return (at_core * half + at % half) * unit + at % (rows // 2) // half

    row = place(lax.broadcasted_iota(jnp.int32, kx_ref.shape, 0))
    lane = lax.broadcasted_iota(jnp.int32, kx_ref.shape, 1)
    later = row >= split
    live = row < jnp.where(later, split + len_b, len_a)
    barred = (lane == jnp.where(later, 0, 1)) | ~live
    kx_ref[...] = jnp.where(
        lane < 2, jnp.where(barred, MASKED_SCORE, 0.0), jnp.where(lane < 5, -1.0, 0.0)
    ).astype(BF)
    col = place(lax.broadcasted_iota(jnp.int32, qx_ref.shape, 1))
    turn = lax.broadcasted_iota(jnp.int32, qx_ref.shape, 0)
    qx_ref[...] = jnp.where(turn == jnp.where(col >= split, 1, 0), 1.0, 0.0).astype(BF)


def plan(lengths, dealing, rows, unit, half):
    smem = pl.BlockSpec(memory_space=pltpu.SMEM)
    vmem = pl.BlockSpec(memory_space=pltpu.VMEM)
    return pl.pallas_call(
        functools.partial(plan_kernel, unit, half),
        in_specs=[smem, smem],
        out_specs=[smem, vmem, vmem],
        out_shape=[
            jax.ShapeDtypeStruct((3, unit), jnp.int32),
            jax.ShapeDtypeStruct((rows, 128), BF),
            jax.ShapeDtypeStruct((EXTRA, rows), BF),
        ],
        scratch_shapes=[pltpu.SMEM(lengths.shape, jnp.int32)],
        name="plan",
    )(lengths, dealing)


def greet(count, with_sibling=True):
    barrier = pltpu.get_barrier_semaphore()
    me = lax.axis_index("dp")

    def one(k, carry):
        pl.semaphore_signal(
            barrier, 1, device_id={"dp": (me + k) % count}, device_id_type=pl.DeviceIdType.MESH
        )
        return carry

    lax.fori_loop(1, count, one, 0)
    pl.semaphore_signal(
        barrier,
        1,
        device_id={"tensor": 1 - lax.axis_index("tensor")},
        device_id_type=pl.DeviceIdType.MESH,
    )
    pl.semaphore_wait(barrier, count)


class PackExchange:
    def __init__(self, count, block, source, target, send_sem, recv_sem):
        self.count, self.block = count, block
        self.source, self.target = source, target
        self.send_sem, self.recv_sem = send_sem, recv_sem
        self.me = lax.axis_index("dp")

    def rows(self, ref, i):
        return ref.at[pl.ds(pl.multiple_of(i * self.block, 16), self.block)]

    def copy(self, peer, landing, sem):
        return pltpu.make_async_remote_copy(
            src_ref=self.rows(self.source, peer),
            dst_ref=self.rows(self.target, landing),
            send_sem=self.send_sem.at[peer],
            recv_sem=self.recv_sem.at[sem],
            device_id={"dp": peer},
            device_id_type=pl.DeviceIdType.MESH,
        )

    def send(self, peer):
        self.copy(peer, self.me, self.me).start()

    def wait_from(self, peer):
        self.copy(peer, peer, peer).wait_recv()

    def wait_sent(self, peer):
        self.copy(peer, self.me, self.me).wait_send()

    def peers(self, body, first=0, last=None):
        def one(i, carry):
            far = self.count // 2 * (1 + (i + 1) % 2) - 1 - i // 2
            body(self.across(self.me, far, self.count))
            return carry

        lax.fori_loop(first, self.count - 1 if last is None else last, one, 0)

    @staticmethod
    def across(index, far, count):
        peer = 0
        for bit in range(count.bit_length() - 1):
            weight = 2**bit
            peer += (index // weight % 2 + far // weight % 2) % 2 * weight
        return peer

    def keep_own(self):
        self.rows(self.target, self.me)[...] = self.rows(self.source, self.me)[...]


def to_sibling(source, target, send_sem, recv_sem):
    return pltpu.make_async_remote_copy(
        src_ref=source,
        dst_ref=target,
        send_sem=send_sem,
        recv_sem=recv_sem,
        device_id={"tensor": 1 - lax.axis_index("tensor")},
        device_id_type=pl.DeviceIdType.MESH,
    )


def deal_kernel(
    unit, half, table, x_ref, g_hbm, own_ref, sib_ref, dealt_g,
    outbox, g_ref, load_sem, send_sem, recv_sem, pass_sem, take_sem,
):
    total = x_ref.shape[0]
    load = pltpu.make_async_copy(g_hbm, g_ref, load_sem)
    load.start()
    greet(unit)
    first = lax.axis_index("tensor") * half
    slot = first + lax.broadcasted_iota(jnp.int32, (half, total), 0)
    col = lax.broadcasted_iota(jnp.int32, (half, total), 1)
    swap = PackExchange(unit, half, outbox, own_ref, send_sem, recv_sem)
    team = 4

    def dealt(ref, packs, target):
        picks = []
        for i in range(team):
            pack = packs * team + i
            shift = jnp.where(slot < table[0, pack], table[1, pack], table[2, pack])
            picks.append(jnp.where(col == slot + shift, 1.0, 0.0).astype(BF))
        rows = dot(jnp.concatenate(picks, axis=0), ref[...]).astype(BF)
        at = pl.multiple_of(packs * team * half, 16)
        target[pl.ds(at, team * half)] = rows

    def passed(pack):
        return to_sibling(
            swap.rows(own_ref, pack), swap.rows(sib_ref, pack), pass_sem.at[pack], take_sem.at[pack]
        )

    def pass_on(pack):
        swap.wait_from(pack)
        passed(pack).start()

    home = swap.me // team

    def deal_out(i, carry):
        teams = [swap.across(home, far - i, unit // team) for far in far_teams]
        for packs in teams:
            dealt(x_ref, packs, outbox)

        def send(j, carry):
            for packs in teams:
                pack = packs * team + j

                @pl.when(pack != swap.me)
                def _(pack=pack):
                    swap.send(pack)

            return carry

        lax.fori_loop(0, team, send, 0)
        return carry

    far_teams = (unit // team - 1, unit // team // 2 - 1)
    lax.fori_loop(0, unit // team // 2, deal_out, 0)
    swap.keep_own()
    passed(swap.me).start()
    load.wait()

    def keep(packs, carry):
        dealt(g_ref, packs, dealt_g)
        return carry

    lax.fori_loop(0, unit // team, keep, 0)
    swap.peers(pass_on)
    swap.peers(swap.wait_sent)

    def end(pack, carry):
        passed(pack).wait_recv()
        passed(pack).wait_send()
        return carry

    lax.fori_loop(0, unit, end, 0)


def deal(x, g, table, unit, half, ident):
    total, width = x.shape
    smem = pl.BlockSpec(memory_space=pltpu.SMEM)
    vmem = pl.BlockSpec(memory_space=pltpu.VMEM)
    return pl.pallas_call(
        functools.partial(deal_kernel, unit, half),
        in_specs=[smem, vmem, pl.BlockSpec(memory_space=pl.ANY)],
        out_specs=[vmem, vmem, vmem],
        out_shape=[jax.ShapeDtypeStruct((total // 2, width), BF)] * 3,
        scratch_shapes=[
            pltpu.VMEM((total // 2, width), BF),
            pltpu.VMEM((total, width), BF),
            pltpu.SemaphoreType.DMA,
            *[pltpu.SemaphoreType.DMA((unit,))] * 4,
        ],
        compiler_params=pltpu.CompilerParams(
            vmem_limit_bytes=ROOM, collective_id=ident, has_side_effects=True
        ),
        cost_estimate=pl.CostEstimate(
            flops=8 * total * width * half, bytes_accessed=40 * total * width, transcendentals=0
        ),
        name="deal",
    )(table, x, g)


def undeal_kernel(unit, half, lengths, dealing, core, own_ref, sib_ref, o_ref, starts):
    total = o_ref.shape[0]
    unit_starts(lengths, starts, unit)
    wide = half + 16
    row = lax.broadcasted_iota(jnp.int32, (2 * wide, half), 0)
    col = lax.broadcasted_iota(jnp.int32, (2 * wide, half), 1)
    o_ref[...] = jnp.zeros_like(o_ref)

    def one(pack, carry):
        for part, ref in ((core[0], own_ref), (1 - core[0], sib_ref)):
            first = part * half
            units_a, shift_a, shift_b, (base_a, base_b) = pack_windows(
                lengths, dealing, starts, unit, pack, first, half, total
            )
            slot = first + col
            near = slot < units_a
            at = jnp.where(near, slot + (shift_a - base_a), slot + (shift_b - base_b + wide))
            pick = (row == at) & (near == (row < wide))
            rows = ref[pl.ds(pl.multiple_of(pack * half, 16), half), :]
            both = dot(pick.astype(F32).astype(BF), rows).astype(BF)
            o_ref[pl.ds(base_a, wide), :] += both[:wide]
            o_ref[pl.ds(base_b, wide), :] += both[wide:]
        return carry

    lax.fori_loop(0, total // (2 * half), one, 0, unroll=8)


def undeal(own, sib, lengths, dealing, core, unit, half):
    total, width = 2 * own.shape[0], own.shape[1]
    smem = pl.BlockSpec(memory_space=pltpu.SMEM)
    vmem = pl.BlockSpec(memory_space=pltpu.VMEM)
    return pl.pallas_call(
        functools.partial(undeal_kernel, unit, half),
        in_specs=[smem, smem, smem, vmem, vmem],
        out_specs=vmem,
        out_shape=jax.ShapeDtypeStruct((total, width), BF),
        scratch_shapes=[pltpu.SMEM(lengths.shape, jnp.int32)],
        compiler_params=pltpu.CompilerParams(vmem_limit_bytes=ROOM),
        cost_estimate=pl.CostEstimate(
            flops=8 * total * width * half, bytes_accessed=4 * total * width, transcendentals=0
        ),
        name="undeal",
    )(lengths, dealing, core, own, sib)


def fwd_kernel(
    ck, unit, half, x_own, x_sib, w_ref, b_ref, kx_ref, qx_ref, dealt_g,
    q_ref, k_ref, v_ref, c_ref, c_other_out, c32_ref, lse_ref, got_g_out,
    kext, vt, c_sib, c_other, got_g, send_sem, recv_sem, pass_sem, take_sem,
):
    n = k_ref.shape[0]
    pair = pl.program_id(0)
    swap = PackExchange(unit, half, dealt_g, got_g, send_sem, recv_sem)

    def passed(pair):
        cols = pl.ds(pl.multiple_of(pair * 128, 128), 128)
        return to_sibling(
            c_sib.at[:, cols], c_other.at[:, cols], pass_sem.at[pair], take_sem.at[pair]
        )

    @pl.when(pair == 0)
    def _():
        greet(unit)
        swap.peers(swap.send)
        swap.keep_own()

    w = jnp.concatenate([w_ref[0], w_ref[1], w_ref[2]], axis=1)
    bias = jnp.concatenate([b_ref[0:1], jnp.zeros((1, 128), F32), b_ref[1:2]], axis=1)
    for part, x_ref in enumerate((x_own, x_sib)):
        for first in range(0, n // 2, 512):
            made = (dot(x_ref[first : first + 512], w) + bias).astype(BF)
            at = slice(part * n // 2 + first, part * n // 2 + first + 512)
            for j, ref in enumerate((q_ref, k_ref, v_ref)):
                ref[at] = made[:, 128 * j : 128 * j + 128]
    kext[:, :128] = k_ref[...]
    kext[:, 128:] = kx_ref[...]
    v_t = v_ref[...].T
    ones = jnp.where(lax.broadcasted_iota(jnp.int32, (EXTRA, n), 0) == 0, 1.0, 0.0).astype(BF)
    for h in range(2):
        vt[h, :HD] = v_t[HD * h : HD * h + HD]
        vt[h, HD:] = ones
    q_t = (q_ref[...] * BF(HD**-0.5)).T
    zero = jnp.zeros((HD, n), BF)
    qx = qx_ref[...]
    q_ext = [
        jnp.concatenate([q_t[:HD], zero, qx], axis=0),
        jnp.concatenate([zero, q_t[HD:], qx], axis=0),
    ]
    tops, sums = [None, None], [None, None]
    for first in range(0, n, ck):
        keys = slice(first, first + ck)
        for h in range(2):
            s = dot(kext[keys, : 128 + EXTRA], q_ext[h])
            top = jnp.max(s, axis=0, keepdims=True)
            if first:
                top = jnp.maximum(tops[h], top)
            part = dot(vt[h, :, keys], jnp.exp(s - top).astype(BF))
            if first:
                part = part + sums[h] * jnp.exp(tops[h] - top)
            tops[h], sums[h] = top, part
    outs = []
    for h in range(2):
        total = sums[h][HD : HD + 1]
        outs.append(sums[h][:HD] / total)
        lse_ref[0, h : h + 1] = tops[h] + jnp.log(total)
    c = jnp.concatenate(outs, axis=0).T
    c32_ref[...] = c
    c_ref[...] = c[: n // 2].astype(BF)
    c_sib[:, pl.ds(pl.multiple_of(pair * 128, 128), 128)] = c[n // 2 :].astype(BF)
    passed(pair).start()

    @pl.when(pair == pl.num_programs(0) - 1)
    def _():
        swap.peers(swap.wait_from)
        swap.peers(swap.wait_sent)

        def end(pair, carry):
            passed(pair).wait_recv()
            passed(pair).wait_send()
            return carry

        lax.fori_loop(0, pl.num_programs(0), end, 0)
        c_other_out[...] = c_other[...]
        got_g_out[...] = got_g[...]


def attn_cost(n, width, products):
    return pl.CostEstimate(
        flops=products * 2 * 4 * n * n * width,
        bytes_accessed=16 * n * width,
        transcendentals=n * n * width // HD,
    )


def attn_fwd(x_own, x_sib, w, b, kx, qx, dealt_g, unit, half, ident, ck=512):
    n, model = 2 * x_own.shape[0], x_own.shape[1]
    width = w.shape[2]
    pairs = width // 128
    keys = pl.BlockSpec((n, 128), lambda p: (0, p))

    def whole(shape):
        return pl.BlockSpec(shape, lambda p: (0, 0), pipeline_mode=pl.Buffered(1))

    return pl.pallas_call(
        functools.partial(fwd_kernel, ck, unit, half),
        grid=(pairs,),
        in_specs=[
            whole(x_own.shape),
            whole(x_sib.shape),
            pl.BlockSpec((3, model, 128), lambda p: (0, 0, p)),
            pl.BlockSpec((2, 128), lambda p: (0, p)),
            whole(kx.shape),
            whole(qx.shape),
            whole(dealt_g.shape),
        ],
        out_specs=[
            keys,
            keys,
            keys,
            pl.BlockSpec((n // 2, 128), lambda p: (0, p)),
            whole((n // 2, width)),
            keys,
            pl.BlockSpec((1, 2, n), lambda p: (p, 0, 0)),
            whole(dealt_g.shape),
        ],
        out_shape=[jax.ShapeDtypeStruct((n, width), BF)] * 3
        + [jax.ShapeDtypeStruct((n // 2, width), BF)] * 2
        + [
            jax.ShapeDtypeStruct((n, width), F32),
            jax.ShapeDtypeStruct((pairs, 2, n), F32),
            jax.ShapeDtypeStruct(dealt_g.shape, BF),
        ],
        scratch_shapes=[
            pltpu.VMEM((n, 256), BF),
            pltpu.VMEM((2, HD + EXTRA, n), BF),
            pltpu.VMEM((n // 2, width), BF),
            pltpu.VMEM((n // 2, width), BF),
            pltpu.VMEM(dealt_g.shape, BF),
            *[pltpu.SemaphoreType.DMA((unit,))] * 2,
            *[pltpu.SemaphoreType.DMA((pairs,))] * 2,
        ],
        compiler_params=pltpu.CompilerParams(
            vmem_limit_bytes=ROOM, collective_id=ident, has_side_effects=True
        ),
        cost_estimate=attn_cost(n, width, 2),
        name="attn_fwd",
    )(x_own, x_sib, w, b, kx, qx, dealt_g)


def split3(x):
    high = x.astype(BF)
    rest = x - high.astype(F32)
    middle = rest.astype(BF)
    return high, middle, (rest - middle.astype(F32)).astype(BF)


def bit_orders(bits):
    first = list(range(bits))
    second = [1, 2, 0] + list(range(3, bits))
    third = [2, 0, 1] + list(range(3, bits))
    return first, second, third


def row_unit(devices):
    return 8 * devices


def cut_rows(rows, devices):
    unit = row_unit(devices)
    units = rows // unit
    counts = [(units + 2) // 3, (units + 1) // 3, units // 3]
    starts = [0, counts[0], counts[0] + counts[1]]
    return [(s * unit, c * unit) for s, c in zip(starts, counts) if c]


def greet_partners(bits):
    me = lax.axis_index("dp")
    barrier = pltpu.get_barrier_semaphore()
    for bit in range(bits):
        pl.semaphore_signal(
            barrier,
            inc=1,
            device_id={"dp": me + (1 - 2 * (me // 2**bit % 2)) * 2**bit},
            device_id_type=pl.DeviceIdType.MESH,
        )
    pl.semaphore_wait(barrier, bits)


class PackSum:
    def __init__(self, devices, big, small, out, came, acc, inbox, small_box, send_sem, recv_sem):
        self.came = came
        self.bits = devices.bit_length() - 1
        self.me = lax.axis_index("dp")
        self.big, self.small, self.acc, self.inbox, self.out = big, small, acc, inbox, out
        self.small_box = small_box
        self.send_sem, self.recv_sem = send_sem, recv_sem
        self.parts = [
            (start, count, order)
            for (start, count), order in zip(cut_rows(big.shape[0], devices), bit_orders(self.bits))
        ]
        self.steps = 2 * self.bits

    def slots(self, first, slot_us, last):
        size = 4e-3 * self.big.shape[0] * self.big.shape[1]
        sizes = [size / 2 ** (level + 1) / 3 for level in range(self.bits - 1)]
        sizes = sizes + [size / 2 ** (self.bits - 2)] + sizes[::-1]
        at, out = 0.0, []
        for step in range(self.steps):
            out.append(min(last, first + math.ceil(at / slot_us)))
            if step < len(sizes) and not (step == 0 and self.came):
                at += 4.5 + sizes[step] / 80
        return out

    @staticmethod
    def scratch(rows, cols, small_shape, devices):
        bits = devices.bit_length() - 1
        return [
            pltpu.VMEM((rows // 2, cols), BF),
            pltpu.VMEM((rows, cols), BF),
            pltpu.VMEM((2 * bits + 1,) + small_shape, F32),
            pltpu.SemaphoreType.DMA((4, 2 * bits)),
            pltpu.SemaphoreType.DMA((4, 2 * bits)),
        ]

    def side(self, bit):
        return (self.me // 2**bit) % 2

    def partner(self, bit):
        return self.me + (1 - 2 * self.side(bit)) * 2**bit

    def region(self, part, level):
        start, count, order = self.parts[part]
        for done in range(level):
            start = start + self.side(order[done]) * (count // 2 ** (done + 1))
        return start, count // 2**level

    def halved(self, part, start):
        return self.parts[part][0] // 2 + start - self.region(part, 1)[0]

    def rows(self, ref, start, count):
        return ref.at[pl.ds(pl.multiple_of(start, 16), count)]

    def slot(self, part, level):
        start, count, _ = self.parts[part]
        return start + count - count // 2**level

    def sending(self, part, level):
        start, count = self.region(part, level)
        bit = self.parts[part][2][level]
        if level < self.bits - 1:
            count = count // 2
            start = start + (1 - self.side(bit)) * count
        return pltpu.make_async_remote_copy(
            src_ref=self.rows(self.acc, self.halved(part, start), count)
            if level
            else self.rows(self.big, start, count),
            dst_ref=self.inbox.at[pl.ds(self.slot(part, level), count)],
            send_sem=self.send_sem.at[part, level],
            recv_sem=self.recv_sem.at[part, level],
            device_id={"dp": self.partner(bit)},
            device_id_type=pl.DeviceIdType.MESH,
        )

    def doubling(self, part, level):
        mine = self.rows(self.out, *self.region(part, level + 1))
        return pltpu.make_async_remote_copy(
            src_ref=mine,
            dst_ref=mine,
            send_sem=self.send_sem.at[part, self.bits + level],
            recv_sem=self.recv_sem.at[part, self.bits + level],
            device_id={"dp": self.partner(self.parts[part][2][level])},
            device_id_type=pl.DeviceIdType.MESH,
        )

    def exchange(self, level):
        return pltpu.make_async_remote_copy(
            src_ref=self.small if level == 0 else self.small_box.at[self.bits + level],
            dst_ref=self.small_box.at[level],
            send_sem=self.send_sem.at[3, level],
            recv_sem=self.recv_sem.at[3, level],
            device_id={"dp": self.partner(level)},
            device_id_type=pl.DeviceIdType.MESH,
        )

    def add(self, part, level):
        last = level == self.bits - 1
        kept, count = self.region(part, level if last else level + 1)
        source, first = (self.acc, self.halved(part, kept)) if level else (self.big, kept)
        if last:
            target, goal = self.out, kept
        else:
            target, goal = self.acc, self.halved(part, kept)
        slot, box = self.slot(part, level), self.inbox
        if self.came and level == 0:
            slot, box = 0, self.came[part]
        tile = math.gcd(count, 64)

        def one(i, carry):
            def at(start):
                return pl.ds(pl.multiple_of(start + i * tile, 16), tile)

            total = source[at(first), :].astype(F32) + box[at(slot), :].astype(F32)
            target[at(goal), :] = total.astype(BF)
            return carry

        lax.fori_loop(0, count // tile, one, 0)

    def step(self, k):
        bits = self.bits
        for part in range(len(self.parts)):
            if 0 < k <= bits:
                if not (self.came and k == 1):
                    self.sending(part, k - 1).wait_recv()
                self.add(part, k - 1)
            elif k > bits:
                self.doubling(part, 2 * bits - 1 - k).wait_recv()
            if k < bits:
                self.sending(part, k).start()
            elif k < self.steps - 1:
                self.doubling(part, 2 * bits - 2 - k).start()
        if self.small is not None:
            if 0 < k <= bits:
                self.exchange(k - 1).wait_recv()
                held = self.small[...] if k == 1 else self.small_box[bits + k - 1]
                self.small_box[bits + k] = held + self.small_box[k - 1]
            if k < bits:
                self.exchange(k).start()
        if k == self.steps - 1:
            for part in range(len(self.parts)):
                for level in range(1 if self.came else 0, bits):
                    self.sending(part, level).wait_send()
                for level in range(bits - 1):
                    self.doubling(part, level).wait_send()
            if self.small is not None:
                for level in range(bits):
                    self.exchange(level).wait_send()


SLOT_US = 3.6


def bwd_kernel(
    ck, devices, turns, q_ref, k_ref, v_ref, g_own_ref, g_sib_ref, c32_ref, lse_ref, kx_ref, qx_ref,
    x_own, x_sib, w_ref, big_a, big_b, small, *refs,
):
    i = pl.program_id(1)
    n = k_ref.shape[0]
    bq = q_ref.shape[0]
    count = len(cut_rows(big_a.shape[0], devices))
    came, refs = refs[:count], refs[count:]
    dx_ref, dx_sib_ref, dw_ref, db_ref, small_out, out_a, out_up, out_last = refs[:8]
    kext, vext, kt, x_t, dq_acc, dk_acc, dv_acc, dx_sib, sum_a, sum_b, *comm_refs = refs[8:]
    comm_a = PackSum(devices, big_a, None, sum_a, came, *comm_refs[:5])
    comm_b = PackSum(devices, big_b, small, sum_b, None, *comm_refs[5:])
    turn = pl.program_id(0) * pl.num_programs(1) + i
    per_turn = n // ck
    slots = turns * per_turn
    slots_a = comm_a.slots(0, SLOT_US, slots)
    slots_b = comm_b.slots(0, SLOT_US, slots)

    def comm_at(which):
        for comm, at in ((comm_a, slots_a), (comm_b, slots_b)):
            for step, slot in enumerate(at):
                if step == 0 and comm.came:
                    continue
                if slot < slots and slot % per_turn == which:

                    @pl.when(turn == slot // per_turn)
                    def _(comm=comm, step=step):
                        comm.step(step)

                elif slot == slots and which is None:
                    comm.step(step)

    @pl.when(turn == 0)
    def _():
        greet_partners(comm_a.bits)

    @pl.when(i == 0)
    def _():
        kext[:, :128] = k_ref[...]
        kext[:, 128:] = kx_ref[...]
        vext[:, :128] = v_ref[...]
        lane = lax.broadcasted_iota(jnp.int32, (n, 128), 1)
        vext[:, 128:] = jnp.where((lane >= 2) & (lane < 5), -1.0, 0.0).astype(BF)
        kt[...] = k_ref[...].T
        dk_acc[...] = jnp.zeros_like(dk_acc)
        dv_acc[...] = jnp.zeros_like(dv_acc)

    q = q_ref[...] * BF(HD**-0.5)
    g = jnp.where(i == 0, g_own_ref[...], g_sib_ref[...])
    q_t, g_t = q.T, g.T
    prod_t = (g.astype(F32) * c32_ref[...]).T
    zero = jnp.zeros((HD, bq), BF)
    lane = lax.broadcasted_iota(jnp.int32, (bq, 128), 1)
    row = lax.broadcasted_iota(jnp.int32, (EXTRA, bq), 0)
    qx = qx_ref[...].astype(F32)

    def with_rows(base, parts):
        for j, part in enumerate(parts):
            base = jnp.where(row == 2 + j, part.astype(F32), base)
        return base.astype(BF)

    q_ext, g_ext, q_own, g_own, dq_t = [], [], [], [], []
    for h in range(2):
        mine = slice(HD * h, HD * h + HD)
        delta = jnp.sum(prod_t[mine], axis=0, keepdims=True)
        q_rows = with_rows(qx, split3(lse_ref[0, h : h + 1]))
        g_rows = with_rows(jnp.zeros((EXTRA, bq), F32), split3(delta))
        for out, turned, extra in ((q_ext, q_t, q_rows), (g_ext, g_t, g_rows)):
            both = [turned[mine], zero] if h == 0 else [zero, turned[mine]]
            out.append(jnp.concatenate(both + [extra], axis=0))
        ours = (lane < HD) if h == 0 else (lane >= HD)
        q_own.append(jnp.where(ours, q, BF(0)))
        g_own.append(jnp.where(ours, g, BF(0)))
        dq_t.append(jnp.zeros((HD, bq), F32))
    for first in range(0, n, ck):
        comm_at(first // ck)
        keys = slice(first, first + ck)
        dv = jnp.zeros((ck, 128), F32)
        dk = jnp.zeros((ck, 128), F32)
        for h in range(2):
            p = jnp.exp(dot(kext[keys, : 128 + EXTRA], q_ext[h]))
            ds = (p * dot(vext[keys, : 128 + EXTRA], g_ext[h])).astype(BF)
            dv = dv + dot(p.astype(BF), g_own[h])
            dk = dk + dot(ds, q_own[h])
            dq_t[h] = dq_t[h] + dot(kt[HD * h : HD * h + HD, keys], ds)
        dv_acc[keys] += dv
        dk_acc[keys] += dk
    dq = jnp.concatenate(dq_t, axis=0).T * HD**-0.5
    dq_acc[pl.ds(pl.multiple_of(i * bq, bq), bq)] = dq.astype(BF)

    @pl.when(turn == 0)
    def _():
        x_t[:, : n // 2] = x_own[...].T
        x_t[:, n // 2 :] = x_sib[...].T
        dx_ref[...] = jnp.zeros_like(dx_ref)
        dx_sib[...] = jnp.zeros_like(dx_sib)

    @pl.when(i == pl.num_programs(1) - 1)
    def _():
        width = x_own.shape[1]
        grads = [dq_acc[...], dk_acc[...].astype(BF), dv_acc[...].astype(BF)]
        joined = jnp.concatenate(grads, axis=1)
        made = dot(x_t[...], joined).astype(BF)
        for j in range(3):
            dw_ref[j * width : (j + 1) * width] = made[:, 128 * j : 128 * j + 128]
        bias = [jnp.sum(grad.astype(F32), axis=0, keepdims=True) for grad in grads[::2]]
        db_ref[...] = jnp.concatenate(bias + [jnp.zeros((6, 128), F32)], axis=0)
        tile = 512
        planes = jnp.concatenate([w_ref[j] for j in range(3)], axis=1)
        for first in range(0, n, tile):
            to_x = dot(joined[first : first + tile], planes, ((1,), (1,)))
            target, goal = (dx_ref, first) if first < n // 2 else (dx_sib, first - n // 2)
            target[goal : goal + tile] += to_x

    @pl.when(turn == turns - 1)
    def _():
        comm_at(None)
        dx_sib_ref[...] = dx_sib[...].astype(BF)
        out_a[...] = sum_a[...]
        tall, across = out_up.shape
        for start in range(0, across, tall):
            out_up[:, start : start + tall] = sum_b[start : start + tall]
        out_last[...] = sum_b[across : across + out_last.shape[0]]
        small_out[...] = comm_b.small_box[2 * comm_b.bits]


def attn_bwd(q, k, v, g_own_rows, g_sib_rows, c32, lse, kx, qx, x_own, x_sib, w, big_a, big_b, small, came, shard, devices, ident, ck=512):
    n, width = q.shape
    bq = n // 2
    pairs = width // 128
    model = x_own.shape[1]
    rows = pl.BlockSpec((bq, 128), lambda p, i: (i, p))
    keys = pl.BlockSpec((n, 128), lambda p, i: (0, p))
    def whole(shape):
        return pl.BlockSpec(shape, lambda p, i: (0, 0), pipeline_mode=pl.Buffered(1))

    return pl.pallas_call(
        functools.partial(bwd_kernel, ck, devices, pairs * (n // bq)),
        grid=(pairs, n // bq),
        in_specs=[
            rows,
            keys,
            keys,
            pl.BlockSpec((bq, 128), lambda p, i: (0, p)),
            pl.BlockSpec((bq, 128), lambda p, i: (0, p)),
            rows,
            pl.BlockSpec((1, 2, bq), lambda p, i: (p, 0, i)),
            pl.BlockSpec((n, 128), lambda p, i: (0, 0)),
            pl.BlockSpec((EXTRA, bq), lambda p, i: (0, i)),
            whole(x_own.shape),
            whole(x_sib.shape),
            pl.BlockSpec((3, model, 128), lambda p, i: (0, 0, p)),
            whole(big_a.shape),
            whole(big_b.shape),
            whole(small.shape),
            *[whole(box.shape) for box in came],
        ],
        out_specs=[
            whole((n // 2, model)),
            whole((n // 2, model)),
            pl.BlockSpec((3 * model, 128), lambda p, i: (0, p)),
            pl.BlockSpec((8, 128), lambda p, i: (0, p)),
            whole(small.shape),
            whole(big_a.shape),
            whole((model, shard)),
            whole((width, model)),
        ],
        out_shape=[
            jax.ShapeDtypeStruct((n // 2, model), F32),
            jax.ShapeDtypeStruct((n // 2, model), BF),
            jax.ShapeDtypeStruct((3 * model, width), BF),
            jax.ShapeDtypeStruct((8, width), F32),
            jax.ShapeDtypeStruct(small.shape, F32),
            jax.ShapeDtypeStruct(big_a.shape, BF),
            jax.ShapeDtypeStruct((model, shard), BF),
            jax.ShapeDtypeStruct((width, model), BF),
        ],
        scratch_shapes=[
            pltpu.VMEM((n, 256), BF),
            pltpu.VMEM((n, 256), BF),
            pltpu.VMEM((128, n), BF),
            pltpu.VMEM((model, n), BF),
            pltpu.VMEM((n, 128), BF),
            pltpu.VMEM((n, 128), F32),
            pltpu.VMEM((n, 128), F32),
            pltpu.VMEM((n // 2, model), F32),
            pltpu.VMEM(big_a.shape, BF),
            pltpu.VMEM(big_b.shape, BF),
            *PackSum.scratch(*big_a.shape, (8, 128), devices),
            *PackSum.scratch(*big_b.shape, small.shape, devices),
        ],
        compiler_params=pltpu.CompilerParams(
            vmem_limit_bytes=60 * 2**20, collective_id=ident, has_side_effects=True
        ),
        cost_estimate=attn_cost(n, width, 5),
        name="attn_bwd",
    )(q, k, v, g_own_rows, g_sib_rows, c32, lse, kx, qx, x_own, x_sib, w, big_a, big_b, small, *came)


def norm_parts(field, gain, shift):
    center = field - jnp.mean(field, axis=-1, keepdims=True)
    inv_std = lax.rsqrt(jnp.mean(center * center, axis=-1, keepdims=True) + NORM_EPSILON)
    normed = center * inv_std
    return normed * gain + shift, normed, inv_std


def norm_back(incoming, normed, inv_std, gain):
    scaled = incoming * gain
    return inv_std * (
        scaled
        - jnp.mean(scaled, axis=-1, keepdims=True)
        - normed * jnp.mean(scaled * normed, axis=-1, keepdims=True)
    )


FF_ROWS = 256


def ff_kernel(
    unit, half, x_ref, c_own, c_sib, g_ref, out_own, out_sib, up_own, up_sib, down_own, down_sib,
    vec_ref, bias_own, bias_sib,
    h1_ref, dc_own, dc_sib, vec_out, bias_out, got_own_out, got_sib_out, down_out, up_out, down_sib_out, up_sib_out,
    z, got, got_sib, slope, act, du, low_all, branch_all, da_all, mine, theirs,
    send_sem, recv_sem, pass_sem, take_sem, out_sem, keep_sem,
):
    i = pl.program_id(0)
    blocks = pl.num_programs(0)
    swap = PackExchange(unit, half, z, got, send_sem, recv_sem)
    team = FF_ROWS // half
    block = ff_block(i, unit, half, z.shape[0] // FF_ROWS)

    def passed(pack):
        return to_sibling(
            swap.rows(got, pack), swap.rows(got_sib, pack), pass_sem.at[pack], take_sem.at[pack]
        )

    @pl.when(i == 0)
    def _():
        greet(unit)
        vec_out[...] = jnp.zeros_like(vec_out)
        bias_out[...] = jnp.zeros_like(bias_out)

    out_bias, first_gain, first_shift, down_bias, second_gain, second_shift = (
        vec_ref[j : j + 1] for j in range(6)
    )
    here = pl.ds(pl.multiple_of(block * FF_ROWS, 16), FF_ROWS)
    attention = dot(c_own[here, :], out_own[...]) + dot(c_sib[here, :], out_sib[...])
    first, first_normed, first_inv = norm_parts(
        x_ref[...].astype(F32) + attention + out_bias, first_gain, first_shift
    )
    low = first.astype(BF)
    low_all[here, :] = low
    shard = up_own.shape[1]
    wide = 512
    sides = ((up_own, down_own, bias_own), (up_sib, down_sib, bias_sib))
    down = jnp.zeros(first.shape, F32)
    for side, (up, back, bias) in enumerate(sides):
        for start in range(0, shard, wide):
            cols = slice(start, start + wide)
            at = slice(side * shard + start, side * shard + start + wide)
            upward = dot(low, up[:, cols]) + bias[:, cols]
            cumulative = 0.5 + 0.5 * lax.erf(upward * math.sqrt(0.5))
            density = jnp.exp(-0.5 * upward * upward) * (1.0 / math.sqrt(2.0 * math.pi))
            active = (upward * cumulative).astype(BF)
            act[here, at] = active
            slope[:, at] = cumulative + upward * density
            down = down + dot(active, back[cols])
    second, second_normed, second_inv = norm_parts(
        first + down + down_bias, second_gain, second_shift
    )
    z[here, :] = second.astype(BF)

    def send(j, carry):
        pack = block * team + j

        @pl.when(pack != swap.me)
        def _():
            swap.send(pack)

        return carry

    lax.fori_loop(0, team, send, 0)
    outer = g_ref[...].astype(F32)
    grad_h2 = norm_back(outer, second_normed, second_inv, second_gain)
    branch = grad_h2.astype(BF)
    branch_all[here, :] = branch
    grad_y1 = grad_h2
    for side, (up, back, _) in enumerate(sides):
        for start in range(0, shard, wide):
            cols = slice(start, start + wide)
            at = slice(side * shard + start, side * shard + start + wide)
            inner = (dot(branch, back[cols], ((1,), (1,))) * slope[:, at]).astype(BF)
            du[here, at] = inner
            bias_out[side : side + 1, cols] += jnp.sum(inner.astype(F32), axis=0, keepdims=True)
            grad_y1 = grad_y1 + dot(inner, up[:, cols], ((1,), (1,)))
    grad_h1 = norm_back(grad_y1, first_normed, first_inv, first_gain)
    h1_ref[...] = grad_h1
    da = grad_h1.astype(BF)
    da_all[here, :] = da
    dc_own[...] = dot(da, out_own[...], ((1,), (1,))).astype(BF)
    dc_sib[...] = dot(da, out_sib[...], ((1,), (1,))).astype(BF)
    terms = (
        grad_h1, grad_y1 * first_normed, grad_y1, grad_h2, outer * second_normed, outer,
    )
    for j, term in enumerate(terms):
        vec_out[j : j + 1] += jnp.sum(term, axis=0, keepdims=True)

    model = z.shape[1]
    pieces = [
        (start, wide, lambda side, start=start: dot(
            act[:, side * shard + start : side * shard + start + wide], branch_all[...], OVER_ROWS
        ))
        for start in range(0, shard, wide)
    ] + [
        (shard + start, model, lambda side, start=start: dot(
            low_all[...], du[:, side * shard + start : side * shard + start + model], OVER_ROWS
        ))
        for start in range(0, shard, model)
    ] + [
        (2 * shard, c_own.shape[1], lambda side: dot(
            (c_sib if side else c_own)[...], da_all[...], OVER_ROWS
        ))
    ]

    def put(j, side):
        start, size, _ = pieces[j]
        source = theirs if side else mine
        down, up = (down_sib_out, up_sib_out) if side else (down_out, up_out)
        target, goal = (down, start) if start < shard else (up, start - shard)
        return pltpu.make_async_copy(
            source.at[pl.ds(start, size)], target.at[pl.ds(goal, size)], out_sem.at[side, j]
        )

    @pl.when(i == blocks - 1)
    def _():
        swap.keep_own()
        passed(swap.me).start()
        for side, kept in ((1, theirs), (0, mine)):
            for j, (start, size, product) in enumerate(pieces):
                kept[start : start + size] = product(side).astype(BF)
                put(j, side).start()

        def pass_on(pack):
            swap.wait_from(pack)
            passed(pack).start()

        swap.peers(pass_on)
        swap.peers(swap.wait_sent)

        def end(pack, carry):
            passed(pack).wait()
            return carry

        lax.fori_loop(0, unit, end, 0)
        keep_own = pltpu.make_async_copy(got, got_own_out, keep_sem.at[0])
        keep_sib = pltpu.make_async_copy(got_sib, got_sib_out, keep_sem.at[1])
        keep_own.start()
        keep_sib.start()
        for j in range(len(pieces)):
            put(j, 0).wait()
            put(j, 1).wait()
        keep_own.wait()
        keep_sib.wait()


OVER_ROWS = ((0,), (0,))


def ff_block(i, unit, half, blocks):
    home = lax.axis_index("dp") // (FF_ROWS // half)
    return PackExchange.across(home, blocks - 1 - i, blocks)


def feed_forward(x, c_own, c_sib, g, weights, vectors, bias_own, bias_sib, unit, half, ident):
    n, model = x.shape
    shard = bias_own.shape[1]
    width = c_own.shape[1]
    blocks = n // FF_ROWS

    def rows(cols):
        return pl.BlockSpec((FF_ROWS, cols), lambda i: (ff_block(i, unit, half, blocks), 0))

    def whole(shape):
        return pl.BlockSpec(shape, lambda i: (0, 0), pipeline_mode=pl.Buffered(1))

    shapes = [(model, F32), (width, BF), (width, BF)]
    kept = [(vectors.shape, F32), ((8, shard), F32)]
    shares = 2 * shard + width
    count = shard // 512 + shard // model + 1
    put = [(n, model)] * 2 + [(shard, model), (shares - shard, model)] * 2
    return pl.pallas_call(
        functools.partial(ff_kernel, unit, half),
        grid=(blocks,),
        in_specs=[rows(model), whole(c_own.shape), whole(c_sib.shape), rows(model)]
        + [whole(w.shape) for w in weights]
        + [whole(vectors.shape), whole(bias_own.shape), whole(bias_sib.shape)],
        out_specs=[rows(cols) for cols, _ in shapes]
        + [whole(shape) for shape, _ in kept]
        + [pl.BlockSpec(memory_space=pl.ANY)] * len(put),
        out_shape=[jax.ShapeDtypeStruct((n, cols), dtype) for cols, dtype in shapes]
        + [jax.ShapeDtypeStruct(shape, dtype) for shape, dtype in kept]
        + [jax.ShapeDtypeStruct(shape, BF) for shape in put],
        scratch_shapes=[
            pltpu.VMEM((n, model), BF),
            pltpu.VMEM((n, model), BF),
            pltpu.VMEM((n, model), BF),
            pltpu.VMEM((FF_ROWS, 2 * shard), F32),
            pltpu.VMEM((n, 2 * shard), BF),
            pltpu.VMEM((n, 2 * shard), BF),
            *[pltpu.VMEM((n, model), BF)] * 3,
            pltpu.VMEM((shares, model), BF),
            pltpu.VMEM((shares, model), BF),
            *[pltpu.SemaphoreType.DMA((unit,))] * 4,
            pltpu.SemaphoreType.DMA((2, count)),
            pltpu.SemaphoreType.DMA((2,)),
        ],
        compiler_params=pltpu.CompilerParams(
            vmem_limit_bytes=62 * 2**20, collective_id=ident, has_side_effects=True
        ),
        cost_estimate=pl.CostEstimate(
            flops=8 * n * model * (width + shard) * 2,
            bytes_accessed=40 * n * model,
            transcendentals=4 * n * shard,
        ),
        name="feed_forward",
    )(x, c_own, c_sib, g, *weights, vectors, bias_own, bias_sib)


def tail_kernel(
    unit, half, h1_ref, dx_ref, dx_sib, big, small, own_ref, sib_ref, big_out, small_out,
    outbox, dx_came, mix_sem, mixed_sem, send_sem, recv_sem, pass_sem, take_sem, *comm_refs,
):
    comm = PackSum(unit, big, small, big_out, None, *comm_refs)
    swap = PackExchange(unit, half, outbox, own_ref, send_sem, recv_sem)

    def mix(pack):
        return to_sibling(
            swap.rows(dx_sib, pack),
            swap.rows(dx_came, pack),
            mix_sem.at[pack],
            mixed_sem.at[pack],
        )

    def passed(pack):
        return to_sibling(
            swap.rows(own_ref, pack), swap.rows(sib_ref, pack), pass_sem.at[pack], take_sem.at[pack]
        )

    def add_up(pack):
        mix(pack).wait_recv()
        at = swap.rows(dx_came, pack)[...].astype(F32)
        total = swap.rows(h1_ref, pack)[...] + swap.rows(dx_ref, pack)[...] + at
        swap.rows(outbox, pack)[...] = total.astype(BF)

    def add_and_send(pack):
        add_up(pack)
        swap.send(pack)

    def pass_on(pack):
        swap.wait_from(pack)
        passed(pack).start()

    greet(unit)
    swap.peers(lambda pack: mix(pack).start())
    mix(swap.me).start()
    comm.step(0)
    share = -(-(unit - 1) // 5)
    for k in range(1, 6):
        swap.peers(add_and_send, (k - 1) * share, min(k * share, unit - 1))
        comm.step(k)
    add_up(swap.me)
    swap.keep_own()
    passed(swap.me).start()
    early = (unit - 1) * 2 // 3
    swap.peers(pass_on, 0, early)
    for k in range(6, comm.steps):
        comm.step(k)
    small_out[...] = comm.small_box[2 * comm.bits]
    swap.peers(pass_on, early)
    swap.peers(swap.wait_sent)

    def end(pack, carry):
        mix(pack).wait_send()
        passed(pack).wait()
        return carry

    lax.fori_loop(0, unit, end, 0)


def tail(h1, dx, dx_sib, big, small, unit, half, ident):
    vmem = pl.BlockSpec(memory_space=pltpu.VMEM)
    kept = [jax.ShapeDtypeStruct(dx_sib.shape, BF)] * 2
    out_shape = kept + [
        jax.ShapeDtypeStruct(big.shape, BF),
        jax.ShapeDtypeStruct(small.shape, F32),
    ]
    return pl.pallas_call(
        functools.partial(tail_kernel, unit, half),
        in_specs=[vmem] * 5,
        out_specs=[vmem] * len(out_shape),
        out_shape=out_shape,
        scratch_shapes=[
            pltpu.VMEM(dx_sib.shape, BF),
            pltpu.VMEM(dx_sib.shape, BF),
            *[pltpu.SemaphoreType.DMA((unit,))] * 6,
            *PackSum.scratch(*big.shape, small.shape, unit),
        ],
        compiler_params=pltpu.CompilerParams(
            vmem_limit_bytes=ROOM, collective_id=ident, has_side_effects=True
        ),
        cost_estimate=pl.CostEstimate(flops=0, bytes_accessed=200 * big.size, transcendentals=0),
        name="tail",
    )(h1, dx, dx_sib, big, small)


def over_rows(first_op, second_op):
    return dot(first_op, second_op, ((0,), (0,)))


def over_cols(first_op, second_op):
    return dot(first_op, second_op, ((1,), (1,)))


def local(
    activations, cotangent, lengths, dealing, qkv_weight, qv_bias, out_weight, out_bias,
    first_gain, first_shift, up_weight, up_bias, down_weight, down_bias, second_gain, second_shift,
):
    unit = lax.axis_size("dp")
    pack = lax.axis_index("dp")
    core = lax.axis_index("tensor")
    rows = activations.shape[0]
    width = activations.shape[2]
    half = rows // unit // 2

    def swap(x):
        return lax.ppermute(x, "tensor", [(0, 1), (1, 0)])

    core_arg = core.astype(jnp.int32).reshape(1)

    def send_back(field):
        got = lax.all_to_all(field.reshape(unit, half, width), "dp", 0, 0, tiled=True)
        return got.reshape(rows // 2, width)

    def undealt(own, sib):
        back = undeal(own, sib, lengths, dealing, core_arg, unit, half)
        return back.reshape(rows, 1, width)

    table, key_extra, query_extra = plan(lengths, dealing, rows, unit, half)
    x_own, x_sib, dealt_cotangent = deal(
        activations.reshape(rows, width), cotangent.reshape(rows, width), table, unit, half, 2
    )
    out_sib, up_sib, down_sib = swap(out_weight), swap(up_weight), swap(down_weight)
    up_bias_sib = swap(up_bias)

    qkv_planes = jnp.transpose(qkv_weight, (1, 0, 2))
    (
        queries, key_rows, values, context_own, context_sib, context_wide, log_total, cotangent_own,
    ) = attn_fwd(
        x_own, x_sib, qkv_planes, qv_bias, key_extra, query_extra, dealt_cotangent, unit, half, 3
    )
    vec_in = jnp.concatenate(
        [
            jnp.stack(
                [out_bias, first_gain, first_shift, down_bias, second_gain, second_shift], axis=0
            ),
            jnp.zeros((2, width), F32),
        ],
        axis=0,
    )
    (
        grad_h1, grad_context_own, grad_context_sib, vectors, up_bias_parts, got_own, got_sib,
        down_own, up_own, down_other, up_other,
    ) = feed_forward(
        x_own, context_own, context_sib, cotangent_own,
        (out_weight, out_sib, up_weight, up_sib, down_weight, down_sib),
        vec_in, up_bias[None], up_bias_sib[None], unit, half, 4,
    )
    shard = down_weight.shape[0]
    granule = row_unit(unit)

    def stacked(parts, rows_of):
        size = sum(part.shape[0] for part in parts)
        pad = -size % rows_of
        if pad:
            parts = parts + [jnp.zeros((pad, parts[0].shape[1]), parts[0].dtype)]
        return jnp.concatenate(parts, axis=0) if len(parts) > 1 else parts[0]


    def chip_sum(own_part, sib_part):
        total = own_part.astype(F32) + swap(sib_part).astype(F32)
        return stacked([total.astype(BF)], granule)

    wide_down = chip_sum(down_own, down_other)
    came = []
    for (start, count), order in zip(
        cut_rows(wide_down.shape[0], unit), bit_orders(unit.bit_length() - 1)
    ):
        step = 2 ** order[0]
        away = lax.dynamic_slice_in_dim(
            wide_down, start + (1 - pack // step % 2) * (count // 2), count // 2, 0
        )
        came.append(lax.ppermute(away, "dp", [(i, i ^ step) for i in range(unit)]))
    up_bias_part = up_bias_parts[0] + swap(up_bias_parts[1])
    vectors = vectors[:6]
    vectors = stacked([vectors + swap(vectors), up_bias_part.reshape(-1, width)], 8)
    wide_up = chip_sum(up_own, up_other)
    input_part, input_sib, qkv_part, qv_part, vectors, sum_down, sum_up, sum_out = attn_bwd(
        queries, key_rows, values, grad_context_own, swap(grad_context_sib), context_wide, log_total,
        key_extra, query_extra, x_own, x_sib, qkv_planes, wide_down, wide_up, vectors, came, shard,
        unit, 0,
    )
    inputs_own, inputs_sib, summed, qv_sum = tail(
        grad_h1, input_part, input_sib, stacked([qkv_part], granule), qv_part, unit, half, 1
    )
    grad_qkv_weight = jnp.transpose(
        summed[: 3 * width].reshape(3, width, -1).astype(F32), (1, 0, 2)
    )
    grad_qv_bias = qv_sum[:2]
    grad_down_weight = sum_down[:shard].astype(F32)
    grad_up_weight = sum_up.astype(F32)
    grad_out_weight = sum_out.astype(F32)
    (
        grad_out_bias,
        grad_first_gain,
        grad_first_shift,
        grad_down_bias,
        grad_second_gain,
        grad_second_shift,
    ) = vectors[:6]
    grad_up_bias = vectors[6 : 6 + shard // width].reshape(-1)

    output = undealt(got_own, got_sib)
    input_grad = undealt(inputs_own, inputs_sib)
    return (
        output,
        input_grad,
        grad_qkv_weight,
        grad_qv_bias,
        grad_out_weight,
        grad_out_bias,
        grad_first_gain,
        grad_first_shift,
        grad_up_weight,
        grad_up_bias,
        grad_down_weight,
        grad_down_bias,
        grad_second_gain,
        grad_second_shift,
    )


def solution(mesh):
    placed = (
        P(None, "dp", None),
        P(None, "dp", None),
        P(),
        P(),
        P(None, None, "tensor"),
        P(None, "tensor"),
        P("tensor", None),
        P(),
        P(),
        P(),
        P(None, "tensor"),
        P("tensor"),
        P("tensor", None),
        P(),
        P(),
        P(),
    )
    return jax.shard_map(
        local,
        mesh=mesh,
        in_specs=placed,
        out_specs=(
            P(None, "dp", None),
            P(None, "dp", None),
            P(None, None, "tensor"),
            P(None, "tensor"),
            P("tensor", None),
            P(),
            P(),
            P(),
            P(None, "tensor"),
            P("tensor"),
            P("tensor", None),
            P(),
            P(),
            P(),
        ),
        check_vma=False,
    )
```

```python
import functools
import math

import jax
import jax.numpy as jnp
from jax import lax
from jax.experimental import pallas as pl
from jax.experimental.pallas import tpu as pltpu
from jax.sharding import PartitionSpec as P

HD = 64
BF = jnp.bfloat16
F32 = jnp.float32
MASKED_SCORE = -1e30
NORM_EPSILON = 1e-05
EXTRA = 16
ROOM = 56 * 2**20


def dot(a, b, dims=((1,), (0,))):
    return lax.dot_general(a, b, (dims, ((), ())), preferred_element_type=F32)


def unit_starts(lengths, starts, unit):
    def step(s, total):
        starts[s] = total
        return total + (lengths[s] + unit - 1) // unit

    lax.fori_loop(0, lengths.shape[0], step, jnp.int32(0))


def pack_windows(lengths, dealing, starts, unit, pack, first, rows, total):
    seq_a = dealing[2 * pack]
    seq_b = dealing[2 * pack + 1]
    units_a = (lengths[seq_a] + unit - 1) // unit
    shift_a = starts[seq_a]
    shift_b = starts[seq_b] - units_a
    bases = []
    for shift in (shift_a, shift_b):
        base = jnp.clip((shift + first) // 16 * 16, 0, total - rows - 16)
        bases.append(pl.multiple_of(base, 16))
    return units_a, shift_a, shift_b, bases


def plan_kernel(unit, half, lengths, dealing, table, kx_ref, qx_ref, starts):
    unit_starts(lengths, starts, unit)

    def one(pack, carry):
        units_a = (lengths[dealing[2 * pack]] + unit - 1) // unit
        table[0, pack] = units_a
        table[1, pack] = starts[dealing[2 * pack]]
        table[2, pack] = starts[dealing[2 * pack + 1]] - units_a
        return carry

    lax.fori_loop(0, unit, one, 0)
    pack = lax.axis_index("dp")
    core = lax.axis_index("tensor")
    len_a, len_b = lengths[dealing[2 * pack]], lengths[dealing[2 * pack + 1]]
    split = (len_a + unit - 1) // unit * unit
    rows = kx_ref.shape[0]

    def place(at):
        at_core = jnp.where(at < rows // 2, core, 1 - core)
        return (at_core * half + at % half) * unit + at % (rows // 2) // half

    row = place(lax.broadcasted_iota(jnp.int32, kx_ref.shape, 0))
    lane = lax.broadcasted_iota(jnp.int32, kx_ref.shape, 1)
    later = row >= split
    live = row < jnp.where(later, split + len_b, len_a)
    barred = (lane == jnp.where(later, 0, 1)) | ~live
    kx_ref[...] = jnp.where(
        lane < 2, jnp.where(barred, MASKED_SCORE, 0.0), jnp.where(lane < 5, -1.0, 0.0)
    ).astype(BF)
    col = place(lax.broadcasted_iota(jnp.int32, qx_ref.shape, 1))
    turn = lax.broadcasted_iota(jnp.int32, qx_ref.shape, 0)
    qx_ref[...] = jnp.where(turn == jnp.where(col >= split, 1, 0), 1.0, 0.0).astype(BF)


def plan(lengths, dealing, rows, unit, half):
    smem = pl.BlockSpec(memory_space=pltpu.SMEM)
    vmem = pl.BlockSpec(memory_space=pltpu.VMEM)
    return pl.pallas_call(
        functools.partial(plan_kernel, unit, half),
        in_specs=[smem, smem],
        out_specs=[smem, vmem, vmem],
        out_shape=[
            jax.ShapeDtypeStruct((3, unit), jnp.int32),
            jax.ShapeDtypeStruct((rows, 128), BF),
            jax.ShapeDtypeStruct((EXTRA, rows), BF),
        ],
        scratch_shapes=[pltpu.SMEM(lengths.shape, jnp.int32)],
        name="plan",
    )(lengths, dealing)


def greet(count, with_sibling=True):
    barrier = pltpu.get_barrier_semaphore()
    me = lax.axis_index("dp")

    def one(k, carry):
        pl.semaphore_signal(
            barrier, 1, device_id={"dp": (me + k) % count}, device_id_type=pl.DeviceIdType.MESH
        )
        return carry

    lax.fori_loop(1, count, one, 0)
    pl.semaphore_signal(
        barrier,
        1,
        device_id={"tensor": 1 - lax.axis_index("tensor")},
        device_id_type=pl.DeviceIdType.MESH,
    )
    pl.semaphore_wait(barrier, count)


class PackExchange:
    def __init__(self, count, block, source, target, send_sem, recv_sem):
        self.count, self.block = count, block
        self.source, self.target = source, target
        self.send_sem, self.recv_sem = send_sem, recv_sem
        self.me = lax.axis_index("dp")

    def rows(self, ref, i):
        return ref.at[pl.ds(pl.multiple_of(i * self.block, 16), self.block)]

    def copy(self, peer, landing, sem):
        return pltpu.make_async_remote_copy(
            src_ref=self.rows(self.source, peer),
            dst_ref=self.rows(self.target, landing),
            send_sem=self.send_sem.at[peer],
            recv_sem=self.recv_sem.at[sem],
            device_id={"dp": peer},
            device_id_type=pl.DeviceIdType.MESH,
        )

    def send(self, peer):
        self.copy(peer, self.me, self.me).start()

    def wait_from(self, peer):
        self.copy(peer, peer, peer).wait_recv()

    def wait_sent(self, peer):
        self.copy(peer, self.me, self.me).wait_send()

    def peers(self, body, first=0, last=None):
        def one(i, carry):
            far = self.count // 2 * (1 + (i + 1) % 2) - 1 - i // 2
            body(self.across(self.me, far, self.count))
            return carry

        lax.fori_loop(first, self.count - 1 if last is None else last, one, 0)

    @staticmethod
    def across(index, far, count):
        peer = 0
        for bit in range(count.bit_length() - 1):
            weight = 2**bit
            peer += (index // weight % 2 + far // weight % 2) % 2 * weight
        return peer

    def keep_own(self):
        self.rows(self.target, self.me)[...] = self.rows(self.source, self.me)[...]


def to_sibling(source, target, send_sem, recv_sem):
    return pltpu.make_async_remote_copy(
        src_ref=source,
        dst_ref=target,
        send_sem=send_sem,
        recv_sem=recv_sem,
        device_id={"tensor": 1 - lax.axis_index("tensor")},
        device_id_type=pl.DeviceIdType.MESH,
    )


def deal_kernel(
    unit, half, table, x_ref, g_hbm, own_ref, sib_ref, dealt_g,
    outbox, g_ref, load_sem, send_sem, recv_sem, pass_sem, take_sem,
):
    total = x_ref.shape[0]
    load = pltpu.make_async_copy(g_hbm, g_ref, load_sem)
    load.start()
    greet(unit)
    first = lax.axis_index("tensor") * half
    slot = first + lax.broadcasted_iota(jnp.int32, (half, total), 0)
    col = lax.broadcasted_iota(jnp.int32, (half, total), 1)
    swap = PackExchange(unit, half, outbox, own_ref, send_sem, recv_sem)
    team = 4

    def dealt(ref, packs, target):
        picks = []
        for i in range(team):
            pack = packs * team + i
            shift = jnp.where(slot < table[0, pack], table[1, pack], table[2, pack])
            picks.append(jnp.where(col == slot + shift, 1.0, 0.0).astype(BF))
        rows = dot(jnp.concatenate(picks, axis=0), ref[...]).astype(BF)
        at = pl.multiple_of(packs * team * half, 16)
        target[pl.ds(at, team * half)] = rows

    def passed(pack):
        return to_sibling(
            swap.rows(own_ref, pack), swap.rows(sib_ref, pack), pass_sem.at[pack], take_sem.at[pack]
        )

    def pass_on(pack):
        swap.wait_from(pack)
        passed(pack).start()

    home = swap.me // team

    def deal_out(i, carry):
        teams = [swap.across(home, far - i, unit // team) for far in far_teams]
        for packs in teams:
            dealt(x_ref, packs, outbox)

        def send(j, carry):
            for packs in teams:
                pack = packs * team + j

                @pl.when(pack != swap.me)
                def _(pack=pack):
                    swap.send(pack)

            return carry

        lax.fori_loop(0, team, send, 0)
        return carry

    far_teams = (unit // team - 1, unit // team // 2 - 1)
    lax.fori_loop(0, unit // team // 2, deal_out, 0)
    swap.keep_own()
    passed(swap.me).start()
    load.wait()

    def keep(packs, carry):
        dealt(g_ref, packs, dealt_g)
        return carry

    lax.fori_loop(0, unit // team, keep, 0)
    swap.peers(pass_on)
    swap.peers(swap.wait_sent)

    def end(pack, carry):
        passed(pack).wait_recv()
        passed(pack).wait_send()
        return carry

    lax.fori_loop(0, unit, end, 0)


def deal(x, g, table, unit, half, ident):
    total, width = x.shape
    smem = pl.BlockSpec(memory_space=pltpu.SMEM)
    vmem = pl.BlockSpec(memory_space=pltpu.VMEM)
    return pl.pallas_call(
        functools.partial(deal_kernel, unit, half),
        in_specs=[smem, vmem, pl.BlockSpec(memory_space=pl.ANY)],
        out_specs=[vmem, vmem, vmem],
        out_shape=[jax.ShapeDtypeStruct((total // 2, width), BF)] * 3,
        scratch_shapes=[
            pltpu.VMEM((total // 2, width), BF),
            pltpu.VMEM((total, width), BF),
            pltpu.SemaphoreType.DMA,
            *[pltpu.SemaphoreType.DMA((unit,))] * 4,
        ],
        compiler_params=pltpu.CompilerParams(
            vmem_limit_bytes=ROOM, collective_id=ident, has_side_effects=True
        ),
        cost_estimate=pl.CostEstimate(
            flops=8 * total * width * half, bytes_accessed=40 * total * width, transcendentals=0
        ),
        name="deal",
    )(table, x, g)


def undeal_kernel(unit, half, lengths, dealing, core, own_ref, sib_ref, o_ref, starts):
    total = o_ref.shape[0]
    unit_starts(lengths, starts, unit)
    wide = half + 16
    row = lax.broadcasted_iota(jnp.int32, (2 * wide, half), 0)
    col = lax.broadcasted_iota(jnp.int32, (2 * wide, half), 1)
    o_ref[...] = jnp.zeros_like(o_ref)

    def one(pack, carry):
        for part, ref in ((core[0], own_ref), (1 - core[0], sib_ref)):
            first = part * half
            units_a, shift_a, shift_b, (base_a, base_b) = pack_windows(
                lengths, dealing, starts, unit, pack, first, half, total
            )
            slot = first + col
            near = slot < units_a
            at = jnp.where(near, slot + (shift_a - base_a), slot + (shift_b - base_b + wide))
            pick = (row == at) & (near == (row < wide))
            rows = ref[pl.ds(pl.multiple_of(pack * half, 16), half), :]
            both = dot(pick.astype(F32).astype(BF), rows).astype(BF)
            o_ref[pl.ds(base_a, wide), :] += both[:wide]
            o_ref[pl.ds(base_b, wide), :] += both[wide:]
        return carry

    lax.fori_loop(0, total // (2 * half), one, 0, unroll=8)


def undeal(own, sib, lengths, dealing, core, unit, half):
    total, width = 2 * own.shape[0], own.shape[1]
    smem = pl.BlockSpec(memory_space=pltpu.SMEM)
    vmem = pl.BlockSpec(memory_space=pltpu.VMEM)
    return pl.pallas_call(
        functools.partial(undeal_kernel, unit, half),
        in_specs=[smem, smem, smem, vmem, vmem],
        out_specs=vmem,
        out_shape=jax.ShapeDtypeStruct((total, width), BF),
        scratch_shapes=[pltpu.SMEM(lengths.shape, jnp.int32)],
        compiler_params=pltpu.CompilerParams(vmem_limit_bytes=ROOM),
        cost_estimate=pl.CostEstimate(
            flops=8 * total * width * half, bytes_accessed=4 * total * width, transcendentals=0
        ),
        name="undeal",
    )(lengths, dealing, core, own, sib)


def fwd_kernel(
    ck, unit, half, x_own, x_sib, w_ref, b_ref, kx_ref, qx_ref, dealt_g,
    q_ref, k_ref, v_ref, c_ref, c_other_out, c32_ref, lse_ref, got_g_out,
    kext, vt, c_sib, c_other, got_g, send_sem, recv_sem, pass_sem, take_sem,
):
    n = k_ref.shape[0]
    pair = pl.program_id(0)
    swap = PackExchange(unit, half, dealt_g, got_g, send_sem, recv_sem)

    def passed(pair):
        cols = pl.ds(pl.multiple_of(pair * 128, 128), 128)
        return to_sibling(
            c_sib.at[:, cols], c_other.at[:, cols], pass_sem.at[pair], take_sem.at[pair]
        )

    @pl.when(pair == 0)
    def _():
        greet(unit)
        swap.peers(swap.send)
        swap.keep_own()

    w = jnp.concatenate([w_ref[0], w_ref[1], w_ref[2]], axis=1)
    bias = jnp.concatenate([b_ref[0:1], jnp.zeros((1, 128), F32), b_ref[1:2]], axis=1)
    for part, x_ref in enumerate((x_own, x_sib)):
        for first in range(0, n // 2, 512):
            made = (dot(x_ref[first : first + 512], w) + bias).astype(BF)
            at = slice(part * n // 2 + first, part * n // 2 + first + 512)
            for j, ref in enumerate((q_ref, k_ref, v_ref)):
                ref[at] = made[:, 128 * j : 128 * j + 128]
    kext[:, :128] = k_ref[...]
    kext[:, 128:] = kx_ref[...]
    v_t = v_ref[...].T
    ones = jnp.where(lax.broadcasted_iota(jnp.int32, (EXTRA, n), 0) == 0, 1.0, 0.0).astype(BF)
    for h in range(2):
        vt[h, :HD] = v_t[HD * h : HD * h + HD]
        vt[h, HD:] = ones
    q_t = (q_ref[...] * BF(HD**-0.5)).T
    zero = jnp.zeros((HD, n), BF)
    qx = qx_ref[...]
    q_ext = [
        jnp.concatenate([q_t[:HD], zero, qx], axis=0),
        jnp.concatenate([zero, q_t[HD:], qx], axis=0),
    ]
    tops, sums = [None, None], [None, None]
    for first in range(0, n, ck):
        keys = slice(first, first + ck)
        for h in range(2):
            s = dot(kext[keys, : 128 + EXTRA], q_ext[h])
            top = jnp.max(s, axis=0, keepdims=True)
            if first:
                top = jnp.maximum(tops[h], top)
            part = dot(vt[h, :, keys], jnp.exp(s - top).astype(BF))
            if first:
                part = part + sums[h] * jnp.exp(tops[h] - top)
            tops[h], sums[h] = top, part
    outs = []
    for h in range(2):
        total = sums[h][HD : HD + 1]
        outs.append(sums[h][:HD] / total)
        lse_ref[0, h : h + 1] = tops[h] + jnp.log(total)
    c = jnp.concatenate(outs, axis=0).T
    c32_ref[...] = c
    c_ref[...] = c[: n // 2].astype(BF)
    c_sib[:, pl.ds(pl.multiple_of(pair * 128, 128), 128)] = c[n // 2 :].astype(BF)
    passed(pair).start()

    @pl.when(pair == pl.num_programs(0) - 1)
    def _():
        swap.peers(swap.wait_from)
        swap.peers(swap.wait_sent)

        def end(pair, carry):
            passed(pair).wait_recv()
            passed(pair).wait_send()
            return carry

        lax.fori_loop(0, pl.num_programs(0), end, 0)
        c_other_out[...] = c_other[...]
        got_g_out[...] = got_g[...]


def attn_cost(n, width, products):
    return pl.CostEstimate(
        flops=products * 2 * 4 * n * n * width,
        bytes_accessed=16 * n * width,
        transcendentals=n * n * width // HD,
    )


def attn_fwd(x_own, x_sib, w, b, kx, qx, dealt_g, unit, half, ident, ck=512):
    n, model = 2 * x_own.shape[0], x_own.shape[1]
    width = w.shape[2]
    pairs = width // 128
    keys = pl.BlockSpec((n, 128), lambda p: (0, p))

    def whole(shape):
        return pl.BlockSpec(shape, lambda p: (0, 0), pipeline_mode=pl.Buffered(1))

    return pl.pallas_call(
        functools.partial(fwd_kernel, ck, unit, half),
        grid=(pairs,),
        in_specs=[
            whole(x_own.shape),
            whole(x_sib.shape),
            pl.BlockSpec((3, model, 128), lambda p: (0, 0, p)),
            pl.BlockSpec((2, 128), lambda p: (0, p)),
            whole(kx.shape),
            whole(qx.shape),
            whole(dealt_g.shape),
        ],
        out_specs=[
            keys,
            keys,
            keys,
            pl.BlockSpec((n // 2, 128), lambda p: (0, p)),
            whole((n // 2, width)),
            keys,
            pl.BlockSpec((1, 2, n), lambda p: (p, 0, 0)),
            whole(dealt_g.shape),
        ],
        out_shape=[jax.ShapeDtypeStruct((n, width), BF)] * 3
        + [jax.ShapeDtypeStruct((n // 2, width), BF)] * 2
        + [
            jax.ShapeDtypeStruct((n, width), F32),
            jax.ShapeDtypeStruct((pairs, 2, n), F32),
            jax.ShapeDtypeStruct(dealt_g.shape, BF),
        ],
        scratch_shapes=[
            pltpu.VMEM((n, 256), BF),
            pltpu.VMEM((2, HD + EXTRA, n), BF),
            pltpu.VMEM((n // 2, width), BF),
            pltpu.VMEM((n // 2, width), BF),
            pltpu.VMEM(dealt_g.shape, BF),
            *[pltpu.SemaphoreType.DMA((unit,))] * 2,
            *[pltpu.SemaphoreType.DMA((pairs,))] * 2,
        ],
        compiler_params=pltpu.CompilerParams(
            vmem_limit_bytes=ROOM, collective_id=ident, has_side_effects=True
        ),
        cost_estimate=attn_cost(n, width, 2),
        name="attn_fwd",
    )(x_own, x_sib, w, b, kx, qx, dealt_g)


def split3(x):
    high = x.astype(BF)
    rest = x - high.astype(F32)
    middle = rest.astype(BF)
    return high, middle, (rest - middle.astype(F32)).astype(BF)


def bit_orders(bits):
    first = list(range(bits))
    second = [1, 2, 0] + list(range(3, bits))
    third = [2, 0, 1] + list(range(3, bits))
    return first, second, third


def row_unit(devices):
    return 8 * devices


def cut_rows(rows, devices):
    unit = row_unit(devices)
    units = rows // unit
    counts = [(units + 2) // 3, (units + 1) // 3, units // 3]
    starts = [0, counts[0], counts[0] + counts[1]]
    return [(s * unit, c * unit) for s, c in zip(starts, counts) if c]


def greet_partners(bits):
    me = lax.axis_index("dp")
    barrier = pltpu.get_barrier_semaphore()
    for bit in range(bits):
        pl.semaphore_signal(
            barrier,
            inc=1,
            device_id={"dp": me + (1 - 2 * (me // 2**bit % 2)) * 2**bit},
            device_id_type=pl.DeviceIdType.MESH,
        )
    pl.semaphore_wait(barrier, bits)


class PackSum:
    def __init__(self, devices, big, small, out, came, acc, inbox, small_box, send_sem, recv_sem):
        self.came = came
        self.bits = devices.bit_length() - 1
        self.me = lax.axis_index("dp")
        self.big, self.small, self.acc, self.inbox, self.out = big, small, acc, inbox, out
        self.small_box = small_box
        self.send_sem, self.recv_sem = send_sem, recv_sem
        self.parts = [
            (start, count, order)
            for (start, count), order in zip(cut_rows(big.shape[0], devices), bit_orders(self.bits))
        ]
        self.steps = 2 * self.bits

    def slots(self, first, slot_us, last):
        size = 4e-3 * self.big.shape[0] * self.big.shape[1]
        sizes = [size / 2 ** (level + 1) / 3 for level in range(self.bits - 1)]
        sizes = sizes + [size / 2 ** (self.bits - 2)] + sizes[::-1]
        at, out = 0.0, []
        for step in range(self.steps):
            out.append(min(last, first + math.ceil(at / slot_us)))
            if step < len(sizes) and not (step == 0 and self.came):
                at += 4.5 + sizes[step] / 80
        return out

    @staticmethod
    def scratch(rows, cols, small_shape, devices):
        bits = devices.bit_length() - 1
        return [
            pltpu.VMEM((rows // 2, cols), BF),
            pltpu.VMEM((rows, cols), BF),
            pltpu.VMEM((2 * bits + 1,) + small_shape, F32),
            pltpu.SemaphoreType.DMA((4, 2 * bits)),
            pltpu.SemaphoreType.DMA((4, 2 * bits)),
        ]

    def side(self, bit):
        return (self.me // 2**bit) % 2

    def partner(self, bit):
        return self.me + (1 - 2 * self.side(bit)) * 2**bit

    def region(self, part, level):
        start, count, order = self.parts[part]
        for done in range(level):
            start = start + self.side(order[done]) * (count // 2 ** (done + 1))
        return start, count // 2**level

    def halved(self, part, start):
        return self.parts[part][0] // 2 + start - self.region(part, 1)[0]

    def rows(self, ref, start, count):
        return ref.at[pl.ds(pl.multiple_of(start, 16), count)]

    def slot(self, part, level):
        start, count, _ = self.parts[part]
        return start + count - count // 2**level

    def sending(self, part, level):
        start, count = self.region(part, level)
        bit = self.parts[part][2][level]
        if level < self.bits - 1:
            count = count // 2
            start = start + (1 - self.side(bit)) * count
        return pltpu.make_async_remote_copy(
            src_ref=self.rows(self.acc, self.halved(part, start), count)
            if level
            else self.rows(self.big, start, count),
            dst_ref=self.inbox.at[pl.ds(self.slot(part, level), count)],
            send_sem=self.send_sem.at[part, level],
            recv_sem=self.recv_sem.at[part, level],
            device_id={"dp": self.partner(bit)},
            device_id_type=pl.DeviceIdType.MESH,
        )

    def doubling(self, part, level):
        mine = self.rows(self.out, *self.region(part, level + 1))
        return pltpu.make_async_remote_copy(
            src_ref=mine,
            dst_ref=mine,
            send_sem=self.send_sem.at[part, self.bits + level],
            recv_sem=self.recv_sem.at[part, self.bits + level],
            device_id={"dp": self.partner(self.parts[part][2][level])},
            device_id_type=pl.DeviceIdType.MESH,
        )

    def exchange(self, level):
        return pltpu.make_async_remote_copy(
            src_ref=self.small if level == 0 else self.small_box.at[self.bits + level],
            dst_ref=self.small_box.at[level],
            send_sem=self.send_sem.at[3, level],
            recv_sem=self.recv_sem.at[3, level],
            device_id={"dp": self.partner(level)},
            device_id_type=pl.DeviceIdType.MESH,
        )

    def add(self, part, level):
        last = level == self.bits - 1
        kept, count = self.region(part, level if last else level + 1)
        source, first = (self.acc, self.halved(part, kept)) if level else (self.big, kept)
        if last:
            target, goal = self.out, kept
        else:
            target, goal = self.acc, self.halved(part, kept)
        slot, box = self.slot(part, level), self.inbox
        if self.came and level == 0:
            slot, box = 0, self.came[part]
        tile = math.gcd(count, 64)

        def one(i, carry):
            def at(start):
                return pl.ds(pl.multiple_of(start + i * tile, 16), tile)

            total = source[at(first), :].astype(F32) + box[at(slot), :].astype(F32)
            target[at(goal), :] = total.astype(BF)
            return carry

        lax.fori_loop(0, count // tile, one, 0)

    def step(self, k):
        bits = self.bits
        for part in range(len(self.parts)):
            if 0 < k <= bits:
                if not (self.came and k == 1):
                    self.sending(part, k - 1).wait_recv()
                self.add(part, k - 1)
            elif k > bits:
                self.doubling(part, 2 * bits - 1 - k).wait_recv()
            if k < bits:
                self.sending(part, k).start()
            elif k < self.steps - 1:
                self.doubling(part, 2 * bits - 2 - k).start()
        if self.small is not None:
            if 0 < k <= bits:
                self.exchange(k - 1).wait_recv()
                held = self.small[...] if k == 1 else self.small_box[bits + k - 1]
                self.small_box[bits + k] = held + self.small_box[k - 1]
            if k < bits:
                self.exchange(k).start()
        if k == self.steps - 1:
            for part in range(len(self.parts)):
                for level in range(1 if self.came else 0, bits):
                    self.sending(part, level).wait_send()
                for level in range(bits - 1):
                    self.doubling(part, level).wait_send()
            if self.small is not None:
                for level in range(bits):
                    self.exchange(level).wait_send()


SLOT_US = 3.6


def bwd_kernel(
    ck, devices, turns, q_ref, k_ref, v_ref, g_own_ref, g_sib_ref, c32_ref, lse_ref, kx_ref, qx_ref,
    x_own, x_sib, w_ref, big_a, big_b, small, *refs,
):
    i = pl.program_id(1)
    n = k_ref.shape[0]
    bq = q_ref.shape[0]
    count = len(cut_rows(big_a.shape[0], devices))
    came, refs = refs[:count], refs[count:]
    dx_ref, dx_sib_ref, dw_ref, db_ref, small_out, out_a, out_up, out_last = refs[:8]
    kext, vext, kt, x_t, dq_acc, dk_acc, dv_acc, dx_sib, sum_a, sum_b, *comm_refs = refs[8:]
    comm_a = PackSum(devices, big_a, None, sum_a, came, *comm_refs[:5])
    comm_b = PackSum(devices, big_b, small, sum_b, None, *comm_refs[5:])
    turn = pl.program_id(0) * pl.num_programs(1) + i
    per_turn = n // ck
    slots = turns * per_turn
    slots_a = comm_a.slots(0, SLOT_US, slots)
    slots_b = comm_b.slots(0, SLOT_US, slots)

    def comm_at(which):
        for comm, at in ((comm_a, slots_a), (comm_b, slots_b)):
            for step, slot in enumerate(at):
                if step == 0 and comm.came:
                    continue
                if slot < slots and slot % per_turn == which:

                    @pl.when(turn == slot // per_turn)
                    def _(comm=comm, step=step):
                        comm.step(step)

                elif slot == slots and which is None:
                    comm.step(step)

    @pl.when(turn == 0)
    def _():
        greet_partners(comm_a.bits)

    @pl.when(i == 0)
    def _():
        kext[:, :128] = k_ref[...]
        kext[:, 128:] = kx_ref[...]
        vext[:, :128] = v_ref[...]
        lane = lax.broadcasted_iota(jnp.int32, (n, 128), 1)
        vext[:, 128:] = jnp.where((lane >= 2) & (lane < 5), -1.0, 0.0).astype(BF)
        kt[...] = k_ref[...].T
        dk_acc[...] = jnp.zeros_like(dk_acc)
        dv_acc[...] = jnp.zeros_like(dv_acc)

    q = q_ref[...] * BF(HD**-0.5)
    g = jnp.where(i == 0, g_own_ref[...], g_sib_ref[...])
    q_t, g_t = q.T, g.T
    prod_t = (g.astype(F32) * c32_ref[...]).T
    zero = jnp.zeros((HD, bq), BF)
    lane = lax.broadcasted_iota(jnp.int32, (bq, 128), 1)
    row = lax.broadcasted_iota(jnp.int32, (EXTRA, bq), 0)
    qx = qx_ref[...].astype(F32)

    def with_rows(base, parts):
        for j, part in enumerate(parts):
            base = jnp.where(row == 2 + j, part.astype(F32), base)
        return base.astype(BF)

    q_ext, g_ext, q_own, g_own, dq_t = [], [], [], [], []
    for h in range(2):
        mine = slice(HD * h, HD * h + HD)
        delta = jnp.sum(prod_t[mine], axis=0, keepdims=True)
        q_rows = with_rows(qx, split3(lse_ref[0, h : h + 1]))
        g_rows = with_rows(jnp.zeros((EXTRA, bq), F32), split3(delta))
        for out, turned, extra in ((q_ext, q_t, q_rows), (g_ext, g_t, g_rows)):
            both = [turned[mine], zero] if h == 0 else [zero, turned[mine]]
            out.append(jnp.concatenate(both + [extra], axis=0))
        ours = (lane < HD) if h == 0 else (lane >= HD)
        q_own.append(jnp.where(ours, q, BF(0)))
        g_own.append(jnp.where(ours, g, BF(0)))
        dq_t.append(jnp.zeros((HD, bq), F32))
    for first in range(0, n, ck):
        comm_at(first // ck)
        keys = slice(first, first + ck)
        dv = jnp.zeros((ck, 128), F32)
        dk = jnp.zeros((ck, 128), F32)
        for h in range(2):
            p = jnp.exp(dot(kext[keys, : 128 + EXTRA], q_ext[h]))
            ds = (p * dot(vext[keys, : 128 + EXTRA], g_ext[h])).astype(BF)
            dv = dv + dot(p.astype(BF), g_own[h])
            dk = dk + dot(ds, q_own[h])
            dq_t[h] = dq_t[h] + dot(kt[HD * h : HD * h + HD, keys], ds)
        dv_acc[keys] += dv
        dk_acc[keys] += dk
    dq = jnp.concatenate(dq_t, axis=0).T * HD**-0.5
    dq_acc[pl.ds(pl.multiple_of(i * bq, bq), bq)] = dq.astype(BF)

    @pl.when(turn == 0)
    def _():
        x_t[:, : n // 2] = x_own[...].T
        x_t[:, n // 2 :] = x_sib[...].T
        dx_ref[...] = jnp.zeros_like(dx_ref)
        dx_sib[...] = jnp.zeros_like(dx_sib)

    @pl.when(i == pl.num_programs(1) - 1)
    def _():
        width = x_own.shape[1]
        grads = [dq_acc[...], dk_acc[...].astype(BF), dv_acc[...].astype(BF)]
        joined = jnp.concatenate(grads, axis=1)
        made = dot(x_t[...], joined).astype(BF)
        for j in range(3):
            dw_ref[j * width : (j + 1) * width] = made[:, 128 * j : 128 * j + 128]
        bias = [jnp.sum(grad.astype(F32), axis=0, keepdims=True) for grad in grads[::2]]
        db_ref[...] = jnp.concatenate(bias + [jnp.zeros((6, 128), F32)], axis=0)
        tile = 512
        planes = jnp.concatenate([w_ref[j] for j in range(3)], axis=1)
        for first in range(0, n, tile):
            to_x = dot(joined[first : first + tile], planes, ((1,), (1,)))
            target, goal = (dx_ref, first) if first < n // 2 else (dx_sib, first - n // 2)
            target[goal : goal + tile] += to_x

    @pl.when(turn == turns - 1)
    def _():
        comm_at(None)
        dx_sib_ref[...] = dx_sib[...].astype(BF)
        out_a[...] = sum_a[...]
        tall, across = out_up.shape
        for start in range(0, across, tall):
            out_up[:, start : start + tall] = sum_b[start : start + tall]
        out_last[...] = sum_b[across : across + out_last.shape[0]]
        small_out[...] = comm_b.small_box[2 * comm_b.bits]


def attn_bwd(q, k, v, g_own_rows, g_sib_rows, c32, lse, kx, qx, x_own, x_sib, w, big_a, big_b, small, came, shard, devices, ident, ck=512):
    n, width = q.shape
    bq = n // 2
    pairs = width // 128
    model = x_own.shape[1]
    rows = pl.BlockSpec((bq, 128), lambda p, i: (i, p))
    keys = pl.BlockSpec((n, 128), lambda p, i: (0, p))
    def whole(shape):
        return pl.BlockSpec(shape, lambda p, i: (0, 0), pipeline_mode=pl.Buffered(1))

    return pl.pallas_call(
        functools.partial(bwd_kernel, ck, devices, pairs * (n // bq)),
        grid=(pairs, n // bq),
        in_specs=[
            rows,
            keys,
            keys,
            pl.BlockSpec((bq, 128), lambda p, i: (0, p)),
            pl.BlockSpec((bq, 128), lambda p, i: (0, p)),
            rows,
            pl.BlockSpec((1, 2, bq), lambda p, i: (p, 0, i)),
            pl.BlockSpec((n, 128), lambda p, i: (0, 0)),
            pl.BlockSpec((EXTRA, bq), lambda p, i: (0, i)),
            whole(x_own.shape),
            whole(x_sib.shape),
            pl.BlockSpec((3, model, 128), lambda p, i: (0, 0, p)),
            whole(big_a.shape),
            whole(big_b.shape),
            whole(small.shape),
            *[whole(box.shape) for box in came],
        ],
        out_specs=[
            whole((n // 2, model)),
            whole((n // 2, model)),
            pl.BlockSpec((3 * model, 128), lambda p, i: (0, p)),
            pl.BlockSpec((8, 128), lambda p, i: (0, p)),
            whole(small.shape),
            whole(big_a.shape),
            whole((model, shard)),
            whole((width, model)),
        ],
        out_shape=[
            jax.ShapeDtypeStruct((n // 2, model), F32),
            jax.ShapeDtypeStruct((n // 2, model), BF),
            jax.ShapeDtypeStruct((3 * model, width), BF),
            jax.ShapeDtypeStruct((8, width), F32),
            jax.ShapeDtypeStruct(small.shape, F32),
            jax.ShapeDtypeStruct(big_a.shape, BF),
            jax.ShapeDtypeStruct((model, shard), BF),
            jax.ShapeDtypeStruct((width, model), BF),
        ],
        scratch_shapes=[
            pltpu.VMEM((n, 256), BF),
            pltpu.VMEM((n, 256), BF),
            pltpu.VMEM((128, n), BF),
            pltpu.VMEM((model, n), BF),
            pltpu.VMEM((n, 128), BF),
            pltpu.VMEM((n, 128), F32),
            pltpu.VMEM((n, 128), F32),
            pltpu.VMEM((n // 2, model), F32),
            pltpu.VMEM(big_a.shape, BF),
            pltpu.VMEM(big_b.shape, BF),
            *PackSum.scratch(*big_a.shape, (8, 128), devices),
            *PackSum.scratch(*big_b.shape, small.shape, devices),
        ],
        compiler_params=pltpu.CompilerParams(
            vmem_limit_bytes=60 * 2**20, collective_id=ident, has_side_effects=True
        ),
        cost_estimate=attn_cost(n, width, 5),
        name="attn_bwd",
    )(q, k, v, g_own_rows, g_sib_rows, c32, lse, kx, qx, x_own, x_sib, w, big_a, big_b, small, *came)


def norm_parts(field, gain, shift):
    center = field - jnp.mean(field, axis=-1, keepdims=True)
    inv_std = lax.rsqrt(jnp.mean(center * center, axis=-1, keepdims=True) + NORM_EPSILON)
    normed = center * inv_std
    return normed * gain + shift, normed, inv_std


def norm_back(incoming, normed, inv_std, gain):
    scaled = incoming * gain
    return inv_std * (
        scaled
        - jnp.mean(scaled, axis=-1, keepdims=True)
        - normed * jnp.mean(scaled * normed, axis=-1, keepdims=True)
    )


FF_ROWS = 256
FF_COLS = 768


def ff_kernel(
    unit, half, x_ref, c_own, c_sib, g_ref, out_own, out_sib, up_own, up_sib, down_own, down_sib,
    vec_ref, bias_own, bias_sib,
    h1_ref, dc_own, dc_sib, vec_out, bias_out, got_own_out, got_sib_out, down_out, up_out, down_sib_out, up_sib_out,
    z, got, got_sib, slope, act, du, low_all, branch_all, da_all, mine, theirs,
    send_sem, recv_sem, pass_sem, take_sem, out_sem, keep_sem,
):
    i = pl.program_id(0)
    blocks = pl.num_programs(0)
    swap = PackExchange(unit, half, z, got, send_sem, recv_sem)
    team = FF_ROWS // half
    block = ff_block(i, unit, half, z.shape[0] // FF_ROWS)

    def passed(pack):
        return to_sibling(
            swap.rows(got, pack), swap.rows(got_sib, pack), pass_sem.at[pack], take_sem.at[pack]
        )

    @pl.when(i == 0)
    def _():
        greet(unit)
        vec_out[...] = jnp.zeros_like(vec_out)
        bias_out[...] = jnp.zeros_like(bias_out)

    out_bias, first_gain, first_shift, down_bias, second_gain, second_shift = (
        vec_ref[j : j + 1] for j in range(6)
    )
    here = pl.ds(pl.multiple_of(block * FF_ROWS, 16), FF_ROWS)
    attention = dot(c_own[here, :], out_own[...]) + dot(c_sib[here, :], out_sib[...])
    first, first_normed, first_inv = norm_parts(
        x_ref[...].astype(F32) + attention + out_bias, first_gain, first_shift
    )
    low = first.astype(BF)
    low_all[here, :] = low
    shard = up_own.shape[1]
    wide = FF_COLS
    sides = ((up_own, down_own, bias_own), (up_sib, down_sib, bias_sib))
    down = jnp.zeros(first.shape, F32)
    for side, (up, back, bias) in enumerate(sides):
        for start in range(0, shard, wide):
            cols = slice(start, start + wide)
            at = slice(side * shard + start, side * shard + start + wide)
            upward = dot(low, up[:, cols]) + bias[:, cols]
            cumulative = 0.5 + 0.5 * lax.erf(upward * math.sqrt(0.5))
            density = jnp.exp(-0.5 * upward * upward) * (1.0 / math.sqrt(2.0 * math.pi))
            active = (upward * cumulative).astype(BF)
            act[here, at] = active
            slope[:, at] = cumulative + upward * density
            down = down + dot(active, back[cols])
    second, second_normed, second_inv = norm_parts(
        first + down + down_bias, second_gain, second_shift
    )
    z[here, :] = second.astype(BF)

    def send(j, carry):
        pack = block * team + j

        @pl.when(pack != swap.me)
        def _():
            swap.send(pack)

        return carry

    lax.fori_loop(0, team, send, 0)
    outer = g_ref[...].astype(F32)
    grad_h2 = norm_back(outer, second_normed, second_inv, second_gain)
    branch = grad_h2.astype(BF)
    branch_all[here, :] = branch
    grad_y1 = grad_h2
    for side, (up, back, _) in enumerate(sides):
        for start in range(0, shard, wide):
            cols = slice(start, start + wide)
            at = slice(side * shard + start, side * shard + start + wide)
            inner = (dot(branch, back[cols], ((1,), (1,))) * slope[:, at]).astype(BF)
            du[here, at] = inner
            bias_out[side : side + 1, cols] += jnp.sum(inner.astype(F32), axis=0, keepdims=True)
            grad_y1 = grad_y1 + dot(inner, up[:, cols], ((1,), (1,)))
    grad_h1 = norm_back(grad_y1, first_normed, first_inv, first_gain)
    h1_ref[...] = grad_h1
    da = grad_h1.astype(BF)
    da_all[here, :] = da
    dc_own[...] = dot(da, out_own[...], ((1,), (1,))).astype(BF)
    dc_sib[...] = dot(da, out_sib[...], ((1,), (1,))).astype(BF)
    terms = (
        grad_h1, grad_y1 * first_normed, grad_y1, grad_h2, outer * second_normed, outer,
    )
    for j, term in enumerate(terms):
        vec_out[j : j + 1] += jnp.sum(term, axis=0, keepdims=True)

    model = z.shape[1]
    pieces = [
        (start, wide, lambda side, start=start: dot(
            act[:, side * shard + start : side * shard + start + wide], branch_all[...], OVER_ROWS
        ))
        for start in range(0, shard, wide)
    ] + [
        (shard + start, model, lambda side, start=start: dot(
            low_all[...], du[:, side * shard + start : side * shard + start + model], OVER_ROWS
        ))
        for start in range(0, shard, model)
    ] + [
        (2 * shard, c_own.shape[1], lambda side: dot(
            (c_sib if side else c_own)[...], da_all[...], OVER_ROWS
        ))
    ]

    def put(j, side):
        start, size, _ = pieces[j]
        source = theirs if side else mine
        down, up = (down_sib_out, up_sib_out) if side else (down_out, up_out)
        target, goal = (down, start) if start < shard else (up, start - shard)
        return pltpu.make_async_copy(
            source.at[pl.ds(start, size)], target.at[pl.ds(goal, size)], out_sem.at[side, j]
        )

    @pl.when(i == blocks - 1)
    def _():
        swap.keep_own()
        passed(swap.me).start()
        for side, kept in ((1, theirs), (0, mine)):
            for j, (start, size, product) in enumerate(pieces):
                kept[start : start + size] = product(side).astype(BF)
                put(j, side).start()

        def pass_on(pack):
            swap.wait_from(pack)
            passed(pack).start()

        swap.peers(pass_on)
        swap.peers(swap.wait_sent)

        def end(pack, carry):
            passed(pack).wait()
            return carry

        lax.fori_loop(0, unit, end, 0)
        keep_own = pltpu.make_async_copy(got, got_own_out, keep_sem.at[0])
        keep_sib = pltpu.make_async_copy(got_sib, got_sib_out, keep_sem.at[1])
        keep_own.start()
        keep_sib.start()
        for j in range(len(pieces)):
            put(j, 0).wait()
            put(j, 1).wait()
        keep_own.wait()
        keep_sib.wait()


OVER_ROWS = ((0,), (0,))


def ff_block(i, unit, half, blocks):
    home = lax.axis_index("dp") // (FF_ROWS // half)
    return PackExchange.across(home, blocks - 1 - i, blocks)


def feed_forward(x, c_own, c_sib, g, weights, vectors, bias_own, bias_sib, unit, half, ident):
    n, model = x.shape
    shard = bias_own.shape[1]
    width = c_own.shape[1]
    blocks = n // FF_ROWS

    def rows(cols):
        return pl.BlockSpec((FF_ROWS, cols), lambda i: (ff_block(i, unit, half, blocks), 0))

    def whole(shape):
        return pl.BlockSpec(shape, lambda i: (0, 0), pipeline_mode=pl.Buffered(1))

    shapes = [(model, F32), (width, BF), (width, BF)]
    kept = [(vectors.shape, F32), ((8, shard), F32)]
    shares = 2 * shard + width
    count = shard // FF_COLS + shard // model + 1
    put = [(n, model)] * 2 + [(shard, model), (shares - shard, model)] * 2
    return pl.pallas_call(
        functools.partial(ff_kernel, unit, half),
        grid=(blocks,),
        in_specs=[rows(model), whole(c_own.shape), whole(c_sib.shape), rows(model)]
        + [whole(w.shape) for w in weights]
        + [whole(vectors.shape), whole(bias_own.shape), whole(bias_sib.shape)],
        out_specs=[rows(cols) for cols, _ in shapes]
        + [whole(shape) for shape, _ in kept]
        + [pl.BlockSpec(memory_space=pl.ANY)] * len(put),
        out_shape=[jax.ShapeDtypeStruct((n, cols), dtype) for cols, dtype in shapes]
        + [jax.ShapeDtypeStruct(shape, dtype) for shape, dtype in kept]
        + [jax.ShapeDtypeStruct(shape, BF) for shape in put],
        scratch_shapes=[
            pltpu.VMEM((n, model), BF),
            pltpu.VMEM((n, model), BF),
            pltpu.VMEM((n, model), BF),
            pltpu.VMEM((FF_ROWS, 2 * shard), F32),
            pltpu.VMEM((n, 2 * shard), BF),
            pltpu.VMEM((n, 2 * shard), BF),
            *[pltpu.VMEM((n, model), BF)] * 3,
            pltpu.VMEM((shares, model), BF),
            pltpu.VMEM((shares, model), BF),
            *[pltpu.SemaphoreType.DMA((unit,))] * 4,
            pltpu.SemaphoreType.DMA((2, count)),
            pltpu.SemaphoreType.DMA((2,)),
        ],
        compiler_params=pltpu.CompilerParams(
            vmem_limit_bytes=62 * 2**20, collective_id=ident, has_side_effects=True
        ),
        cost_estimate=pl.CostEstimate(
            flops=8 * n * model * (width + shard) * 2,
            bytes_accessed=40 * n * model,
            transcendentals=4 * n * shard,
        ),
        name="feed_forward",
    )(x, c_own, c_sib, g, *weights, vectors, bias_own, bias_sib)


def tail_kernel(
    unit, half, h1_ref, dx_ref, dx_sib, big, small, own_ref, sib_ref, big_out, small_out,
    outbox, dx_came, mix_sem, mixed_sem, send_sem, recv_sem, pass_sem, take_sem, *comm_refs,
):
    comm = PackSum(unit, big, small, big_out, None, *comm_refs)
    swap = PackExchange(unit, half, outbox, own_ref, send_sem, recv_sem)

    def mix(pack):
        return to_sibling(
            swap.rows(dx_sib, pack),
            swap.rows(dx_came, pack),
            mix_sem.at[pack],
            mixed_sem.at[pack],
        )

    def passed(pack):
        return to_sibling(
            swap.rows(own_ref, pack), swap.rows(sib_ref, pack), pass_sem.at[pack], take_sem.at[pack]
        )

    def add_up(pack):
        mix(pack).wait_recv()
        at = swap.rows(dx_came, pack)[...].astype(F32)
        total = swap.rows(h1_ref, pack)[...] + swap.rows(dx_ref, pack)[...] + at
        swap.rows(outbox, pack)[...] = total.astype(BF)

    def add_and_send(pack):
        add_up(pack)
        swap.send(pack)

    def pass_on(pack):
        swap.wait_from(pack)
        passed(pack).start()

    greet(unit)
    swap.peers(lambda pack: mix(pack).start())
    mix(swap.me).start()
    comm.step(0)
    share = -(-(unit - 1) // 5)
    for k in range(1, 6):
        swap.peers(add_and_send, (k - 1) * share, min(k * share, unit - 1))
        comm.step(k)
    add_up(swap.me)
    swap.keep_own()
    passed(swap.me).start()
    early = (unit - 1) * 2 // 3
    swap.peers(pass_on, 0, early)
    for k in range(6, comm.steps):
        comm.step(k)
    small_out[...] = comm.small_box[2 * comm.bits]
    swap.peers(pass_on, early)
    swap.peers(swap.wait_sent)

    def end(pack, carry):
        mix(pack).wait_send()
        passed(pack).wait()
        return carry

    lax.fori_loop(0, unit, end, 0)


def tail(h1, dx, dx_sib, big, small, unit, half, ident):
    vmem = pl.BlockSpec(memory_space=pltpu.VMEM)
    kept = [jax.ShapeDtypeStruct(dx_sib.shape, BF)] * 2
    out_shape = kept + [
        jax.ShapeDtypeStruct(big.shape, BF),
        jax.ShapeDtypeStruct(small.shape, F32),
    ]
    return pl.pallas_call(
        functools.partial(tail_kernel, unit, half),
        in_specs=[vmem] * 5,
        out_specs=[vmem] * len(out_shape),
        out_shape=out_shape,
        scratch_shapes=[
            pltpu.VMEM(dx_sib.shape, BF),
            pltpu.VMEM(dx_sib.shape, BF),
            *[pltpu.SemaphoreType.DMA((unit,))] * 6,
            *PackSum.scratch(*big.shape, small.shape, unit),
        ],
        compiler_params=pltpu.CompilerParams(
            vmem_limit_bytes=ROOM, collective_id=ident, has_side_effects=True
        ),
        cost_estimate=pl.CostEstimate(flops=0, bytes_accessed=200 * big.size, transcendentals=0),
        name="tail",
    )(h1, dx, dx_sib, big, small)


def over_rows(first_op, second_op):
    return dot(first_op, second_op, ((0,), (0,)))


def over_cols(first_op, second_op):
    return dot(first_op, second_op, ((1,), (1,)))


def local(
    activations, cotangent, lengths, dealing, qkv_weight, qv_bias, out_weight, out_bias,
    first_gain, first_shift, up_weight, up_bias, down_weight, down_bias, second_gain, second_shift,
):
    unit = lax.axis_size("dp")
    pack = lax.axis_index("dp")
    core = lax.axis_index("tensor")
    rows = activations.shape[0]
    width = activations.shape[2]
    half = rows // unit // 2

    def swap(x):
        return lax.ppermute(x, "tensor", [(0, 1), (1, 0)])

    core_arg = core.astype(jnp.int32).reshape(1)

    def send_back(field):
        got = lax.all_to_all(field.reshape(unit, half, width), "dp", 0, 0, tiled=True)
        return got.reshape(rows // 2, width)

    def undealt(own, sib):
        back = undeal(own, sib, lengths, dealing, core_arg, unit, half)
        return back.reshape(rows, 1, width)

    table, key_extra, query_extra = plan(lengths, dealing, rows, unit, half)
    x_own, x_sib, dealt_cotangent = deal(
        activations.reshape(rows, width), cotangent.reshape(rows, width), table, unit, half, 2
    )
    out_sib, up_sib, down_sib = swap(out_weight), swap(up_weight), swap(down_weight)
    up_bias_sib = swap(up_bias)

    qkv_planes = jnp.transpose(qkv_weight, (1, 0, 2))
    (
        queries, key_rows, values, context_own, context_sib, context_wide, log_total, cotangent_own,
    ) = attn_fwd(
        x_own, x_sib, qkv_planes, qv_bias, key_extra, query_extra, dealt_cotangent, unit, half, 3
    )
    vec_in = jnp.concatenate(
        [
            jnp.stack(
                [out_bias, first_gain, first_shift, down_bias, second_gain, second_shift], axis=0
            ),
            jnp.zeros((2, width), F32),
        ],
        axis=0,
    )
    (
        grad_h1, grad_context_own, grad_context_sib, vectors, up_bias_parts, got_own, got_sib,
        down_own, up_own, down_other, up_other,
    ) = feed_forward(
        x_own, context_own, context_sib, cotangent_own,
        (out_weight, out_sib, up_weight, up_sib, down_weight, down_sib),
        vec_in, up_bias[None], up_bias_sib[None], unit, half, 4,
    )
    shard = down_weight.shape[0]
    granule = row_unit(unit)

    def stacked(parts, rows_of):
        size = sum(part.shape[0] for part in parts)
        pad = -size % rows_of
        if pad:
            parts = parts + [jnp.zeros((pad, parts[0].shape[1]), parts[0].dtype)]
        return jnp.concatenate(parts, axis=0) if len(parts) > 1 else parts[0]


    def chip_sum(own_part, sib_part):
        total = own_part.astype(F32) + swap(sib_part).astype(F32)
        return stacked([total.astype(BF)], granule)

    wide_down = chip_sum(down_own, down_other)
    came = []
    for (start, count), order in zip(
        cut_rows(wide_down.shape[0], unit), bit_orders(unit.bit_length() - 1)
    ):
        step = 2 ** order[0]
        away = lax.dynamic_slice_in_dim(
            wide_down, start + (1 - pack // step % 2) * (count // 2), count // 2, 0
        )
        came.append(lax.ppermute(away, "dp", [(i, i ^ step) for i in range(unit)]))
    up_bias_part = up_bias_parts[0] + swap(up_bias_parts[1])
    vectors = vectors[:6]
    vectors = stacked([vectors + swap(vectors), up_bias_part.reshape(-1, width)], 8)
    wide_up = chip_sum(up_own, up_other)
    input_part, input_sib, qkv_part, qv_part, vectors, sum_down, sum_up, sum_out = attn_bwd(
        queries, key_rows, values, grad_context_own, swap(grad_context_sib), context_wide, log_total,
        key_extra, query_extra, x_own, x_sib, qkv_planes, wide_down, wide_up, vectors, came, shard,
        unit, 0,
    )
    inputs_own, inputs_sib, summed, qv_sum = tail(
        grad_h1, input_part, input_sib, stacked([qkv_part], granule), qv_part, unit, half, 1
    )
    grad_qkv_weight = jnp.transpose(
        summed[: 3 * width].reshape(3, width, -1).astype(F32), (1, 0, 2)
    )
    grad_qv_bias = qv_sum[:2]
    grad_down_weight = sum_down[:shard].astype(F32)
    grad_up_weight = sum_up.astype(F32)
    grad_out_weight = sum_out.astype(F32)
    (
        grad_out_bias,
        grad_first_gain,
        grad_first_shift,
        grad_down_bias,
        grad_second_gain,
        grad_second_shift,
    ) = vectors[:6]
    grad_up_bias = vectors[6 : 6 + shard // width].reshape(-1)

    output = undealt(got_own, got_sib)
    input_grad = undealt(inputs_own, inputs_sib)
    return (
        output,
        input_grad,
        grad_qkv_weight,
        grad_qv_bias,
        grad_out_weight,
        grad_out_bias,
        grad_first_gain,
        grad_first_shift,
        grad_up_weight,
        grad_up_bias,
        grad_down_weight,
        grad_down_bias,
        grad_second_gain,
        grad_second_shift,
    )


def solution(mesh):
    placed = (
        P(None, "dp", None),
        P(None, "dp", None),
        P(),
        P(),
        P(None, None, "tensor"),
        P(None, "tensor"),
        P("tensor", None),
        P(),
        P(),
        P(),
        P(None, "tensor"),
        P("tensor"),
        P("tensor", None),
        P(),
        P(),
        P(),
    )
    return jax.shard_map(
        local,
        mesh=mesh,
        in_specs=placed,
        out_specs=(
            P(None, "dp", None),
            P(None, "dp", None),
            P(None, None, "tensor"),
            P(None, "tensor"),
            P("tensor", None),
            P(),
            P(),
            P(),
            P(None, "tensor"),
            P("tensor"),
            P("tensor", None),
            P(),
            P(),
            P(),
        ),
        check_vma=False,
    )
```
